512 devices in a mesh: wide: 64 (over y_hi, z, core), narrow: 8 (over x, y_lo).
Axes of the slice: x: 4, y: 8 (y_hi: 4, y_lo: 2; y = y_hi * 2 + y_lo), z: 8, core: 2. Of those that a mesh axis runs over, the one named last changes fastest.
Arguments:
- images: bfloat16 [8192, 72, 256], P('wide'), may hold values from -512 to 512
- defocus: float32 [8192], P('wide'), may hold values from 1 to 3
- class_index: int32 [8192], P('wide'), may hold values from 0 to 191
- rotation_index: int32 [8192], P('wide'), may hold values from 0 to 71
- owner_map: int32 [192], replicated, may hold values from 0 to 63, as said below
- roster: int32 [8, 3], replicated, may hold values from 0 to 63, as said below
- ref_store: bfloat16 [64, 8, 8, 72, 256], P('wide', 'narrow'), may hold values from -0.25 to 0.25
Outputs:
- new_references: bfloat16 [64, 8, 4, 72, 256], P('wide', 'narrow')
- log_evidence: float32 [8192], P('wide')
The draws below stay inside these ranges and needn't reach their ends.
Inputs may be any that keep to these rules, and one draw needn't show every extreme that they name: Each row of roster names 3 different indices. `owner_map`: in each group of 24 consecutive classes, no index is named more than 4 times, and one index is named exactly 4 times.
All inputs are finite; a program needn't handle non-finite values.
Results may differ from the reference program's by a relative error of at most 0.0038.
The reference program's roundings to bfloat16 on the way (of `references`, `weighted` and `aligned`) count: a program that leaves them out, or rounds other values in their place, can miss the bound.
Values may be sent and summed in bfloat16 or wider, within the bound.
No kernel may reach another device: no remote copies, remote signals or barrier semaphores. Data moves between devices by JAX's collectives and lax.ppermute only.
A program may use at most 128 MiB of HBM per device.

```python
import math
import jax
import jax.numpy as jnp
from jax import lax

CYCLES = 128
ANGLES = 72
BLOCK = 8
STEPS = 3
OWN_MAX = 4
CLS_GRP = 24
CLASSES = 192
SIGMA_ROT = 8
PART = 8192
N_WIDE = 64
N_NARROW = 8


def ref_values(key):
    base_key, scale_key = jax.random.split(jax.random.fold_in(key, 7))
    shape_all = (N_WIDE, N_NARROW, BLOCK, ANGLES, 2 * CYCLES)
    scales = jnp.exp(jax.random.uniform(scale_key, (N_WIDE, N_NARROW, BLOCK, 1, 1), jnp.float32, math.log(0.01), math.log(0.04)))
    values = jnp.clip(jax.random.normal(base_key, shape_all, jnp.float32), -6.0, 6.0)
    return (values * scales).astype(jnp.bfloat16)


def draw_ref_store(key, part):
    return ref_values(key)


def defocus_values(key):
    spread = jax.random.uniform(jax.random.fold_in(key, 31), (PART,), jnp.float32, 0.0, math.log(3.0))
    return jnp.exp(spread)


def draw_defocus(key, part):
    return defocus_values(key)


def class_values(key):
    return jax.random.randint(jax.random.fold_in(key, 37), (PART,), 0, CLASSES).astype(jnp.int32)


def draw_class_index(key, part):
    return class_values(key)


def rotation_values(key):
    return jax.random.randint(jax.random.fold_in(key, 41), (PART,), 0, ANGLES).astype(jnp.int32)


def draw_rotation_index(key, part):
    return rotation_values(key)


def owners_of_group(group_key):
    rank_key, pool_key = jax.random.split(group_key)
    ranking = jax.random.permutation(rank_key, CLS_GRP).astype(jnp.int32)
    pool = jax.random.permutation(pool_key, N_WIDE).astype(jnp.int32)
    position = jnp.where(ranking < OWN_MAX, 0, 1 + (ranking - OWN_MAX) // 2)
    return pool[position]


def draw_owner_map(key, part):
    group_keys = jax.random.split(jax.random.fold_in(key, 11), N_NARROW)
    return jax.vmap(owners_of_group)(group_keys).reshape(CLASSES).astype(jnp.int32)


def holders_of_group(group_key):
    return jax.random.permutation(group_key, N_WIDE)[:STEPS].astype(jnp.int32)


def roster_values(key):
    group_keys = jax.random.split(jax.random.fold_in(key, 23), N_NARROW)
    return jax.vmap(holders_of_group)(group_keys).astype(jnp.int32)


def draw_roster(key, part):
    return roster_values(key)


def contrast_of(defocus_rows):
    cycle_freq = (jnp.arange(CYCLES, dtype=jnp.float32) + 1.0) / CYCLES
    phase_angle = 8.0 * math.pi * defocus_rows[:, None] * cycle_freq[None, :] ** 2
    return -jnp.sin(phase_angle) - 0.1 * jnp.cos(phase_angle)


def draw_images(key, part):
    base_key = jax.random.fold_in(jax.random.fold_in(key, 5), 0)
    values = jnp.clip(jax.random.normal(base_key, (PART, ANGLES, 2 * CYCLES), jnp.float32), -6.0, 6.0)
    planted_count = PART // 64
    rows = jnp.arange(planted_count, dtype=jnp.int32) * 64 + 5
    refs = ref_values(key).astype(jnp.float32)
    roster = roster_values(key)
    chosen = class_values(key)[rows]
    centre = rotation_values(key)[rows]
    group_ids = chosen // CLS_GRP
    step_ids = chosen % CLS_GRP // BLOCK
    slot_ids = chosen % BLOCK
    holders = roster[group_ids, step_ids]
    picked = refs[holders, group_ids, slot_ids]
    contrast_rows = contrast_of(defocus_values(key)[rows])
    squares = jnp.sum(picked * picked, axis=1)
    power = ANGLES * (squares[:, :CYCLES] + squares[:, CYCLES:])
    energy = jnp.sum(contrast_rows * contrast_rows * power, axis=-1)
    ranks = jax.random.permutation(jax.random.fold_in(key, 43), planted_count).astype(jnp.float32)
    target = 110.0 + 140.0 * ranks / max(planted_count - 1, 1)
    sigma = float(SIGMA_ROT)
    first_amp = 0.5 + target * ANGLES / energy
    second_amp = 0.5 + (target - 2.0 + 0.5 / (sigma * sigma)) * ANGLES / energy
    counting = jnp.arange(ANGLES, dtype=jnp.int32)
    first_src = (counting[None, :] - centre[:, None]) % ANGLES
    second_src = (counting[None, :] - centre[:, None] - 1) % ANGLES
    first_turn = jnp.take_along_axis(picked, first_src[:, :, None], axis=1)
    second_turn = jnp.take_along_axis(picked, second_src[:, :, None], axis=1)
    doubled = jnp.concatenate([contrast_rows, contrast_rows], axis=-1)
    planted = (first_amp[:, None, None] * first_turn + second_amp[:, None, None] * second_turn) * doubled[:, None, :]
    values = values.at[rows].add(planted)
    return jnp.clip(values, -512.0, 512.0).astype(jnp.bfloat16)


def setup_inputs(seed: int = 0) -> dict:
    keys = jax.random.split(jax.random.key(seed), 8)
    images = draw_images(jax.random.fold_in(keys[7], 71), 0)
    defocus = draw_defocus(jax.random.fold_in(keys[7], 71), 0)
    class_index = draw_class_index(jax.random.fold_in(keys[7], 71), 0)
    rotation_index = draw_rotation_index(jax.random.fold_in(keys[7], 71), 0)
    owner_map = draw_owner_map(jax.random.fold_in(keys[7], 71), 0)
    roster = draw_roster(jax.random.fold_in(keys[7], 71), 0)
    ref_store = draw_ref_store(jax.random.fold_in(keys[7], 71), 0)
    return {"images": images, "defocus": defocus, "class_index": class_index, "rotation_index": rotation_index, "owner_map": owner_map, "roster": roster, "ref_store": ref_store}


TAU = 1.0
CONTRAST = 0.1
TOP_PRECISION = lax.Precision.HIGHEST


def angle_tables(length):
    counting = jnp.arange(length, dtype=jnp.int32)
    products = (counting[:, None] * counting[None, :]) % length
    phase_angle = products.astype(jnp.float32) * (2.0 * math.pi / length)
    return jnp.cos(phase_angle), jnp.sin(phase_angle)


def contrast(defocus_rows):
    cycle_freq = (jnp.arange(CYCLES, dtype=jnp.float32) + 1.0) / CYCLES
    phase_angle = 8.0 * math.pi * defocus_rows[:, None] * cycle_freq[None, :] ** 2
    return -jnp.sin(phase_angle) - CONTRAST * jnp.cos(phase_angle)


def spectrum(polar, cosines_low, sines_low):
    polar_wide = polar.astype(jnp.float32)
    cos_part = jnp.einsum("ma,naj->nmj", cosines_low.astype(jnp.float32), polar_wide)
    sin_part = jnp.einsum("ma,naj->nmj", sines_low.astype(jnp.float32), polar_wide)
    real_part = cos_part[..., :CYCLES] + sin_part[..., CYCLES:]
    imag_part = cos_part[..., CYCLES:] - sin_part[..., :CYCLES]
    return jnp.concatenate([real_part, imag_part], axis=-1).astype(jnp.bfloat16)


def rotation_prior(rotation_rows):
    counting = jnp.arange(ANGLES, dtype=jnp.int32)
    distance = jnp.abs(counting[None, :] - rotation_rows[:, None])
    distance = jnp.minimum(distance, ANGLES - distance).astype(jnp.float32)
    return -0.5 * (distance / SIGMA_ROT) ** 2


def polar_image(harmonic, cosine_table, sine_table):
    real_part = harmonic[..., :CYCLES]
    imag_part = harmonic[..., CYCLES:]
    polar_real = (jnp.einsum("cmk,ma->cak", real_part, cosine_table, precision=TOP_PRECISION) - jnp.einsum("cmk,ma->cak", imag_part, sine_table, precision=TOP_PRECISION)) / ANGLES
    polar_imag = (jnp.einsum("cmk,ma->cak", imag_part, cosine_table, precision=TOP_PRECISION) + jnp.einsum("cmk,ma->cak", real_part, sine_table, precision=TOP_PRECISION)) / ANGLES
    return jnp.concatenate([polar_real, polar_imag], axis=-1)


def reference(images, defocus, class_index, rotation_index, owner_map, roster, ref_store):
    cosine_table, sine_table = angle_tables(ANGLES)
    cosines_low = cosine_table.astype(jnp.bfloat16)
    sines_low = sine_table.astype(jnp.bfloat16)
    class_ids = jnp.arange(CLASSES, dtype=jnp.int32)
    group_ids = class_ids // CLS_GRP
    step_ids = (class_ids % CLS_GRP) // BLOCK
    slot_numbers = class_ids % BLOCK
    holders = roster[group_ids, step_ids]
    references = ref_store[holders, group_ids, slot_numbers]
    ref_spec = spectrum(references, cosines_low, sines_low)
    ref_swap = jnp.concatenate([-ref_spec[..., CYCLES:], ref_spec[..., :CYCLES]], axis=-1)
    ref_wide = ref_spec.astype(jnp.float32)
    swap_wide = ref_swap.astype(jnp.float32)
    power = jnp.sum(jnp.square(ref_wide), axis=1)
    power = power[:, :CYCLES] + power[:, CYCLES:]
    rows_block = math.gcd(PART, 256)
    blocks_count = PART // rows_block
    feature_len = ANGLES * 2 * CYCLES

    def scan_block(carried, inputs):
        numerator, denominator = carried
        image_rows, defocus_rows, class_rows, rotation_rows = inputs
        contrast_rows = contrast(defocus_rows)
        doubled = jnp.concatenate([contrast_rows, contrast_rows], axis=-1)
        weighted = (image_rows.astype(jnp.float32) * doubled[:, None, :]).astype(jnp.bfloat16)
        spectra = spectrum(weighted, cosines_low, sines_low)
        spectra_wide = spectra.astype(jnp.float32)
        real_correlation = jnp.einsum("pmj,cmj->pcm", spectra_wide, ref_wide)
        imaginary_correlation = jnp.einsum("pmj,cmj->pcm", spectra_wide, swap_wide)
        turned_images = jnp.einsum("exj,ji->exi", real_correlation, cosine_table, precision=TOP_PRECISION) - jnp.einsum("exj,ji->exi", imaginary_correlation, sine_table, precision=TOP_PRECISION)
        energy = jnp.dot(contrast_rows * contrast_rows, power.T, precision=TOP_PRECISION)
        scores = (turned_images - 0.5 * energy[:, :, None]) / ANGLES + rotation_prior(rotation_rows)[:, None, :]
        running_max = jnp.max(scores, axis=(1, 2))
        evidence = running_max + jnp.log(jnp.sum(jnp.exp(scores - running_max[:, None, None]), axis=(1, 2)))
        own_scores = jnp.take_along_axis(scores, class_rows[:, None, None].astype(jnp.int32), axis=1)[:, 0, :]
        weight = jax.nn.softmax(own_scores, axis=-1)
        h_real = jnp.dot(weight, cosine_table, precision=TOP_PRECISION)
        h_imag = jnp.dot(weight, sine_table, precision=TOP_PRECISION)
        x_real = spectra_wide[..., :CYCLES]
        x_imag = spectra_wide[..., CYCLES:]
        a_real = x_real * h_real[:, :, None] - x_imag * h_imag[:, :, None]
        a_imag = x_real * h_imag[:, :, None] + x_imag * h_real[:, :, None]
        aligned = jnp.concatenate([a_real, a_imag], axis=-1).astype(jnp.bfloat16)
        numerator = numerator + jax.ops.segment_sum(aligned.astype(jnp.float32).reshape(rows_block, feature_len), class_rows, num_segments=CLASSES)
        denominator = denominator + jax.ops.segment_sum(contrast_rows * contrast_rows, class_rows, num_segments=CLASSES)
        return (numerator, denominator), evidence

    start = (jnp.zeros((CLASSES, feature_len), jnp.float32), jnp.zeros((CLASSES, CYCLES), jnp.float32))
    inputs = (images.reshape(blocks_count, rows_block, ANGLES, 2 * CYCLES), defocus.reshape(blocks_count, rows_block), class_index.reshape(blocks_count, rows_block), rotation_index.reshape(blocks_count, rows_block))
    (numerator, denominator), evidence = lax.scan(scan_block, start, inputs)
    doubled_den = jnp.concatenate([denominator, denominator], axis=-1)
    harmonic = numerator.reshape(CLASSES, ANGLES, 2 * CYCLES) / (doubled_den[:, None, :] + TAU)
    polar = polar_image(harmonic, cosine_table, sine_table)
    owners = owner_map.reshape(N_NARROW, CLS_GRP)
    wide_ids = jnp.arange(N_WIDE, dtype=jnp.int32)
    matches = (owners[:, None, :] == wide_ids[None, :, None]).astype(jnp.int32)
    ranking = jnp.cumsum(matches, axis=2) - 1
    slot_range = jnp.arange(OWN_MAX, dtype=jnp.int32)
    slot_pick = ((matches[:, :, None, :] == 1) & (ranking[:, :, None, :] == slot_range[None, None, :, None])).astype(jnp.float32)
    grouped = polar.reshape(N_NARROW, CLS_GRP, feature_len)
    placed = jnp.einsum("gwsc,gcf->wgsf", slot_pick, grouped, precision=TOP_PRECISION)
    new_references = placed.reshape(N_WIDE, N_NARROW, OWN_MAX, ANGLES, 2 * CYCLES).astype(jnp.bfloat16)
    return new_references, evidence.reshape(PART)
```

```python
import math

import jax
import jax.numpy as jnp
from jax import lax
from jax.sharding import Mesh
from jax.sharding import PartitionSpec as P

CYCLES = 128
ANGLES = 72
STEPS = 3
BLOCK = 8
OWN_MAX = 4
CLS_GRP = 24
SIGMA_ROT = 8
ROWS = 9
WIDE = ("wide_0", "wide_1", "wide_2")


TAU = 1.0
CONTRAST = 0.1
TOP_PRECISION = lax.Precision.HIGHEST


def spread(x, axis):
    copies = jnp.broadcast_to(x[None], (lax.axis_size(axis), *x.shape))
    return lax.all_to_all(copies, axis, 0, 0, tiled=True)


def swapped(x):
    return lax.ppermute(x, "wide_2", [(0, 1), (1, 0)])


def angle_tables(length):
    counting = jnp.arange(length, dtype=jnp.int32)
    products = counting[:, None] * counting[None, :] % length
    phase_angle = products.astype(jnp.float32) * (2.0 * math.pi / length)
    return (jnp.cos(phase_angle), jnp.sin(phase_angle))


def contrast(defocus_rows):
    cycle_freq = (jnp.arange(CYCLES, dtype=jnp.float32) + 1.0) / CYCLES
    phase_angle = 8.0 * math.pi * defocus_rows[:, None] * cycle_freq[None, :] ** 2
    return -jnp.sin(phase_angle) - CONTRAST * jnp.cos(phase_angle)


def spectrum(polar, cosines_low, sines_low):
    cos_part = jnp.einsum("ma,naj->nmj", cosines_low, polar, preferred_element_type=jnp.float32)
    sin_part = jnp.einsum("ma,naj->nmj", sines_low, polar, preferred_element_type=jnp.float32)
    real_part = cos_part[..., :CYCLES] + sin_part[..., CYCLES:]
    imag_part = cos_part[..., CYCLES:] - sin_part[..., :CYCLES]
    return jnp.concatenate([real_part, imag_part], axis=-1).astype(jnp.bfloat16)


def rotation_prior(rotation_rows):
    counting = jnp.arange(ANGLES, dtype=jnp.int32)
    distance = jnp.abs(counting[None, :] - rotation_rows[:, None])
    distance = jnp.minimum(distance, ANGLES - distance).astype(jnp.float32)
    return -0.5 * (distance / SIGMA_ROT) ** 2


def fetch(blocks, holders):
    halves = blocks.reshape(BLOCK, ANGLES, 2, CYCLES).transpose(0, 2, 1, 3)
    halves = halves.reshape(BLOCK * 2, ANGLES, CYCLES)
    sliced = lax.all_to_all(halves, ("wide_1", "wide_2"), 0, 0, tiled=True)
    inner, outer = holders % 16, holders // 16
    picked = jnp.stack(
        [lax.dynamic_index_in_dim(sliced, inner[s], 0, keepdims=False) for s in range(STEPS)]
    )
    planes = spread(picked, "wide_0")
    picked = jnp.stack(
        [lax.dynamic_index_in_dim(planes[:, s], outer[s], 0, keepdims=False) for s in range(STEPS)]
    )
    mine = spread(picked, "wide_1").reshape(CLS_GRP, ANGLES, CYCLES)
    other = swapped(mine)
    first = lax.axis_index("wide_2") == 0
    return jnp.concatenate(
        [jnp.where(first, mine, other), jnp.where(first, other, mine)], axis=-1
    )


def per_device(images, defocus, class_index, rotation_index, owner_map, roster, ref_store):
    class_group = lax.axis_index("narrow")
    z_index = lax.axis_index("wide_1")
    core = lax.axis_index("wide_2")
    wide_count = lax.axis_size(WIDE)
    cosine_table, sine_table = angle_tables(ANGLES)
    cosines_low = cosine_table.astype(jnp.bfloat16)
    sines_low = sine_table.astype(jnp.bfloat16)
    leading_class = class_group * CLS_GRP
    arrival = jnp.arange(CLS_GRP, dtype=jnp.int32)
    within = arrival % STEPS * BLOCK + arrival // STEPS
    class_ids = leading_class + within
    holders = lax.dynamic_index_in_dim(roster, class_group, 0, keepdims=False)

    contrast_rows = contrast(defocus)
    contrast_sq = contrast_rows * contrast_rows
    doubled = jnp.concatenate([contrast_rows, contrast_rows], axis=-1)
    weighted = (images.astype(jnp.float32) * doubled[:, None, :]).astype(jnp.bfloat16)
    spectra = spectrum(weighted, cosines_low, sines_low)
    turned = spectra.transpose(1, 0, 2)
    prior_rows = rotation_prior(rotation_index)

    refs = fetch(ref_store[0, 0], holders)
    ref_spec = spectrum(refs, cosines_low, sines_low)
    ref_swap = jnp.concatenate([-ref_spec[..., CYCLES:], ref_spec[..., :CYCLES]], axis=-1)
    real_correlation = jnp.einsum(
        "mpj,cmj->pcm", turned, ref_spec, preferred_element_type=jnp.float32
    )
    imaginary_correlation = jnp.einsum(
        "mpj,cmj->pcm", turned, ref_swap, preferred_element_type=jnp.float32
    )
    turned_images = jnp.einsum(
        "exj,ji->exi", real_correlation, cosine_table, precision=TOP_PRECISION
    ) - jnp.einsum("exj,ji->exi", imaginary_correlation, sine_table, precision=TOP_PRECISION)
    power = jnp.sum(jnp.square(ref_spec.astype(jnp.float32)), axis=1)
    power = power[:, :CYCLES] + power[:, CYCLES:]
    energy = jnp.dot(contrast_sq, power.T, precision=TOP_PRECISION)
    scores = (turned_images - 0.5 * energy[:, :, None]) / ANGLES + prior_rows[:, None, :]
    members = class_index[:, None] == class_ids[None, :]
    own_scores = jnp.einsum(
        "pj,pjr->pr", members.astype(jnp.float32), scores, precision=TOP_PRECISION
    )
    block_max = jnp.max(scores, axis=(1, 2))
    block_sum = jnp.sum(jnp.exp(scores - block_max[:, None, None]), axis=(1, 2))

    weight = jax.nn.softmax(own_scores, axis=-1)
    h_real = jnp.einsum("pr,rm->mp", weight, cosine_table, precision=TOP_PRECISION)
    h_imag = jnp.einsum("pr,rm->mp", weight, sine_table, precision=TOP_PRECISION)
    x_real = turned[..., :CYCLES].astype(jnp.float32)
    x_imag = turned[..., CYCLES:].astype(jnp.float32)
    a_real = x_real * h_real[:, :, None] - x_imag * h_imag[:, :, None]
    a_imag = x_real * h_imag[:, :, None] + x_imag * h_real[:, :, None]
    chosen = members.astype(jnp.bfloat16)
    numer_real = jnp.einsum(
        "pc,mpk->mck", chosen, a_real.astype(jnp.bfloat16), preferred_element_type=jnp.float32
    )
    numer_imag = jnp.einsum(
        "pc,mpk->mck", chosen, a_imag.astype(jnp.bfloat16), preferred_element_type=jnp.float32
    )
    denom = jnp.einsum(
        "pc,pk->ck", members.astype(jnp.float32), contrast_sq, precision=TOP_PRECISION
    )

    denom = denom + swapped(denom)
    numer = jnp.where(core == 0, numer_real, numer_imag) + swapped(
        jnp.where(core == 0, numer_imag, numer_real)
    )
    high = denom.astype(jnp.bfloat16)
    low = (denom - high.astype(jnp.float32)).astype(jnp.bfloat16)
    extra = jnp.concatenate([high[None], low[None], jnp.zeros((6, CLS_GRP, CYCLES), jnp.bfloat16)])
    share = jnp.concatenate(
        [numer.astype(jnp.bfloat16).reshape(8, ROWS, CLS_GRP, CYCLES), extra[:, None]], axis=1
    )
    share = share.reshape(8, (ROWS + 1) * CLS_GRP, CYCLES)
    share = lax.all_to_all(share, "wide_1", 0, 0, tiled=True)
    share = share.astype(jnp.float32).sum(axis=0).reshape(ROWS + 1, CLS_GRP, CYCLES)
    owners = lax.dynamic_slice_in_dim(owner_map, leading_class, CLS_GRP)
    owners = owners.reshape(STEPS, BLOCK).T.reshape(CLS_GRP)
    same = owners[:, None] == owners[None, :]
    ranking = jnp.sum(same & (within[None, :] < within[:, None]), axis=1)
    place = owners * OWN_MAX + ranking
    pick = place[None, :] == jnp.arange(wide_count * OWN_MAX, dtype=jnp.int32)[:, None]
    numer_share = share[:ROWS].astype(jnp.bfloat16)
    denom_high = share[ROWS:].astype(jnp.bfloat16)
    denom_low = (share[ROWS:] - denom_high.astype(jnp.float32)).astype(jnp.bfloat16)
    share = jnp.concatenate([numer_share, jnp.where(core == 0, denom_high, denom_low)])
    sent = jnp.einsum(
        "wsc,tck->wtsk",
        pick.reshape(wide_count, OWN_MAX, CLS_GRP).astype(jnp.bfloat16),
        share,
        preferred_element_type=jnp.float32,
    ).astype(jnp.bfloat16)
    sent = sent.reshape(wide_count, (ROWS + 1) * OWN_MAX, CYCLES)
    got = lax.all_to_all(sent, WIDE, 0, 0, tiled=True)
    got = got.reshape(4, 8, 2, ROWS + 1, OWN_MAX, CYCLES).astype(jnp.float32).sum(axis=0)
    denominator = got[0, 0, ROWS] + got[0, 1, ROWS] + got[1, 0, ROWS]
    scale = 1.0 / (denominator + TAU) / ANGLES
    real_part = got[:, 0, :ROWS].reshape(ANGLES, OWN_MAX, CYCLES) * scale
    imag_part = got[:, 1, :ROWS].reshape(ANGLES, OWN_MAX, CYCLES) * scale
    mixed = lambda x, table: jnp.einsum("mck,ma->cak", x, table, precision=TOP_PRECISION)
    polar = jnp.concatenate(
        [
            mixed(real_part, cosine_table) - mixed(imag_part, sine_table),
            mixed(imag_part, cosine_table) + mixed(real_part, sine_table),
        ],
        axis=-1,
    )
    new_references = polar.astype(jnp.bfloat16).reshape(1, 1, OWN_MAX, ANGLES, 2 * CYCLES)

    pairs = spread(jnp.stack([block_max, block_sum]), "narrow")
    joined = jnp.max(pairs[:, 0], axis=0)
    log_evidence = joined + jnp.log(jnp.sum(pairs[:, 1] * jnp.exp(pairs[:, 0] - joined), axis=0))
    return (new_references, log_evidence)


def solution(mesh):
    split = Mesh(
        mesh.devices.reshape(4, 8, 2, mesh.shape["narrow"]),
        ("wide_0", "wide_1", "wide_2", "narrow"),
    )
    placed = (
        P(WIDE, None, None),
        P(WIDE),
        P(WIDE),
        P(WIDE),
        P(),
        P(),
        P(WIDE, "narrow", None, None, None),
    )
    return jax.shard_map(
        per_device,
        mesh=split,
        in_specs=placed,
        out_specs=(P(WIDE, "narrow", None, None, None), P(WIDE)),
        check_vma=False,
    )
```

```python
import math

import jax
import jax.numpy as jnp
from jax import lax
from jax.experimental import pallas as pl
from jax.experimental.pallas import tpu as pltpu
from jax.sharding import Mesh
from jax.sharding import PartitionSpec as P

CYCLES = 128
ANGLES = 72
STEPS = 3
BLOCK = 8
OWN_MAX = 4
CLS_GRP = 24
SIGMA_ROT = 8
ROWS = 9
WIDE = ("wide_0", "wide_1", "wide_2")


TAU = 1.0
CONTRAST = 0.1
TOP_PRECISION = lax.Precision.HIGHEST


def swapped(x):
    return lax.ppermute(x, "wide_2", [(0, 1), (1, 0)])


def angle_tables(length):
    counting = jnp.arange(length, dtype=jnp.int32)
    products = counting[:, None] * counting[None, :] % length
    phase_angle = products.astype(jnp.float32) * (2.0 * math.pi / length)
    return (jnp.cos(phase_angle), jnp.sin(phase_angle))


def contrast(defocus_rows):
    cycle_freq = (jnp.arange(CYCLES, dtype=jnp.float32) + 1.0) / CYCLES
    phase_angle = 8.0 * math.pi * defocus_rows[:, None] * cycle_freq[None, :] ** 2
    return -jnp.sin(phase_angle) - CONTRAST * jnp.cos(phase_angle)


def spectrum_of(polar, table):
    both = jnp.dot(table, polar, preferred_element_type=jnp.float32)
    cos_part, sin_part = both[:ANGLES], both[ANGLES:]
    real_part = cos_part[:, :CYCLES] + sin_part[:, CYCLES:]
    imag_part = cos_part[:, CYCLES:] - sin_part[:, :CYCLES]
    return real_part, imag_part


def spectra_kernel(table_ref, contrast_ref, image_ref, out_ref, held_real, held_imag):
    table = table_ref[...]
    count = image_ref.shape[0]
    for row in range(count):
        factor = contrast_ref[row : row + 1, :]
        factor = jnp.concatenate([factor, factor], axis=-1)
        weighted = (image_ref[row].astype(jnp.float32) * factor).astype(jnp.bfloat16)
        rows = pl.ds(row, ANGLES, stride=count)
        held_real[rows, :], held_imag[rows, :] = spectrum_of(weighted, table)
    shape = (ANGLES, count, CYCLES)
    out_ref[:, :, :CYCLES] = held_real[...].reshape(shape).astype(jnp.bfloat16)
    out_ref[:, :, CYCLES:] = held_imag[...].reshape(shape).astype(jnp.bfloat16)


def image_spectra(images, contrast_rows, table):
    particles = images.shape[0]
    count = 16
    return pl.pallas_call(
        spectra_kernel,
        grid=(particles // count,),
        in_specs=[
            pl.BlockSpec((2 * ANGLES, ANGLES), lambda i: (0, 0)),
            pl.BlockSpec((count, CYCLES), lambda i: (i, 0)),
            pl.BlockSpec((count, ANGLES, 2 * CYCLES), lambda i: (i, 0, 0)),
        ],
        out_specs=pl.BlockSpec((ANGLES, count, 2 * CYCLES), lambda i: (0, i, 0)),
        out_shape=jax.ShapeDtypeStruct((ANGLES, particles, 2 * CYCLES), jnp.bfloat16),
        scratch_shapes=[pltpu.VMEM((ANGLES * count, CYCLES), jnp.float32)] * 2,
        cost_estimate=pl.CostEstimate(
            flops=particles * 4 * ANGLES * ANGLES * 2 * CYCLES,
            bytes_accessed=4 * particles * ANGLES * 2 * CYCLES,
            transcendentals=0,
        ),
    )(table, contrast_rows, images)


def pick_kernel(index_ref, source_ref, out_ref):
    for step in range(STEPS):
        at = index_ref[step]
        value = source_ref[at, step if source_ref.shape[1] == STEPS else 0]
        for copy in range(out_ref.shape[0]):
            out_ref[copy, step] = value


def pick(source, index, copies):
    return pl.pallas_call(
        pick_kernel,
        in_specs=[
            pl.BlockSpec(memory_space=pltpu.SMEM),
            pl.BlockSpec(memory_space=pltpu.VMEM),
        ],
        out_specs=pl.BlockSpec(memory_space=pltpu.VMEM),
        out_shape=jax.ShapeDtypeStruct((copies, STEPS, ANGLES, CYCLES), jnp.bfloat16),
    )(index, source)


def score_kernel(
    core_ref,
    mine_ref,
    other_ref,
    spectra_ref,
    low_ref,
    turn_ref,
    back_ref,
    square_ref,
    prior_ref,
    member_ref,
    keep_ref,
    send_ref,
    top_ref,
    sum_ref,
    ref_real,
    ref_imag,
    corr,
    scores,
    power,
):
    particles = spectra_ref.shape[1]
    first = core_ref[0] == 0
    table = low_ref[...]
    for c in range(CLS_GRP):
        mine, other = mine_ref[c], other_ref[c]
        polar = jnp.concatenate(
            [jnp.where(first, mine, other), jnp.where(first, other, mine)], axis=-1
        )
        real, imag = (
            part.astype(jnp.bfloat16).astype(jnp.float32) for part in spectrum_of(polar, table)
        )
        rows = pl.ds(c, ANGLES, stride=CLS_GRP)
        ref_real[rows, :], ref_imag[rows, :] = real, imag
        power[c : c + 1, :] = jnp.sum(real * real + imag * imag, axis=0, keepdims=True)
    square = square_ref[...]
    across = (((1,), (1,)), ((), ()))
    energy = 0.5 * lax.dot_general(
        power[...], square, across, precision=TOP_PRECISION, preferred_element_type=jnp.float32
    )
    for m in range(ANGLES):
        rows = slice(m * CLS_GRP, (m + 1) * CLS_GRP)
        real, imag = ref_real[rows, :], ref_imag[rows, :]
        both = jnp.concatenate(
            [jnp.concatenate([real, -imag], axis=0), jnp.concatenate([imag, real], axis=0)],
            axis=-1,
        ).astype(jnp.bfloat16)
        corr[m * 2 * CLS_GRP : (m + 1) * 2 * CLS_GRP, :] = lax.dot_general(
            both, spectra_ref[m], across, preferred_element_type=jnp.float32
        )
    turn, prior = turn_ref[...], prior_ref[...]
    best = jnp.full((ANGLES, particles), -jnp.inf, jnp.float32)
    own = jnp.zeros((ANGLES, particles), jnp.float32)
    for c in range(0, CLS_GRP, 2):
        pair = [
            jnp.concatenate(
                [
                    corr[pl.ds(k, ANGLES, stride=2 * CLS_GRP), :],
                    corr[pl.ds(CLS_GRP + k, ANGLES, stride=2 * CLS_GRP), :],
                ],
                axis=0,
            )
            for k in (c, c + 1)
        ]
        rotated = jnp.dot(
            turn,
            jnp.concatenate(pair, axis=-1),
            precision=TOP_PRECISION,
            preferred_element_type=jnp.float32,
        )
        for k in range(2):
            value = rotated[:, k * particles : (k + 1) * particles]
            value = (value - energy[c + k : c + k + 1, :]) * (1.0 / ANGLES) + prior
            scores[c + k] = value
            best = jnp.maximum(best, value)
            own = own + jnp.where(member_ref[c + k : c + k + 1, :] > 0, value, 0.0)
    top = jnp.max(best, axis=0, keepdims=True)
    total = jnp.zeros((ANGLES, particles), jnp.float32)
    for c in range(CLS_GRP):
        total = total + jnp.exp(scores[c] - top)
    top_ref[...] = top
    sum_ref[...] = jnp.sum(total, axis=0, keepdims=True)
    weight = jnp.exp(own - jnp.max(own, axis=0, keepdims=True))
    weight = weight / jnp.sum(weight, axis=0, keepdims=True)
    turned_back = jnp.dot(
        back_ref[...], weight, precision=TOP_PRECISION, preferred_element_type=jnp.float32
    )
    h_real = turned_back[:particles].T
    h_imag = turned_back[particles:].T
    member = member_ref[...]
    chosen = member.astype(jnp.bfloat16)
    for m in range(ANGLES):
        x_real = spectra_ref[m, :, :CYCLES].astype(jnp.float32)
        x_imag = spectra_ref[m, :, CYCLES:].astype(jnp.float32)
        hr, hi = h_real[:, m : m + 1], h_imag[:, m : m + 1]
        aligned = jnp.concatenate(
            [x_real * hr - x_imag * hi, x_real * hi + x_imag * hr], axis=-1
        ).astype(jnp.bfloat16)
        sums = jnp.dot(chosen, aligned, preferred_element_type=jnp.float32)
        real_sum, imag_sum = sums[:, :CYCLES], sums[:, CYCLES:]
        keep_ref[m] = jnp.where(first, real_sum, imag_sum)
        send_ref[m] = jnp.where(first, imag_sum, real_sum)
    denom = jnp.dot(
        member, square, precision=TOP_PRECISION, preferred_element_type=jnp.float32
    )
    keep_ref[ANGLES] = denom
    send_ref[ANGLES] = denom


def score(core, mine, other, spectra, low_table, turn, back, square, prior, member):
    particles = spectra.shape[1]
    sums = jax.ShapeDtypeStruct((ANGLES + 1, CLS_GRP, CYCLES), jnp.float32)
    row = jax.ShapeDtypeStruct((1, particles), jnp.float32)
    vmem = pl.BlockSpec(memory_space=pltpu.VMEM)
    return pl.pallas_call(
        score_kernel,
        in_specs=[pl.BlockSpec(memory_space=pltpu.SMEM)] + [vmem] * 9,
        out_specs=(vmem, vmem, vmem, vmem),
        out_shape=(sums, sums, row, row),
        scratch_shapes=[
            pltpu.VMEM((ANGLES * CLS_GRP, CYCLES), jnp.float32),
            pltpu.VMEM((ANGLES * CLS_GRP, CYCLES), jnp.float32),
            pltpu.VMEM((ANGLES * 2 * CLS_GRP, particles), jnp.float32),
            pltpu.VMEM((CLS_GRP, ANGLES, particles), jnp.float32),
            pltpu.VMEM((CLS_GRP, CYCLES), jnp.float32),
        ],
        compiler_params=pltpu.CompilerParams(vmem_limit_bytes=40 * 1024 * 1024),
    )(core, mine, other, spectra, low_table, turn, back, square, prior, member)


def pack_kernel(keep_ref, got_ref, out_ref):
    denom = keep_ref[ANGLES] + got_ref[ANGLES]
    high = denom.astype(jnp.bfloat16)
    low = (denom - high.astype(jnp.float32)).astype(jnp.bfloat16)
    for z in range(out_ref.shape[0]):
        at = pl.ds(z * ROWS, ROWS)
        out_ref[z, :ROWS] = (keep_ref[at] + got_ref[at]).astype(jnp.bfloat16)
        out_ref[z, ROWS] = high if z == 0 else low


def pack(keep, got):
    vmem = pl.BlockSpec(memory_space=pltpu.VMEM)
    return pl.pallas_call(
        pack_kernel,
        in_specs=[vmem, vmem],
        out_specs=vmem,
        out_shape=jax.ShapeDtypeStruct((8, ROWS + 1, CLS_GRP, CYCLES), jnp.bfloat16),
    )(keep, got)


def rotation_prior(rotation_rows):
    counting = jnp.arange(ANGLES, dtype=jnp.int32)
    distance = jnp.abs(counting[None, :] - rotation_rows[:, None])
    distance = jnp.minimum(distance, ANGLES - distance).astype(jnp.float32)
    return -0.5 * (distance / SIGMA_ROT) ** 2


def fetch(blocks, holders):
    halves = jnp.stack([blocks[..., :CYCLES], blocks[..., CYCLES:]], axis=1)
    halves = halves.reshape(BLOCK * 2, ANGLES, CYCLES)
    sliced = lax.all_to_all(halves, ("wide_1", "wide_2"), 0, 0, tiled=True)
    picked = pick(sliced[:, None], holders % 16, 4)
    planes = lax.all_to_all(picked, "wide_0", 0, 0, tiled=True)
    picked = pick(planes, holders // 16, 8)
    return lax.all_to_all(picked, "wide_1", 0, 0, tiled=True).reshape(CLS_GRP, ANGLES, CYCLES)


def joined_evidence(top, total):
    for bit in (1, 2, 4):
        pair = jnp.concatenate([top, total])
        got = lax.ppermute(pair, "narrow", [(k, k ^ bit) for k in range(8)])
        joined = jnp.maximum(top, got[:1])
        total = total * jnp.exp(top - joined) + got[1:] * jnp.exp(got[:1] - joined)
        top = joined
    return (top + jnp.log(total)).reshape(-1)


def per_device(images, defocus, class_index, rotation_index, owner_map, roster, ref_store):
    class_group = lax.axis_index("narrow")
    z_index = lax.axis_index("wide_1")
    core = lax.axis_index("wide_2")
    wide_count = lax.axis_size(WIDE)
    cosine_table, sine_table = angle_tables(ANGLES)
    cosines_low = cosine_table.astype(jnp.bfloat16)
    sines_low = sine_table.astype(jnp.bfloat16)
    leading_class = class_group * CLS_GRP
    arrival = jnp.arange(CLS_GRP, dtype=jnp.int32)
    within = arrival % STEPS * BLOCK + arrival // STEPS
    class_ids = leading_class + within
    holders = lax.dynamic_index_in_dim(roster, class_group, 0, keepdims=False)

    low_table = jnp.concatenate([cosines_low, sines_low])
    turn = jnp.concatenate([cosine_table, -sine_table], axis=-1)
    filled = ((0, CYCLES - ANGLES), (0, 0))
    back = jnp.concatenate([jnp.pad(cosine_table, filled), jnp.pad(sine_table, filled)])
    contrast_rows = contrast(defocus)
    square = contrast_rows * contrast_rows
    prior = rotation_prior(rotation_index).T
    member = (class_index[None, :] == class_ids[:, None]).astype(jnp.float32)
    spectra = image_spectra(images, contrast_rows, low_table)

    mine = fetch(ref_store[0, 0], holders)
    other = swapped(mine)
    keep, send, top, total = score(
        core.reshape(1), mine, other, spectra, low_table, turn, back, square, prior, member
    )
    share = pack(keep, swapped(send)).reshape(8, (ROWS + 1) * CLS_GRP, CYCLES)
    share = lax.all_to_all(share, "wide_1", 0, 0, tiled=True)
    share = share.astype(jnp.float32).sum(axis=0).reshape(ROWS + 1, CLS_GRP, CYCLES)
    owners = lax.dynamic_slice_in_dim(owner_map, leading_class, CLS_GRP)
    owners = owners.reshape(STEPS, BLOCK).T.reshape(CLS_GRP)
    same = owners[:, None] == owners[None, :]
    ranking = jnp.sum(same & (within[None, :] < within[:, None]), axis=1)
    place = owners * OWN_MAX + ranking
    pick = place[None, :] == jnp.arange(wide_count * OWN_MAX, dtype=jnp.int32)[:, None]
    numer_share = share[:ROWS].astype(jnp.bfloat16)
    denom_high = share[ROWS:].astype(jnp.bfloat16)
    denom_low = (share[ROWS:] - denom_high.astype(jnp.float32)).astype(jnp.bfloat16)
    share = jnp.concatenate([numer_share, jnp.where(core == 0, denom_high, denom_low)])
    sent = jnp.einsum(
        "wsc,tck->wtsk",
        pick.reshape(wide_count, OWN_MAX, CLS_GRP).astype(jnp.bfloat16),
        share,
        preferred_element_type=jnp.float32,
    ).astype(jnp.bfloat16)
    sent = sent.reshape(wide_count, (ROWS + 1) * OWN_MAX, CYCLES)
    got = lax.all_to_all(sent, WIDE, 0, 0, tiled=True)
    got = got.reshape(4, 8, 2, ROWS + 1, OWN_MAX, CYCLES).astype(jnp.float32).sum(axis=0)
    denominator = got[0, 0, ROWS] + got[0, 1, ROWS] + got[1, 0, ROWS]
    scale = 1.0 / (denominator + TAU) / ANGLES
    real_part = got[:, 0, :ROWS].reshape(ANGLES, OWN_MAX, CYCLES) * scale
    imag_part = got[:, 1, :ROWS].reshape(ANGLES, OWN_MAX, CYCLES) * scale
    mixed = lambda x, table: jnp.einsum("mck,ma->cak", x, table, precision=TOP_PRECISION)
    polar = jnp.concatenate(
        [
            mixed(real_part, cosine_table) - mixed(imag_part, sine_table),
            mixed(imag_part, cosine_table) + mixed(real_part, sine_table),
        ],
        axis=-1,
    )
    new_references = polar.astype(jnp.bfloat16).reshape(1, 1, OWN_MAX, ANGLES, 2 * CYCLES)

    top, total, _ = lax.optimization_barrier((top, total, sent))
    log_evidence = joined_evidence(top, total)
    return (new_references, log_evidence)


def solution(mesh):
    split = Mesh(
        mesh.devices.reshape(4, 8, 2, mesh.shape["narrow"]),
        ("wide_0", "wide_1", "wide_2", "narrow"),
    )
    placed = (
        P(WIDE, None, None),
        P(WIDE),
        P(WIDE),
        P(WIDE),
        P(),
        P(),
        P(WIDE, "narrow", None, None, None),
    )
    return jax.shard_map(
        per_device,
        mesh=split,
        in_specs=placed,
        out_specs=(P(WIDE, "narrow", None, None, None), P(WIDE)),
        check_vma=False,
    )
```

```python
import math

import jax
import jax.numpy as jnp
from jax import lax
from jax.experimental import pallas as pl
from jax.experimental.pallas import tpu as pltpu
from jax.sharding import Mesh
from jax.sharding import PartitionSpec as P

CYCLES = 128
ANGLES = 72
STEPS = 3
BLOCK = 8
OWN_MAX = 4
CLS_GRP = 24
SIGMA_ROT = 8
ROWS = 9
WIDE = ("wide_0", "wide_1", "wide_2")


TAU = 1.0
CONTRAST = 0.1
TOP_PRECISION = lax.Precision.HIGHEST


def swapped(x):
    return lax.ppermute(x, "wide_2", [(0, 1), (1, 0)])


def angle_tables(length):
    counting = jnp.arange(length, dtype=jnp.int32)
    products = counting[:, None] * counting[None, :] % length
    phase_angle = products.astype(jnp.float32) * (2.0 * math.pi / length)
    return (jnp.cos(phase_angle), jnp.sin(phase_angle))


def contrast(defocus_rows):
    cycle_freq = (jnp.arange(CYCLES, dtype=jnp.float32) + 1.0) / CYCLES
    phase_angle = 8.0 * math.pi * defocus_rows[:, None] * cycle_freq[None, :] ** 2
    return -jnp.sin(phase_angle) - CONTRAST * jnp.cos(phase_angle)


def spectrum_of(polar, table):
    both = jnp.dot(table, polar, preferred_element_type=jnp.float32)
    cos_part, sin_part = both[:ANGLES], both[ANGLES:]
    real_part = cos_part[:, :CYCLES] + sin_part[:, CYCLES:]
    imag_part = cos_part[:, CYCLES:] - sin_part[:, :CYCLES]
    return real_part, imag_part


def spectra_kernel(table_ref, contrast_ref, image_ref, out_ref, held_real, held_imag):
    table = table_ref[...]
    count = image_ref.shape[0]
    for row in range(count):
        factor = contrast_ref[row : row + 1, :]
        factor = jnp.concatenate([factor, factor], axis=-1)
        weighted = (image_ref[row].astype(jnp.float32) * factor).astype(jnp.bfloat16)
        rows = pl.ds(row, ANGLES, stride=count)
        held_real[rows, :], held_imag[rows, :] = spectrum_of(weighted, table)
    shape = (ANGLES, count, CYCLES)
    out_ref[:, :, :CYCLES] = held_real[...].reshape(shape).astype(jnp.bfloat16)
    out_ref[:, :, CYCLES:] = held_imag[...].reshape(shape).astype(jnp.bfloat16)


def image_spectra(images, contrast_rows, table):
    particles = images.shape[0]
    count = 16
    return pl.pallas_call(
        spectra_kernel,
        grid=(particles // count,),
        in_specs=[
            pl.BlockSpec((2 * ANGLES, ANGLES), lambda i: (0, 0)),
            pl.BlockSpec((count, CYCLES), lambda i: (i, 0)),
            pl.BlockSpec((count, ANGLES, 2 * CYCLES), lambda i: (i, 0, 0)),
        ],
        out_specs=pl.BlockSpec((ANGLES, count, 2 * CYCLES), lambda i: (0, i, 0)),
        out_shape=jax.ShapeDtypeStruct((ANGLES, particles, 2 * CYCLES), jnp.bfloat16),
        scratch_shapes=[pltpu.VMEM((ANGLES * count, CYCLES), jnp.float32)] * 2,
        compiler_params=pltpu.CompilerParams(vmem_limit_bytes=8 * 1024 * 1024),
        cost_estimate=pl.CostEstimate(
            flops=particles * 4 * ANGLES * ANGLES * 2 * CYCLES,
            bytes_accessed=4 * particles * ANGLES * 2 * CYCLES,
            transcendentals=0,
        ),
    )(table, contrast_rows, images)


def pick_kernel(index_ref, source_ref, out_ref):
    for step in range(STEPS):
        at = index_ref[step]
        value = source_ref[at, step if source_ref.shape[1] == STEPS else 0]
        for copy in range(out_ref.shape[0]):
            out_ref[copy, step] = value


def pick(source, index, copies):
    return pl.pallas_call(
        pick_kernel,
        in_specs=[
            pl.BlockSpec(memory_space=pltpu.SMEM),
            pl.BlockSpec(memory_space=pltpu.VMEM),
        ],
        out_specs=pl.BlockSpec(memory_space=pltpu.VMEM),
        out_shape=jax.ShapeDtypeStruct((copies, STEPS, ANGLES, CYCLES), jnp.bfloat16),
        compiler_params=pltpu.CompilerParams(vmem_limit_bytes=2 * 1024 * 1024),
    )(index, source)


def score_kernel(
    core_ref,
    mine_ref,
    other_ref,
    source_ref,
    low_ref,
    turn_ref,
    back_ref,
    square_ref,
    prior_ref,
    member_ref,
    keep_ref,
    send_ref,
    top_ref,
    sum_ref,
    ref_real,
    ref_imag,
    corr,
    scores,
    power,
    spectra_ref,
    sem,
):
    particles = spectra_ref.shape[1]
    arriving = pltpu.make_async_copy(source_ref, spectra_ref, sem)
    arriving.start()
    first = core_ref[0] == 0
    table = low_ref[...]
    for c in range(CLS_GRP):
        mine, other = mine_ref[c], other_ref[c]
        polar = jnp.concatenate(
            [jnp.where(first, mine, other), jnp.where(first, other, mine)], axis=-1
        )
        real, imag = (
            part.astype(jnp.bfloat16).astype(jnp.float32) for part in spectrum_of(polar, table)
        )
        rows = pl.ds(c, ANGLES, stride=CLS_GRP)
        ref_real[rows, :], ref_imag[rows, :] = real, imag
        power[c : c + 1, :] = jnp.sum(real * real + imag * imag, axis=0, keepdims=True)
    square = square_ref[...]
    across = (((1,), (1,)), ((), ()))
    energy = 0.5 * lax.dot_general(
        power[...], square, across, precision=TOP_PRECISION, preferred_element_type=jnp.float32
    )
    arriving.wait()
    for m in range(ANGLES):
        rows = slice(m * CLS_GRP, (m + 1) * CLS_GRP)
        real, imag = ref_real[rows, :], ref_imag[rows, :]
        both = jnp.concatenate(
            [jnp.concatenate([real, -imag], axis=0), jnp.concatenate([imag, real], axis=0)],
            axis=-1,
        ).astype(jnp.bfloat16)
        corr[m * 2 * CLS_GRP : (m + 1) * 2 * CLS_GRP, :] = lax.dot_general(
            both, spectra_ref[m], across, preferred_element_type=jnp.float32
        )
    turn, prior = turn_ref[...], prior_ref[...]
    best = jnp.full((ANGLES, particles), -jnp.inf, jnp.float32)
    own = jnp.zeros((ANGLES, particles), jnp.float32)
    for c in range(0, CLS_GRP, 2):
        pair = [
            jnp.concatenate(
                [
                    corr[pl.ds(k, ANGLES, stride=2 * CLS_GRP), :],
                    corr[pl.ds(CLS_GRP + k, ANGLES, stride=2 * CLS_GRP), :],
                ],
                axis=0,
            )
            for k in (c, c + 1)
        ]
        rotated = jnp.dot(
            turn,
            jnp.concatenate(pair, axis=-1),
            precision=TOP_PRECISION,
            preferred_element_type=jnp.float32,
        )
        for k in range(2):
            value = rotated[:, k * particles : (k + 1) * particles]
            value = (value - energy[c + k : c + k + 1, :]) * (1.0 / ANGLES) + prior
            scores[c + k] = value
            best = jnp.maximum(best, value)
            own = own + jnp.where(member_ref[c + k : c + k + 1, :] > 0, value, 0.0)
    top = jnp.max(best, axis=0, keepdims=True)
    total = jnp.zeros((ANGLES, particles), jnp.float32)
    for c in range(CLS_GRP):
        total = total + jnp.exp(scores[c] - top)
    top_ref[...] = top
    sum_ref[...] = jnp.sum(total, axis=0, keepdims=True)
    weight = jnp.exp(own - jnp.max(own, axis=0, keepdims=True))
    weight = weight / jnp.sum(weight, axis=0, keepdims=True)
    turned_back = jnp.dot(
        back_ref[...], weight, precision=TOP_PRECISION, preferred_element_type=jnp.float32
    )
    h_real = turned_back[:particles].T
    h_imag = turned_back[particles:].T
    member = member_ref[...]
    chosen = member.astype(jnp.bfloat16)
    for m in range(ANGLES):
        x_real = spectra_ref[m, :, :CYCLES].astype(jnp.float32)
        x_imag = spectra_ref[m, :, CYCLES:].astype(jnp.float32)
        hr, hi = h_real[:, m : m + 1], h_imag[:, m : m + 1]
        aligned = jnp.concatenate(
            [x_real * hr - x_imag * hi, x_real * hi + x_imag * hr], axis=-1
        ).astype(jnp.bfloat16)
        sums = jnp.dot(chosen, aligned, preferred_element_type=jnp.float32)
        real_sum, imag_sum = sums[:, :CYCLES], sums[:, CYCLES:]
        keep_ref[m] = jnp.where(first, real_sum, imag_sum)
        send_ref[m] = jnp.where(first, imag_sum, real_sum)
    denom = jnp.dot(
        member, square, precision=TOP_PRECISION, preferred_element_type=jnp.float32
    )
    keep_ref[ANGLES] = denom
    send_ref[ANGLES] = denom


def score(core, mine, other, spectra, low_table, turn, back, square, prior, member):
    particles = spectra.shape[1]
    sums = jax.ShapeDtypeStruct((ANGLES + 1, CLS_GRP, CYCLES), jnp.float32)
    row = jax.ShapeDtypeStruct((1, particles), jnp.float32)
    vmem = pl.BlockSpec(memory_space=pltpu.VMEM)
    return pl.pallas_call(
        score_kernel,
        in_specs=[pl.BlockSpec(memory_space=pltpu.SMEM), vmem, vmem]
        + [pl.BlockSpec(memory_space=pltpu.HBM)]
        + [vmem] * 6,
        out_specs=(vmem, vmem, vmem, vmem),
        out_shape=(sums, sums, row, row),
        scratch_shapes=[
            pltpu.VMEM((ANGLES * CLS_GRP, CYCLES), jnp.float32),
            pltpu.VMEM((ANGLES * CLS_GRP, CYCLES), jnp.float32),
            pltpu.VMEM((ANGLES * 2 * CLS_GRP, particles), jnp.float32),
            pltpu.VMEM((CLS_GRP, ANGLES, particles), jnp.float32),
            pltpu.VMEM((CLS_GRP, CYCLES), jnp.float32),
            pltpu.VMEM((ANGLES, particles, 2 * CYCLES), jnp.bfloat16),
            pltpu.SemaphoreType.DMA,
        ],
        compiler_params=pltpu.CompilerParams(vmem_limit_bytes=20 * 1024 * 1024),
    )(core, mine, other, spectra, low_table, turn, back, square, prior, member)


def pack_kernel(keep_ref, got_ref, out_ref):
    denom = keep_ref[ANGLES] + got_ref[ANGLES]
    high = denom.astype(jnp.bfloat16)
    low = (denom - high.astype(jnp.float32)).astype(jnp.bfloat16)
    for z in range(out_ref.shape[0]):
        at = pl.ds(z * ROWS, ROWS)
        out_ref[z, :ROWS] = (keep_ref[at] + got_ref[at]).astype(jnp.bfloat16)
        out_ref[z, ROWS] = high if z == 0 else low


def pack(keep, got):
    vmem = pl.BlockSpec(memory_space=pltpu.VMEM)
    return pl.pallas_call(
        pack_kernel,
        in_specs=[vmem, vmem],
        out_specs=vmem,
        out_shape=jax.ShapeDtypeStruct((8, ROWS + 1, CLS_GRP, CYCLES), jnp.bfloat16),
        compiler_params=pltpu.CompilerParams(vmem_limit_bytes=4 * 1024 * 1024),
    )(keep, got)


def rotation_prior(rotation_rows):
    counting = jnp.arange(ANGLES, dtype=jnp.int32)
    distance = jnp.abs(counting[None, :] - rotation_rows[:, None])
    distance = jnp.minimum(distance, ANGLES - distance).astype(jnp.float32)
    return -0.5 * (distance / SIGMA_ROT) ** 2


def halve_kernel(blocks_ref, out_ref, sems):
    copies = [
        pltpu.make_async_copy(
            blocks_ref.at[:, :, half * CYCLES : (half + 1) * CYCLES], out_ref.at[:, half], sems.at[half]
        )
        for half in range(2)
    ]
    for copy in copies:
        copy.start()
    for copy in copies:
        copy.wait()


def halve(blocks):
    return pl.pallas_call(
        halve_kernel,
        in_specs=[pl.BlockSpec(memory_space=pltpu.HBM)],
        out_specs=pl.BlockSpec(memory_space=pltpu.HBM),
        out_shape=jax.ShapeDtypeStruct((BLOCK, 2, ANGLES, CYCLES), jnp.bfloat16),
        scratch_shapes=[pltpu.SemaphoreType.DMA((2,))],
        compiler_params=pltpu.CompilerParams(vmem_limit_bytes=1024 * 1024),
    )(blocks)


def route_kernel(core_ref, place_ref, got_ref, out_ref):
    total = got_ref[0].astype(jnp.float32)
    for z in range(1, got_ref.shape[0]):
        total = total + got_ref[z].astype(jnp.float32)
    denom = total[ROWS * CLS_GRP :]
    high = denom.astype(jnp.bfloat16).astype(jnp.float32)
    denom = jnp.where(core_ref[0] == 0, high, denom - high)
    share = jnp.concatenate([total[: ROWS * CLS_GRP], denom], axis=0).astype(jnp.bfloat16)
    rows, columns = (ROWS + 1) * OWN_MAX, (ROWS + 1) * CLS_GRP
    place = place_ref[...]
    line = lax.broadcasted_iota(jnp.int32, (rows, columns), 0)
    line = (line // OWN_MAX) * 1024 + line % OWN_MAX - place
    for owner in range(0, 64, 8):
        chosen = jnp.concatenate(
            [jnp.where(line == -OWN_MAX * (owner + k), 1.0, 0.0) for k in range(8)], axis=0
        ).astype(jnp.bfloat16)
        out_ref[owner * rows : (owner + 8) * rows, :] = jnp.dot(
            chosen, share, preferred_element_type=jnp.float32
        ).astype(jnp.bfloat16)


def route(core, place, got):
    vmem = pl.BlockSpec(memory_space=pltpu.VMEM)
    return pl.pallas_call(
        route_kernel,
        in_specs=[pl.BlockSpec(memory_space=pltpu.SMEM), vmem, vmem],
        out_specs=vmem,
        out_shape=jax.ShapeDtypeStruct((64 * (ROWS + 1) * OWN_MAX, CYCLES), jnp.bfloat16),
        compiler_params=pltpu.CompilerParams(vmem_limit_bytes=6 * 1024 * 1024),
    )(core, place, got)


def finish_kernel(table_ref, got_ref, out_ref, held):
    total = got_ref[0].astype(jnp.float32)
    for plane in range(1, got_ref.shape[0]):
        total = total + got_ref[plane].astype(jnp.float32)
    held[...] = total
    rows = (ROWS + 1) * OWN_MAX
    at = ROWS * OWN_MAX
    denom = total[at : at + OWN_MAX] + total[rows + at : rows + at + OWN_MAX]
    denom = denom + total[2 * rows + at : 2 * rows + at + OWN_MAX]
    scale = (1.0 / ANGLES) / (denom + TAU)
    for slot in range(0, OWN_MAX, 2):
        pair = [
            held[pl.ds(k, 16 * (ROWS + 1), stride=OWN_MAX), :] * scale[k : k + 1]
            for k in (slot, slot + 1)
        ]
        polar = jnp.dot(
            table_ref[...],
            jnp.concatenate(pair, axis=-1),
            precision=TOP_PRECISION,
            preferred_element_type=jnp.float32,
        ).astype(jnp.bfloat16)
        for k in range(2):
            columns = slice(k * CYCLES, (k + 1) * CYCLES)
            out_ref[slot + k, :, :CYCLES] = polar[:ANGLES, columns]
            out_ref[slot + k, :, CYCLES:] = polar[ANGLES:, columns]


def finish(table, got):
    vmem = pl.BlockSpec(memory_space=pltpu.VMEM)
    return pl.pallas_call(
        finish_kernel,
        in_specs=[vmem, vmem],
        out_specs=vmem,
        out_shape=jax.ShapeDtypeStruct((OWN_MAX, ANGLES, 2 * CYCLES), jnp.bfloat16),
        scratch_shapes=[pltpu.VMEM((16 * (ROWS + 1) * OWN_MAX, CYCLES), jnp.float32)],
        compiler_params=pltpu.CompilerParams(vmem_limit_bytes=6 * 1024 * 1024),
    )(table, got)


def finish_table(cosine_table, sine_table):
    def laid(table):
        table = table.reshape(ANGLES, 8, 1, ROWS)
        return jnp.pad(table, ((0, 0), (0, 0), (0, 0), (0, 1)))

    cosine, sine = laid(cosine_table), laid(sine_table)
    real = jnp.concatenate([cosine, -sine], axis=2).reshape(ANGLES, 16 * (ROWS + 1))
    imag = jnp.concatenate([sine, cosine], axis=2).reshape(ANGLES, 16 * (ROWS + 1))
    return jnp.concatenate([real, imag])


def fetch(blocks, holders):
    halves = halve(blocks).reshape(BLOCK * 2, ANGLES, CYCLES)
    sliced = lax.all_to_all(halves, ("wide_1", "wide_2"), 0, 0, tiled=True)
    picked = pick(sliced[:, None], holders % 16, 4)
    planes = lax.all_to_all(picked, "wide_0", 0, 0, tiled=True)
    picked = pick(planes, holders // 16, 8)
    return lax.all_to_all(picked, "wide_1", 0, 0, tiled=True).reshape(CLS_GRP, ANGLES, CYCLES)


def joined_evidence(top, total):
    for bit in (1, 2, 4):
        pair = jnp.concatenate([top, total])
        got = lax.ppermute(pair, "narrow", [(k, k ^ bit) for k in range(8)])
        joined = jnp.maximum(top, got[:1])
        total = total * jnp.exp(top - joined) + got[1:] * jnp.exp(got[:1] - joined)
        top = joined
    return (top + jnp.log(total)).reshape(-1)


def per_device(images, defocus, class_index, rotation_index, owner_map, roster, ref_store):
    class_group = lax.axis_index("narrow")
    core = lax.axis_index("wide_2")
    cosine_table, sine_table = angle_tables(ANGLES)
    cosines_low = cosine_table.astype(jnp.bfloat16)
    sines_low = sine_table.astype(jnp.bfloat16)
    leading_class = class_group * CLS_GRP
    arrival = jnp.arange(CLS_GRP, dtype=jnp.int32)
    within = arrival % STEPS * BLOCK + arrival // STEPS
    class_ids = leading_class + within
    holders = lax.dynamic_index_in_dim(roster, class_group, 0, keepdims=False)

    low_table = jnp.concatenate([cosines_low, sines_low])
    turn = jnp.concatenate([cosine_table, -sine_table], axis=-1)
    filled = ((0, CYCLES - ANGLES), (0, 0))
    back = jnp.concatenate([jnp.pad(cosine_table, filled), jnp.pad(sine_table, filled)])
    contrast_rows = contrast(defocus)
    square = contrast_rows * contrast_rows
    prior = rotation_prior(rotation_index).T
    member = (class_index[None, :] == class_ids[:, None]).astype(jnp.float32)
    spectra = image_spectra(images, contrast_rows, low_table)

    mine = fetch(ref_store[0, 0], holders)
    other = swapped(mine)
    keep, send, top, total = score(
        core.reshape(1), mine, other, spectra, low_table, turn, back, square, prior, member
    )
    owners = lax.dynamic_slice_in_dim(owner_map, leading_class, CLS_GRP)
    owners = owners.reshape(STEPS, BLOCK).T.reshape(CLS_GRP)
    same = owners[:, None] == owners[None, :]
    ranking = jnp.sum(same & (within[None, :] < within[:, None]), axis=1)
    place = owners * OWN_MAX + ranking
    place = jnp.arange(ROWS + 1, dtype=jnp.int32)[:, None] * 1024 + place[None, :]
    place = place.reshape(1, (ROWS + 1) * CLS_GRP)
    table = finish_table(cosine_table, sine_table)
    share = pack(keep, swapped(send)).reshape(8, (ROWS + 1) * CLS_GRP, CYCLES)
    top, total, share = lax.optimization_barrier((top, total, share))
    share = lax.all_to_all(share, "wide_1", 0, 0, tiled=True)
    log_evidence = joined_evidence(top, total)
    share, log_evidence = lax.optimization_barrier((share, log_evidence))
    sent = route(core.reshape(1), place, share).reshape(64, (ROWS + 1) * OWN_MAX, CYCLES)
    got = lax.all_to_all(sent, WIDE, 0, 0, tiled=True)
    got = got.reshape(4, 16 * (ROWS + 1) * OWN_MAX, CYCLES)
    new_references = finish(table, got).reshape(1, 1, OWN_MAX, ANGLES, 2 * CYCLES)
    return (new_references, log_evidence)


def solution(mesh):
    split = Mesh(
        mesh.devices.reshape(4, 8, 2, mesh.shape["narrow"]),
        ("wide_0", "wide_1", "wide_2", "narrow"),
    )
    placed = (
        P(WIDE, None, None),
        P(WIDE),
        P(WIDE),
        P(WIDE),
        P(),
        P(),
        P(WIDE, "narrow", None, None, None),
    )
    return jax.shard_map(
        per_device,
        mesh=split,
        in_specs=placed,
        out_specs=(P(WIDE, "narrow", None, None, None), P(WIDE)),
        check_vma=False,
    )
```

```python
import math

import jax
import jax.numpy as jnp
from jax import lax
from jax.experimental import pallas as pl
from jax.experimental.pallas import tpu as pltpu
from jax.sharding import Mesh
from jax.sharding import PartitionSpec as P

CYCLES = 128
ANGLES = 72
STEPS = 3
BLOCK = 8
OWN_MAX = 4
CLS_GRP = 24
SIGMA_ROT = 8
ROWS = 9
WIDE = ("wide_0", "wide_1", "wide_2")


TAU = 1.0
CONTRAST = 0.1
TOP_PRECISION = lax.Precision.HIGHEST


def swapped(x):
    return lax.ppermute(x, "wide_2", [(0, 1), (1, 0)])


def angle_tables(length):
    counting = jnp.arange(length, dtype=jnp.int32)
    products = counting[:, None] * counting[None, :] % length
    phase_angle = products.astype(jnp.float32) * (2.0 * math.pi / length)
    return (jnp.cos(phase_angle), jnp.sin(phase_angle))


def contrast(defocus_rows):
    cycle_freq = (jnp.arange(CYCLES, dtype=jnp.float32) + 1.0) / CYCLES
    phase_angle = 8.0 * math.pi * defocus_rows[:, None] * cycle_freq[None, :] ** 2
    return -jnp.sin(phase_angle) - CONTRAST * jnp.cos(phase_angle)


def spectrum_of(polar, table):
    both = jnp.dot(table, polar, preferred_element_type=jnp.float32)
    cos_part, sin_part = both[:ANGLES], both[ANGLES:]
    real_part = cos_part[:, :CYCLES] + sin_part[:, CYCLES:]
    imag_part = cos_part[:, CYCLES:] - sin_part[:, :CYCLES]
    return real_part, imag_part


def spectra_kernel(table_ref, contrast_ref, image_ref, out_ref, held_real, held_imag):
    table = table_ref[...]
    count = image_ref.shape[0]
    for row in range(count):
        factor = contrast_ref[row : row + 1, :]
        factor = jnp.concatenate([factor, factor], axis=-1)
        weighted = (image_ref[row].astype(jnp.float32) * factor).astype(jnp.bfloat16)
        rows = pl.ds(row, ANGLES, stride=count)
        held_real[rows, :], held_imag[rows, :] = spectrum_of(weighted, table)
    shape = (ANGLES, count, CYCLES)
    out_ref[:, :, :CYCLES] = held_real[...].reshape(shape).astype(jnp.bfloat16)
    out_ref[:, :, CYCLES:] = held_imag[...].reshape(shape).astype(jnp.bfloat16)


def image_spectra(images, half, contrast_rows, table):
    particles = contrast_rows.shape[0]
    count = 16
    skipped = half * particles // count
    return pl.pallas_call(
        spectra_kernel,
        grid=(particles // count,),
        in_specs=[
            pl.BlockSpec((2 * ANGLES, ANGLES), lambda i: (0, 0)),
            pl.BlockSpec((count, CYCLES), lambda i: (i, 0)),
            pl.BlockSpec((count, ANGLES, 2 * CYCLES), lambda i: (i + skipped, 0, 0)),
        ],
        out_specs=pl.BlockSpec((ANGLES, count, 2 * CYCLES), lambda i: (0, i, 0)),
        out_shape=jax.ShapeDtypeStruct((ANGLES, particles, 2 * CYCLES), jnp.bfloat16),
        scratch_shapes=[pltpu.VMEM((ANGLES * count, CYCLES), jnp.float32)] * 2,
        compiler_params=pltpu.CompilerParams(vmem_limit_bytes=56 * 1024 * 1024),
        cost_estimate=pl.CostEstimate(
            flops=particles * 4 * ANGLES * ANGLES * 2 * CYCLES,
            bytes_accessed=4 * particles * ANGLES * 2 * CYCLES,
            transcendentals=0,
        ),
    )(table, contrast_rows, images)


def pick_kernel(index_ref, source_ref, out_ref):
    for step in range(STEPS):
        at = index_ref[step]
        value = source_ref[at, step if source_ref.shape[1] == STEPS else 0]
        for copy in range(out_ref.shape[0]):
            out_ref[copy, step] = value


def pick(source, index, copies):
    return pl.pallas_call(
        pick_kernel,
        in_specs=[
            pl.BlockSpec(memory_space=pltpu.SMEM),
            pl.BlockSpec(memory_space=pltpu.VMEM),
        ],
        out_specs=pl.BlockSpec(memory_space=pltpu.VMEM),
        out_shape=jax.ShapeDtypeStruct((copies, STEPS, ANGLES, CYCLES), jnp.bfloat16),
        compiler_params=pltpu.CompilerParams(vmem_limit_bytes=2 * 1024 * 1024),
    )(index, source)


def score_kernel(
    core_ref,
    mine_ref,
    other_ref,
    early_ref,
    late_ref,
    low_ref,
    turn_ref,
    back_ref,
    square_ref,
    prior_ref,
    member_ref,
    keep_ref,
    send_ref,
    top_ref,
    sum_ref,
    ref_real,
    ref_imag,
    corr,
    scores,
    power,
    spectra_ref,
    sem,
):
    particles = spectra_ref.shape[1]
    arriving = [
        pltpu.make_async_copy(
            source, spectra_ref.at[:, pl.ds(k * particles // 2, particles // 2)], sem.at[k]
        )
        for k, source in enumerate((early_ref, late_ref))
    ]
    for copy in arriving:
        copy.start()
    first = core_ref[0] == 0
    table = low_ref[...]
    for c in range(CLS_GRP):
        mine, other = mine_ref[c], other_ref[c]
        polar = jnp.concatenate(
            [jnp.where(first, mine, other), jnp.where(first, other, mine)], axis=-1
        )
        real, imag = (
            part.astype(jnp.bfloat16).astype(jnp.float32) for part in spectrum_of(polar, table)
        )
        rows = pl.ds(c, ANGLES, stride=CLS_GRP)
        ref_real[rows, :], ref_imag[rows, :] = real, imag
        power[c : c + 1, :] = jnp.sum(real * real + imag * imag, axis=0, keepdims=True)
    square = square_ref[...]
    across = (((1,), (1,)), ((), ()))
    energy = 0.5 * lax.dot_general(
        power[...], square, across, precision=TOP_PRECISION, preferred_element_type=jnp.float32
    )
    for copy in arriving:
        copy.wait()
    for m in range(ANGLES):
        rows = slice(m * CLS_GRP, (m + 1) * CLS_GRP)
        real, imag = ref_real[rows, :], ref_imag[rows, :]
        both = jnp.concatenate(
            [jnp.concatenate([real, -imag], axis=0), jnp.concatenate([imag, real], axis=0)],
            axis=-1,
        ).astype(jnp.bfloat16)
        corr[m * 2 * CLS_GRP : (m + 1) * 2 * CLS_GRP, :] = lax.dot_general(
            both, spectra_ref[m], across, preferred_element_type=jnp.float32
        )
    turn, prior = turn_ref[...], prior_ref[...]
    best = jnp.full((ANGLES, particles), -jnp.inf, jnp.float32)
    own = jnp.zeros((ANGLES, particles), jnp.float32)
    for c in range(0, CLS_GRP, 2):
        pair = [
            jnp.concatenate(
                [
                    corr[pl.ds(k, ANGLES, stride=2 * CLS_GRP), :],
                    corr[pl.ds(CLS_GRP + k, ANGLES, stride=2 * CLS_GRP), :],
                ],
                axis=0,
            )
            for k in (c, c + 1)
        ]
        rotated = jnp.dot(
            turn,
            jnp.concatenate(pair, axis=-1),
            precision=TOP_PRECISION,
            preferred_element_type=jnp.float32,
        )
        for k in range(2):
            value = rotated[:, k * particles : (k + 1) * particles]
            value = (value - energy[c + k : c + k + 1, :]) * (1.0 / ANGLES) + prior
            scores[c + k] = value
            best = jnp.maximum(best, value)
            own = own + jnp.where(member_ref[c + k : c + k + 1, :] > 0, value, 0.0)
    top = jnp.max(best, axis=0, keepdims=True)
    total = jnp.zeros((ANGLES, particles), jnp.float32)
    for c in range(CLS_GRP):
        total = total + jnp.exp(scores[c] - top)
    top_ref[...] = top
    sum_ref[...] = jnp.sum(total, axis=0, keepdims=True)
    weight = jnp.exp(own - jnp.max(own, axis=0, keepdims=True))
    weight = weight / jnp.sum(weight, axis=0, keepdims=True)
    turned_back = jnp.dot(
        back_ref[...], weight, precision=TOP_PRECISION, preferred_element_type=jnp.float32
    )
    h_real = turned_back[:particles].T
    h_imag = turned_back[particles:].T
    member = member_ref[...]
    chosen = member.astype(jnp.bfloat16)
    for m in range(ANGLES):
        x_real = spectra_ref[m, :, :CYCLES].astype(jnp.float32)
        x_imag = spectra_ref[m, :, CYCLES:].astype(jnp.float32)
        hr, hi = h_real[:, m : m + 1], h_imag[:, m : m + 1]
        aligned = jnp.concatenate(
            [x_real * hr - x_imag * hi, x_real * hi + x_imag * hr], axis=-1
        ).astype(jnp.bfloat16)
        sums = jnp.dot(chosen, aligned, preferred_element_type=jnp.float32)
        real_sum, imag_sum = sums[:, :CYCLES], sums[:, CYCLES:]
        keep_ref[m] = jnp.where(first, real_sum, imag_sum)
        send_ref[m] = jnp.where(first, imag_sum, real_sum)
    denom = jnp.dot(
        member, square, precision=TOP_PRECISION, preferred_element_type=jnp.float32
    )
    keep_ref[ANGLES] = denom
    send_ref[ANGLES] = denom


def score(core, mine, other, early, late, low_table, turn, back, square, prior, member):
    particles = 2 * early.shape[1]
    sums = jax.ShapeDtypeStruct((ANGLES + 1, CLS_GRP, CYCLES), jnp.float32)
    row = jax.ShapeDtypeStruct((1, particles), jnp.float32)
    vmem = pl.BlockSpec(memory_space=pltpu.VMEM)
    return pl.pallas_call(
        score_kernel,
        in_specs=[pl.BlockSpec(memory_space=pltpu.SMEM), vmem, vmem]
        + [pl.BlockSpec(memory_space=pltpu.HBM)] * 2
        + [vmem] * 6,
        out_specs=(vmem, vmem, vmem, vmem),
        out_shape=(sums, sums, row, row),
        scratch_shapes=[
            pltpu.VMEM((ANGLES * CLS_GRP, CYCLES), jnp.float32),
            pltpu.VMEM((ANGLES * CLS_GRP, CYCLES), jnp.float32),
            pltpu.VMEM((ANGLES * 2 * CLS_GRP, particles), jnp.float32),
            pltpu.VMEM((CLS_GRP, ANGLES, particles), jnp.float32),
            pltpu.VMEM((CLS_GRP, CYCLES), jnp.float32),
            pltpu.VMEM((ANGLES, particles, 2 * CYCLES), jnp.bfloat16),
            pltpu.SemaphoreType.DMA((2,)),
        ],
        compiler_params=pltpu.CompilerParams(vmem_limit_bytes=50 * 1024 * 1024),
    )(core, mine, other, early, late, low_table, turn, back, square, prior, member)


def pack_kernel(keep_ref, got_ref, out_ref):
    denom = keep_ref[ANGLES] + got_ref[ANGLES]
    high = denom.astype(jnp.bfloat16)
    low = (denom - high.astype(jnp.float32)).astype(jnp.bfloat16)
    for z in range(out_ref.shape[0]):
        at = pl.ds(z * ROWS, ROWS)
        out_ref[z, :ROWS] = (keep_ref[at] + got_ref[at]).astype(jnp.bfloat16)
        out_ref[z, ROWS] = high if z == 0 else low


def pack(keep, got):
    vmem = pl.BlockSpec(memory_space=pltpu.VMEM)
    return pl.pallas_call(
        pack_kernel,
        in_specs=[vmem, vmem],
        out_specs=vmem,
        out_shape=jax.ShapeDtypeStruct((8, ROWS + 1, CLS_GRP, CYCLES), jnp.bfloat16),
        compiler_params=pltpu.CompilerParams(vmem_limit_bytes=4 * 1024 * 1024),
    )(keep, got)


def rotation_prior(rotation_rows):
    counting = jnp.arange(ANGLES, dtype=jnp.int32)
    distance = jnp.abs(counting[None, :] - rotation_rows[:, None])
    distance = jnp.minimum(distance, ANGLES - distance).astype(jnp.float32)
    return -0.5 * (distance / SIGMA_ROT) ** 2


def halve_kernel(blocks_ref, out_ref, sems):
    copies = [
        pltpu.make_async_copy(
            blocks_ref.at[:, :, half * CYCLES : (half + 1) * CYCLES], out_ref.at[:, half], sems.at[half]
        )
        for half in range(2)
    ]
    for copy in copies:
        copy.start()
    for copy in copies:
        copy.wait()


def halve(blocks):
    return pl.pallas_call(
        halve_kernel,
        in_specs=[pl.BlockSpec(memory_space=pltpu.HBM)],
        out_specs=pl.BlockSpec(memory_space=pltpu.HBM),
        out_shape=jax.ShapeDtypeStruct((BLOCK, 2, ANGLES, CYCLES), jnp.bfloat16),
        scratch_shapes=[pltpu.SemaphoreType.DMA((2,))],
        compiler_params=pltpu.CompilerParams(vmem_limit_bytes=62 * 1024 * 1024),
    )(blocks)


def route_kernel(core_ref, place_ref, got_ref, out_ref):
    total = got_ref[0].astype(jnp.float32)
    for z in range(1, got_ref.shape[0]):
        total = total + got_ref[z].astype(jnp.float32)
    denom = total[ROWS * CLS_GRP :]
    high = denom.astype(jnp.bfloat16).astype(jnp.float32)
    denom = jnp.where(core_ref[0] == 0, high, denom - high)
    share = jnp.concatenate([total[: ROWS * CLS_GRP], denom], axis=0).astype(jnp.bfloat16)
    rows, columns = (ROWS + 1) * OWN_MAX, (ROWS + 1) * CLS_GRP
    place = place_ref[...]
    line = lax.broadcasted_iota(jnp.int32, (rows, columns), 0)
    line = (line // OWN_MAX) * 1024 + line % OWN_MAX - place
    for owner in range(0, 64, 8):
        chosen = jnp.concatenate(
            [jnp.where(line == -OWN_MAX * (owner + k), 1.0, 0.0) for k in range(8)], axis=0
        ).astype(jnp.bfloat16)
        out_ref[owner * rows : (owner + 8) * rows, :] = jnp.dot(
            chosen, share, preferred_element_type=jnp.float32
        ).astype(jnp.bfloat16)


def route(core, place, got):
    vmem = pl.BlockSpec(memory_space=pltpu.VMEM)
    return pl.pallas_call(
        route_kernel,
        in_specs=[pl.BlockSpec(memory_space=pltpu.SMEM), vmem, vmem],
        out_specs=vmem,
        out_shape=jax.ShapeDtypeStruct((64 * (ROWS + 1) * OWN_MAX, CYCLES), jnp.bfloat16),
        compiler_params=pltpu.CompilerParams(vmem_limit_bytes=6 * 1024 * 1024),
    )(core, place, got)


def finish_kernel(table_ref, got_ref, out_ref, held):
    total = got_ref[0].astype(jnp.float32)
    for plane in range(1, got_ref.shape[0]):
        total = total + got_ref[plane].astype(jnp.float32)
    held[...] = total
    rows = (ROWS + 1) * OWN_MAX
    at = ROWS * OWN_MAX
    denom = total[at : at + OWN_MAX] + total[rows + at : rows + at + OWN_MAX]
    denom = denom + total[2 * rows + at : 2 * rows + at + OWN_MAX]
    scale = (1.0 / ANGLES) / (denom + TAU)
    for slot in range(0, OWN_MAX, 2):
        pair = [
            held[pl.ds(k, 16 * (ROWS + 1), stride=OWN_MAX), :] * scale[k : k + 1]
            for k in (slot, slot + 1)
        ]
        polar = jnp.dot(
            table_ref[...],
            jnp.concatenate(pair, axis=-1),
            precision=TOP_PRECISION,
            preferred_element_type=jnp.float32,
        ).astype(jnp.bfloat16)
        for k in range(2):
            columns = slice(k * CYCLES, (k + 1) * CYCLES)
            out_ref[slot + k, :, :CYCLES] = polar[:ANGLES, columns]
            out_ref[slot + k, :, CYCLES:] = polar[ANGLES:, columns]


def finish(table, got):
    vmem = pl.BlockSpec(memory_space=pltpu.VMEM)
    return pl.pallas_call(
        finish_kernel,
        in_specs=[vmem, vmem],
        out_specs=vmem,
        out_shape=jax.ShapeDtypeStruct((OWN_MAX, ANGLES, 2 * CYCLES), jnp.bfloat16),
        scratch_shapes=[pltpu.VMEM((16 * (ROWS + 1) * OWN_MAX, CYCLES), jnp.float32)],
        compiler_params=pltpu.CompilerParams(vmem_limit_bytes=6 * 1024 * 1024),
    )(table, got)


def finish_table(cosine_table, sine_table):
    def laid(table):
        table = table.reshape(ANGLES, 8, 1, ROWS)
        return jnp.pad(table, ((0, 0), (0, 0), (0, 0), (0, 1)))

    cosine, sine = laid(cosine_table), laid(sine_table)
    real = jnp.concatenate([cosine, -sine], axis=2).reshape(ANGLES, 16 * (ROWS + 1))
    imag = jnp.concatenate([sine, cosine], axis=2).reshape(ANGLES, 16 * (ROWS + 1))
    return jnp.concatenate([real, imag])


def fetch(blocks, holders, images, contrast_rows, table):
    half = contrast_rows.shape[0] // 2
    halves = halve(blocks).reshape(BLOCK * 2, ANGLES, CYCLES)
    sliced = lax.all_to_all(halves, ("wide_1", "wide_2"), 0, 0, tiled=True)
    early = image_spectra(images, 0, contrast_rows[:half], table)
    sliced, early, later = lax.optimization_barrier((sliced, early, contrast_rows[half:]))
    picked = pick(sliced[:, None], holders % 16, 4)
    planes = lax.all_to_all(picked, "wide_0", 0, 0, tiled=True)
    late = image_spectra(images, 1, later, table)
    planes, late = lax.optimization_barrier((planes, late))
    picked = pick(planes, holders // 16, 8)
    mine = lax.all_to_all(picked, "wide_1", 0, 0, tiled=True).reshape(CLS_GRP, ANGLES, CYCLES)
    return mine, early, late


def exchanged_evidence(top, total, bit):
    pair = jnp.concatenate([top, total])
    got = lax.ppermute(pair, "narrow", [(k, k ^ bit) for k in range(8)])
    joined = jnp.maximum(top, got[:1])
    return joined, total * jnp.exp(top - joined) + got[1:] * jnp.exp(got[:1] - joined)


def per_device(images, defocus, class_index, rotation_index, owner_map, roster, ref_store):
    class_group = lax.axis_index("narrow")
    core = lax.axis_index("wide_2")
    cosine_table, sine_table = angle_tables(ANGLES)
    cosines_low = cosine_table.astype(jnp.bfloat16)
    sines_low = sine_table.astype(jnp.bfloat16)
    leading_class = class_group * CLS_GRP
    arrival = jnp.arange(CLS_GRP, dtype=jnp.int32)
    within = arrival % STEPS * BLOCK + arrival // STEPS
    class_ids = leading_class + within
    holders = lax.dynamic_index_in_dim(roster, class_group, 0, keepdims=False)

    low_table = jnp.concatenate([cosines_low, sines_low])
    turn = jnp.concatenate([cosine_table, -sine_table], axis=-1)
    filled = ((0, CYCLES - ANGLES), (0, 0))
    back = jnp.concatenate([jnp.pad(cosine_table, filled), jnp.pad(sine_table, filled)])
    contrast_rows = contrast(defocus)
    square = contrast_rows * contrast_rows
    prior = rotation_prior(rotation_index).T
    member = (class_index[None, :] == class_ids[:, None]).astype(jnp.float32)
    mine, early, late = fetch(ref_store[0, 0], holders, images, contrast_rows, low_table)
    other = swapped(mine)
    keep, send, top, total = score(
        core.reshape(1), mine, other, early, late, low_table, turn, back, square, prior, member
    )
    owners = lax.dynamic_slice_in_dim(owner_map, leading_class, CLS_GRP)
    owners = owners.reshape(STEPS, BLOCK).T.reshape(CLS_GRP)
    same = owners[:, None] == owners[None, :]
    ranking = jnp.sum(same & (within[None, :] < within[:, None]), axis=1)
    place = owners * OWN_MAX + ranking
    place = jnp.arange(ROWS + 1, dtype=jnp.int32)[:, None] * 1024 + place[None, :]
    place = place.reshape(1, (ROWS + 1) * CLS_GRP)
    table = finish_table(cosine_table, sine_table)
    share = pack(keep, swapped(send)).reshape(8, (ROWS + 1) * CLS_GRP, CYCLES)
    top, total, share = lax.optimization_barrier((top, total, share))
    share = lax.all_to_all(share, "wide_1", 0, 0, tiled=True)
    top, total = exchanged_evidence(top, total, 1)
    share, top, total = lax.optimization_barrier((share, top, total))
    sent = route(core.reshape(1), place, share).reshape(64, (ROWS + 1) * OWN_MAX, CYCLES)
    top, total, sent = lax.optimization_barrier((top, total, sent))
    got = lax.all_to_all(sent, WIDE, 0, 0, tiled=True)
    got = got.reshape(4, 16 * (ROWS + 1) * OWN_MAX, CYCLES)
    top, total = exchanged_evidence(top, total, 2)
    top, total = exchanged_evidence(top, total, 4)
    log_evidence = (top + jnp.log(total)).reshape(-1)
    new_references = finish(table, got).reshape(1, 1, OWN_MAX, ANGLES, 2 * CYCLES)
    return (new_references, log_evidence)


def solution(mesh):
    split = Mesh(
        mesh.devices.reshape(4, 8, 2, mesh.shape["narrow"]),
        ("wide_0", "wide_1", "wide_2", "narrow"),
    )
    placed = (
        P(WIDE, None, None),
        P(WIDE),
        P(WIDE),
        P(WIDE),
        P(),
        P(),
        P(WIDE, "narrow", None, None, None),
    )
    return jax.shard_map(
        per_device,
        mesh=split,
        in_specs=placed,
        out_specs=(P(WIDE, "narrow", None, None, None), P(WIDE)),
        check_vma=False,
    )
```

```python
import math

import jax
import jax.numpy as jnp
from jax import lax
from jax.experimental import pallas as pl
from jax.experimental.pallas import tpu as pltpu
from jax.sharding import Mesh
from jax.sharding import PartitionSpec as P

CYCLES = 128
ANGLES = 72
STEPS = 3
BLOCK = 8
OWN_MAX = 4
CLS_GRP = 24
SIGMA_ROT = 8
ROWS = 9
EVIDENCE_ROWS = 256
CHUNKS = 4
WIDE = ("wide_0", "wide_1", "wide_2")


TAU = 1.0
CONTRAST = 0.1
TOP_PRECISION = lax.Precision.HIGHEST


def swapped(x):
    return lax.ppermute(x, "wide_2", [(0, 1), (1, 0)])


def angle_tables(length):
    counting = jnp.arange(length, dtype=jnp.int32)
    products = counting[:, None] * counting[None, :] % length
    phase_angle = products.astype(jnp.float32) * (2.0 * math.pi / length)
    return (jnp.cos(phase_angle), jnp.sin(phase_angle))


def contrast(defocus_rows):
    cycle_freq = (jnp.arange(CYCLES, dtype=jnp.float32) + 1.0) / CYCLES
    phase_angle = 8.0 * math.pi * defocus_rows[:, None] * cycle_freq[None, :] ** 2
    return -jnp.sin(phase_angle) - CONTRAST * jnp.cos(phase_angle)


def spectrum_of(polar, table):
    both = jnp.dot(table, polar, preferred_element_type=jnp.float32)
    cos_part, sin_part = both[:ANGLES], both[ANGLES:]
    real_part = cos_part[:, :CYCLES] + sin_part[:, CYCLES:]
    imag_part = cos_part[:, CYCLES:] - sin_part[:, :CYCLES]
    return real_part, imag_part


def spectra_kernel(table_ref, contrast_ref, image_ref, out_ref, held_real, held_imag):
    table = table_ref[...]
    count = image_ref.shape[0]
    for row in range(count):
        factor = contrast_ref[row : row + 1, :]
        factor = jnp.concatenate([factor, factor], axis=-1)
        weighted = (image_ref[row].astype(jnp.float32) * factor).astype(jnp.bfloat16)
        rows = pl.ds(row, ANGLES, stride=count)
        held_real[rows, :], held_imag[rows, :] = spectrum_of(weighted, table)
    shape = (ANGLES, count, CYCLES)
    out_ref[:, :, :CYCLES] = held_real[...].reshape(shape).astype(jnp.bfloat16)
    out_ref[:, :, CYCLES:] = held_imag[...].reshape(shape).astype(jnp.bfloat16)


def image_spectra(images, half, contrast_rows, table):
    particles = contrast_rows.shape[0]
    count = 16
    skipped = half * particles // count
    return pl.pallas_call(
        spectra_kernel,
        grid=(particles // count,),
        in_specs=[
            pl.BlockSpec((2 * ANGLES, ANGLES), lambda i: (0, 0)),
            pl.BlockSpec((count, CYCLES), lambda i: (i, 0)),
            pl.BlockSpec((count, ANGLES, 2 * CYCLES), lambda i: (i + skipped, 0, 0)),
        ],
        out_specs=pl.BlockSpec((ANGLES, count, 2 * CYCLES), lambda i: (0, i, 0)),
        out_shape=jax.ShapeDtypeStruct((ANGLES, particles, 2 * CYCLES), jnp.bfloat16),
        scratch_shapes=[pltpu.VMEM((ANGLES * count, CYCLES), jnp.float32)] * 2,
        compiler_params=pltpu.CompilerParams(vmem_limit_bytes=56 * 1024 * 1024),
        cost_estimate=pl.CostEstimate(
            flops=particles * 4 * ANGLES * ANGLES * 2 * CYCLES,
            bytes_accessed=4 * particles * ANGLES * 2 * CYCLES,
            transcendentals=0,
        ),
    )(table, contrast_rows, images)


def pick_kernel(index_ref, source_ref, out_ref):
    for step in range(STEPS):
        at = index_ref[step]
        value = source_ref[at, step if source_ref.shape[1] == STEPS else 0]
        for copy in range(out_ref.shape[0]):
            out_ref[copy, step] = value


def pick(source, index, copies):
    return pl.pallas_call(
        pick_kernel,
        in_specs=[
            pl.BlockSpec(memory_space=pltpu.SMEM),
            pl.BlockSpec(memory_space=pltpu.VMEM),
        ],
        out_specs=pl.BlockSpec(memory_space=pltpu.VMEM),
        out_shape=jax.ShapeDtypeStruct((copies, STEPS, ANGLES, CYCLES), jnp.bfloat16),
        compiler_params=pltpu.CompilerParams(vmem_limit_bytes=2 * 1024 * 1024),
    )(index, source)


def score_kernel(
    core_ref,
    mine_ref,
    other_ref,
    early_ref,
    late_ref,
    low_ref,
    turn_ref,
    back_ref,
    square_ref,
    prior_ref,
    member_ref,
    keep_ref,
    send_ref,
    evidence_ref,
    ref_real,
    ref_imag,
    corr,
    scores,
    power,
    spectra_ref,
    sem,
):
    particles = spectra_ref.shape[1]
    depth, half = ANGLES // CHUNKS, particles // 2
    arriving = [
        pltpu.make_async_copy(
            source.at[pl.ds(n * depth, depth)],
            spectra_ref.at[pl.ds(n * depth, depth), pl.ds(k * half, half)],
            sem.at[n, k],
        )
        for n in range(CHUNKS)
        for k, source in enumerate((early_ref, late_ref))
    ]
    for copy in arriving:
        copy.start()
    first = core_ref[0] == 0
    table = low_ref[...]
    for c in range(CLS_GRP):
        mine, other = mine_ref[c], other_ref[c]
        polar = jnp.concatenate(
            [jnp.where(first, mine, other), jnp.where(first, other, mine)], axis=-1
        )
        real, imag = (
            part.astype(jnp.bfloat16).astype(jnp.float32) for part in spectrum_of(polar, table)
        )
        rows = pl.ds(c, ANGLES, stride=CLS_GRP)
        ref_real[rows, :], ref_imag[rows, :] = real, imag
        power[c : c + 1, :] = jnp.sum(real * real + imag * imag, axis=0, keepdims=True)
    square = square_ref[...]
    across = (((1,), (1,)), ((), ()))
    energy = 0.5 * lax.dot_general(
        power[...], square, across, precision=TOP_PRECISION, preferred_element_type=jnp.float32
    )
    for m in range(ANGLES):
        if m % depth == 0:
            for copy in arriving[m // depth * 2 : m // depth * 2 + 2]:
                copy.wait()
        rows = slice(m * CLS_GRP, (m + 1) * CLS_GRP)
        real, imag = ref_real[rows, :], ref_imag[rows, :]
        both = jnp.concatenate(
            [jnp.concatenate([real, -imag], axis=0), jnp.concatenate([imag, real], axis=0)],
            axis=-1,
        ).astype(jnp.bfloat16)
        corr[m * 2 * CLS_GRP : (m + 1) * 2 * CLS_GRP, :] = lax.dot_general(
            both, spectra_ref[m], across, preferred_element_type=jnp.float32
        )
    turn, prior = turn_ref[...], prior_ref[...]
    best = jnp.full((ANGLES, particles), -jnp.inf, jnp.float32)
    own = jnp.zeros((ANGLES, particles), jnp.float32)
    for c in range(0, CLS_GRP, 2):
        pair = [
            jnp.concatenate(
                [
                    corr[pl.ds(k, ANGLES, stride=2 * CLS_GRP), :],
                    corr[pl.ds(CLS_GRP + k, ANGLES, stride=2 * CLS_GRP), :],
                ],
                axis=0,
            )
            for k in (c, c + 1)
        ]
        rotated = jnp.dot(
            turn,
            jnp.concatenate(pair, axis=-1),
            precision=TOP_PRECISION,
            preferred_element_type=jnp.float32,
        )
        for k in range(2):
            value = rotated[:, k * particles : (k + 1) * particles]
            value = (value - energy[c + k : c + k + 1, :]) * (1.0 / ANGLES) + prior
            scores[c + k] = value
            best = jnp.maximum(best, value)
            own = own + jnp.where(member_ref[c + k : c + k + 1, :] > 0, value, 0.0)
    top = jnp.max(best, axis=0, keepdims=True)
    total = jnp.zeros((ANGLES, particles), jnp.float32)
    for c in range(CLS_GRP):
        total = total + jnp.exp(scores[c] - top)
    evidence_ref[...] = jnp.zeros_like(evidence_ref)
    evidence_ref[0:1, :] = top
    evidence_ref[1:2, :] = jnp.sum(total, axis=0, keepdims=True)
    weight = jnp.exp(own - jnp.max(own, axis=0, keepdims=True))
    weight = weight / jnp.sum(weight, axis=0, keepdims=True)
    turned_back = jnp.dot(
        back_ref[...], weight, precision=TOP_PRECISION, preferred_element_type=jnp.float32
    )
    h_real = turned_back[:particles].T
    h_imag = turned_back[particles:].T
    member = member_ref[...]
    chosen = member.astype(jnp.bfloat16)
    for m in range(ANGLES):
        x_real = spectra_ref[m, :, :CYCLES].astype(jnp.float32)
        x_imag = spectra_ref[m, :, CYCLES:].astype(jnp.float32)
        hr, hi = h_real[:, m : m + 1], h_imag[:, m : m + 1]
        aligned = jnp.concatenate(
            [x_real * hr - x_imag * hi, x_real * hi + x_imag * hr], axis=-1
        ).astype(jnp.bfloat16)
        sums = jnp.dot(chosen, aligned, preferred_element_type=jnp.float32)
        real_sum, imag_sum = sums[:, :CYCLES], sums[:, CYCLES:]
        keep_ref[m] = jnp.where(first, real_sum, imag_sum)
        send_ref[m] = jnp.where(first, imag_sum, real_sum)
    denom = jnp.dot(
        member, square, precision=TOP_PRECISION, preferred_element_type=jnp.float32
    )
    keep_ref[ANGLES] = denom
    send_ref[ANGLES] = denom


def score(core, mine, other, early, late, low_table, turn, back, square, prior, member):
    particles = 2 * early.shape[1]
    sums = jax.ShapeDtypeStruct((ANGLES + 1, CLS_GRP, CYCLES), jnp.float32)
    evidence = jax.ShapeDtypeStruct((EVIDENCE_ROWS, particles), jnp.float32)
    vmem = pl.BlockSpec(memory_space=pltpu.VMEM)
    return pl.pallas_call(
        score_kernel,
        in_specs=[pl.BlockSpec(memory_space=pltpu.SMEM), vmem, vmem]
        + [pl.BlockSpec(memory_space=pltpu.HBM)] * 2
        + [vmem] * 6,
        out_specs=(vmem, vmem, vmem),
        out_shape=(sums, sums, evidence),
        scratch_shapes=[
            pltpu.VMEM((ANGLES * CLS_GRP, CYCLES), jnp.float32),
            pltpu.VMEM((ANGLES * CLS_GRP, CYCLES), jnp.float32),
            pltpu.VMEM((ANGLES * 2 * CLS_GRP, particles), jnp.float32),
            pltpu.VMEM((CLS_GRP, ANGLES, particles), jnp.float32),
            pltpu.VMEM((CLS_GRP, CYCLES), jnp.float32),
            pltpu.VMEM((ANGLES, particles, 2 * CYCLES), jnp.bfloat16),
            pltpu.SemaphoreType.DMA((CHUNKS, 2)),
        ],
        compiler_params=pltpu.CompilerParams(vmem_limit_bytes=50 * 1024 * 1024),
    )(core, mine, other, early, late, low_table, turn, back, square, prior, member)


def pack_kernel(keep_ref, got_ref, out_ref):
    denom = keep_ref[ANGLES] + got_ref[ANGLES]
    high = denom.astype(jnp.bfloat16)
    low = (denom - high.astype(jnp.float32)).astype(jnp.bfloat16)
    for z in range(out_ref.shape[0]):
        at = pl.ds(z * ROWS, ROWS)
        out_ref[z, :ROWS] = (keep_ref[at] + got_ref[at]).astype(jnp.bfloat16)
        out_ref[z, ROWS] = high if z == 0 else low


def pack(keep, got):
    vmem = pl.BlockSpec(memory_space=pltpu.VMEM)
    return pl.pallas_call(
        pack_kernel,
        in_specs=[vmem, vmem],
        out_specs=vmem,
        out_shape=jax.ShapeDtypeStruct((8, ROWS + 1, CLS_GRP, CYCLES), jnp.bfloat16),
        compiler_params=pltpu.CompilerParams(vmem_limit_bytes=4 * 1024 * 1024),
    )(keep, got)


def rotation_prior(rotation_rows):
    counting = jnp.arange(ANGLES, dtype=jnp.int32)
    distance = jnp.abs(counting[None, :] - rotation_rows[:, None])
    distance = jnp.minimum(distance, ANGLES - distance).astype(jnp.float32)
    return -0.5 * (distance / SIGMA_ROT) ** 2


def halve_kernel(blocks_ref, out_ref, sems):
    copies = [
        pltpu.make_async_copy(
            blocks_ref.at[:, :, half * CYCLES : (half + 1) * CYCLES], out_ref.at[:, half], sems.at[half]
        )
        for half in range(2)
    ]
    for copy in copies:
        copy.start()
    for copy in copies:
        copy.wait()


def halve(blocks):
    return pl.pallas_call(
        halve_kernel,
        in_specs=[pl.BlockSpec(memory_space=pl.ANY)],
        out_specs=pl.BlockSpec(memory_space=pl.ANY),
        out_shape=jax.ShapeDtypeStruct((BLOCK, 2, ANGLES, CYCLES), jnp.bfloat16),
        scratch_shapes=[pltpu.SemaphoreType.DMA((2,))],
        compiler_params=pltpu.CompilerParams(vmem_limit_bytes=1024 * 1024),
    )(blocks)


def route_kernel(core_ref, place_ref, got_ref, out_ref):
    total = got_ref[0].astype(jnp.float32)
    for z in range(1, got_ref.shape[0]):
        total = total + got_ref[z].astype(jnp.float32)
    denom = total[ROWS * CLS_GRP :]
    high = denom.astype(jnp.bfloat16).astype(jnp.float32)
    denom = jnp.where(core_ref[0] == 0, high, denom - high)
    share = jnp.concatenate([total[: ROWS * CLS_GRP], denom], axis=0).astype(jnp.bfloat16)
    rows, columns = (ROWS + 1) * OWN_MAX, (ROWS + 1) * CLS_GRP
    place = place_ref[...]
    line = lax.broadcasted_iota(jnp.int32, (rows, columns), 0)
    line = (line // OWN_MAX) * 1024 + line % OWN_MAX - place
    for owner in range(0, 64, 8):
        chosen = jnp.concatenate(
            [jnp.where(line == -OWN_MAX * (owner + k), 1.0, 0.0) for k in range(8)], axis=0
        ).astype(jnp.bfloat16)
        out_ref[owner * rows : (owner + 8) * rows, :] = jnp.dot(
            chosen, share, preferred_element_type=jnp.float32
        ).astype(jnp.bfloat16)


def route(core, place, got):
    vmem = pl.BlockSpec(memory_space=pltpu.VMEM)
    return pl.pallas_call(
        route_kernel,
        in_specs=[pl.BlockSpec(memory_space=pltpu.SMEM), vmem, vmem],
        out_specs=vmem,
        out_shape=jax.ShapeDtypeStruct((64 * (ROWS + 1) * OWN_MAX, CYCLES), jnp.bfloat16),
        compiler_params=pltpu.CompilerParams(vmem_limit_bytes=6 * 1024 * 1024),
    )(core, place, got)


def finish_kernel(table_ref, got_ref, out_ref, held):
    total = got_ref[0].astype(jnp.float32)
    for plane in range(1, got_ref.shape[0]):
        total = total + got_ref[plane].astype(jnp.float32)
    held[...] = total
    rows = (ROWS + 1) * OWN_MAX
    at = ROWS * OWN_MAX
    denom = total[at : at + OWN_MAX] + total[rows + at : rows + at + OWN_MAX]
    denom = denom + total[2 * rows + at : 2 * rows + at + OWN_MAX]
    scale = (1.0 / ANGLES) / (denom + TAU)
    for slot in range(0, OWN_MAX, 2):
        pair = [
            held[pl.ds(k, 16 * (ROWS + 1), stride=OWN_MAX), :] * scale[k : k + 1]
            for k in (slot, slot + 1)
        ]
        polar = jnp.dot(
            table_ref[...],
            jnp.concatenate(pair, axis=-1),
            precision=TOP_PRECISION,
            preferred_element_type=jnp.float32,
        ).astype(jnp.bfloat16)
        for k in range(2):
            columns = slice(k * CYCLES, (k + 1) * CYCLES)
            out_ref[slot + k, :, :CYCLES] = polar[:ANGLES, columns]
            out_ref[slot + k, :, CYCLES:] = polar[ANGLES:, columns]


def finish(table, got):
    vmem = pl.BlockSpec(memory_space=pltpu.VMEM)
    return pl.pallas_call(
        finish_kernel,
        in_specs=[vmem, vmem],
        out_specs=vmem,
        out_shape=jax.ShapeDtypeStruct((OWN_MAX, ANGLES, 2 * CYCLES), jnp.bfloat16),
        scratch_shapes=[pltpu.VMEM((16 * (ROWS + 1) * OWN_MAX, CYCLES), jnp.float32)],
        compiler_params=pltpu.CompilerParams(vmem_limit_bytes=6 * 1024 * 1024),
    )(table, got)


def finish_table(cosine_table, sine_table):
    def laid(table):
        table = table.reshape(ANGLES, 8, 1, ROWS)
        return jnp.pad(table, ((0, 0), (0, 0), (0, 0), (0, 1)))

    cosine, sine = laid(cosine_table), laid(sine_table)
    real = jnp.concatenate([cosine, -sine], axis=2).reshape(ANGLES, 16 * (ROWS + 1))
    imag = jnp.concatenate([sine, cosine], axis=2).reshape(ANGLES, 16 * (ROWS + 1))
    return jnp.concatenate([real, imag])


def fetch(blocks, holders, images, contrast_rows, table):
    half = contrast_rows.shape[0] // 2
    halves = halve(blocks).reshape(BLOCK * 2, ANGLES, CYCLES)
    sliced = lax.all_to_all(halves, ("wide_1", "wide_2"), 0, 0, tiled=True)
    early = image_spectra(images, 0, contrast_rows[:half], table)
    sliced, early, later = lax.optimization_barrier((sliced, early, contrast_rows[half:]))
    picked = pick(sliced[:, None], holders % 16, 4)
    planes = lax.all_to_all(picked, "wide_0", 0, 0, tiled=True)
    late = image_spectra(images, 1, later, table)
    planes, late = lax.optimization_barrier((planes, late))
    picked = pick(planes, holders // 16, 8)
    mine = lax.all_to_all(picked, "wide_1", 0, 0, tiled=True).reshape(CLS_GRP, ANGLES, CYCLES)
    return mine, early, late


def joined_evidence(blocks):
    top = jnp.max(blocks[:, 0], axis=0)
    return top + jnp.log(jnp.sum(blocks[:, 1] * jnp.exp(blocks[:, 0] - top), axis=0))


def per_device(images, defocus, class_index, rotation_index, owner_map, roster, ref_store):
    class_group = lax.axis_index("narrow")
    core = lax.axis_index("wide_2")
    cosine_table, sine_table = angle_tables(ANGLES)
    cosines_low = cosine_table.astype(jnp.bfloat16)
    sines_low = sine_table.astype(jnp.bfloat16)
    leading_class = class_group * CLS_GRP
    arrival = jnp.arange(CLS_GRP, dtype=jnp.int32)
    within = arrival % STEPS * BLOCK + arrival // STEPS
    class_ids = leading_class + within
    holders = lax.dynamic_index_in_dim(roster, class_group, 0, keepdims=False)

    low_table = jnp.concatenate([cosines_low, sines_low])
    turn = jnp.concatenate([cosine_table, -sine_table], axis=-1)
    filled = ((0, CYCLES - ANGLES), (0, 0))
    back = jnp.concatenate([jnp.pad(cosine_table, filled), jnp.pad(sine_table, filled)])
    contrast_rows = contrast(defocus)
    square = contrast_rows * contrast_rows
    prior = rotation_prior(rotation_index).T
    member = (class_index[None, :] == class_ids[:, None]).astype(jnp.float32)
    mine, early, late = fetch(ref_store[0, 0], holders, images, contrast_rows, low_table)
    other = swapped(mine)
    keep, send, evidence = score(
        core.reshape(1), mine, other, early, late, low_table, turn, back, square, prior, member
    )
    owners = lax.dynamic_slice_in_dim(owner_map, leading_class, CLS_GRP)
    owners = owners.reshape(STEPS, BLOCK).T.reshape(CLS_GRP)
    same = owners[:, None] == owners[None, :]
    ranking = jnp.sum(same & (within[None, :] < within[:, None]), axis=1)
    place = owners * OWN_MAX + ranking
    place = jnp.arange(ROWS + 1, dtype=jnp.int32)[:, None] * 1024 + place[None, :]
    place = place.reshape(1, (ROWS + 1) * CLS_GRP)
    table = finish_table(cosine_table, sine_table)
    share = pack(keep, swapped(send)).reshape(8, (ROWS + 1) * CLS_GRP, CYCLES)
    share = lax.all_to_all(share, "wide_1", 0, 0, tiled=True)
    evidence = lax.all_gather(evidence, "narrow")
    sent = route(core.reshape(1), place, share).reshape(64, (ROWS + 1) * OWN_MAX, CYCLES)
    got = lax.all_to_all(sent, WIDE, 0, 0, tiled=True)
    log_evidence = joined_evidence(evidence[:, :2])
    got = got.reshape(4, 16 * (ROWS + 1) * OWN_MAX, CYCLES)
    new_references = finish(table, got).reshape(1, 1, OWN_MAX, ANGLES, 2 * CYCLES)
    return (new_references, log_evidence)


def solution(mesh):
    split = Mesh(
        mesh.devices.reshape(4, 8, 2, mesh.shape["narrow"]),
        ("wide_0", "wide_1", "wide_2", "narrow"),
    )
    placed = (
        P(WIDE, None, None),
        P(WIDE),
        P(WIDE),
        P(WIDE),
        P(),
        P(),
        P(WIDE, "narrow", None, None, None),
    )
    return jax.shard_map(
        per_device,
        mesh=split,
        in_specs=placed,
        out_specs=(P(WIDE, "narrow", None, None, None), P(WIDE)),
        check_vma=False,
    )
```

```python
import math

import jax
import jax.numpy as jnp
from jax import lax
from jax.experimental import pallas as pl
from jax.experimental.pallas import tpu as pltpu
from jax.sharding import Mesh
from jax.sharding import PartitionSpec as P

CYCLES = 128
ANGLES = 72
STEPS = 3
BLOCK = 8
OWN_MAX = 4
CLS_GRP = 24
SIGMA_ROT = 8
ROWS = 9
CHUNKS = 4
WIDE = ("wide_0", "wide_1", "wide_2")


TAU = 1.0
CONTRAST = 0.1
TOP_PRECISION = lax.Precision.HIGHEST


def swapped(x):
    return lax.ppermute(x, "wide_2", [(0, 1), (1, 0)])


def angle_tables(length):
    counting = jnp.arange(length, dtype=jnp.int32)
    products = counting[:, None] * counting[None, :] % length
    phase_angle = products.astype(jnp.float32) * (2.0 * math.pi / length)
    return (jnp.cos(phase_angle), jnp.sin(phase_angle))


def contrast(defocus_rows):
    cycle_freq = (jnp.arange(CYCLES, dtype=jnp.float32) + 1.0) / CYCLES
    phase_angle = 8.0 * math.pi * defocus_rows[:, None] * cycle_freq[None, :] ** 2
    return -jnp.sin(phase_angle) - CONTRAST * jnp.cos(phase_angle)


def spectrum_of(polar, table):
    both = jnp.dot(table, polar, preferred_element_type=jnp.float32)
    cos_part, sin_part = both[:ANGLES], both[ANGLES:]
    real_part = cos_part[:, :CYCLES] + sin_part[:, CYCLES:]
    imag_part = cos_part[:, CYCLES:] - sin_part[:, :CYCLES]
    return real_part, imag_part


def spectra_kernel(table_ref, contrast_ref, image_ref, out_ref, held_real, held_imag):
    table = table_ref[...]
    count = image_ref.shape[0]
    for row in range(count):
        factor = contrast_ref[row : row + 1, :]
        factor = jnp.concatenate([factor, factor], axis=-1)
        weighted = (image_ref[row].astype(jnp.float32) * factor).astype(jnp.bfloat16)
        rows = pl.ds(row, ANGLES, stride=count)
        held_real[rows, :], held_imag[rows, :] = spectrum_of(weighted, table)
    shape = (ANGLES, count, CYCLES)
    out_ref[:, :, :CYCLES] = held_real[...].reshape(shape).astype(jnp.bfloat16)
    out_ref[:, :, CYCLES:] = held_imag[...].reshape(shape).astype(jnp.bfloat16)


def image_spectra(images, half, contrast_rows, table):
    particles = contrast_rows.shape[0]
    count = 16
    skipped = half * particles // count
    return pl.pallas_call(
        spectra_kernel,
        grid=(particles // count,),
        in_specs=[
            pl.BlockSpec((2 * ANGLES, ANGLES), lambda i: (0, 0)),
            pl.BlockSpec((count, CYCLES), lambda i: (i, 0)),
            pl.BlockSpec((count, ANGLES, 2 * CYCLES), lambda i: (i + skipped, 0, 0)),
        ],
        out_specs=pl.BlockSpec((ANGLES, count, 2 * CYCLES), lambda i: (0, i, 0)),
        out_shape=jax.ShapeDtypeStruct((ANGLES, particles, 2 * CYCLES), jnp.bfloat16),
        scratch_shapes=[pltpu.VMEM((ANGLES * count, CYCLES), jnp.float32)] * 2,
        compiler_params=pltpu.CompilerParams(vmem_limit_bytes=56 * 1024 * 1024),
        cost_estimate=pl.CostEstimate(
            flops=particles * 4 * ANGLES * ANGLES * 2 * CYCLES,
            bytes_accessed=4 * particles * ANGLES * 2 * CYCLES,
            transcendentals=0,
        ),
    )(table, contrast_rows, images)


def pick_kernel(index_ref, source_ref, out_ref):
    for step in range(STEPS):
        at = index_ref[step]
        value = source_ref[at, step if source_ref.shape[1] == STEPS else 0]
        for copy in range(out_ref.shape[0]):
            out_ref[copy, step] = value


def pick(source, index, copies):
    return pl.pallas_call(
        pick_kernel,
        in_specs=[
            pl.BlockSpec(memory_space=pltpu.SMEM),
            pl.BlockSpec(memory_space=pltpu.VMEM),
        ],
        out_specs=pl.BlockSpec(memory_space=pltpu.VMEM),
        out_shape=jax.ShapeDtypeStruct((copies, STEPS, ANGLES, CYCLES), jnp.bfloat16),
        compiler_params=pltpu.CompilerParams(vmem_limit_bytes=2 * 1024 * 1024),
    )(index, source)


def score_kernel(
    core_ref,
    mine_ref,
    other_ref,
    early_ref,
    late_ref,
    low_ref,
    turn_ref,
    back_ref,
    square_ref,
    prior_ref,
    member_ref,
    keep_ref,
    send_ref,
    evidence_ref,
    ref_real,
    ref_imag,
    corr,
    scores,
    power,
    spectra_ref,
    sem,
):
    particles = spectra_ref.shape[1]
    depth, half = ANGLES // CHUNKS, particles // 2
    arriving = [
        pltpu.make_async_copy(
            source.at[pl.ds(n * depth, depth)],
            spectra_ref.at[pl.ds(n * depth, depth), pl.ds(k * half, half)],
            sem.at[n, k],
        )
        for n in range(CHUNKS)
        for k, source in enumerate((early_ref, late_ref))
    ]
    for copy in arriving:
        copy.start()
    first = core_ref[0] == 0
    table = low_ref[...]
    for c in range(CLS_GRP):
        mine, other = mine_ref[c], other_ref[c]
        polar = jnp.concatenate(
            [jnp.where(first, mine, other), jnp.where(first, other, mine)], axis=-1
        )
        real, imag = (
            part.astype(jnp.bfloat16).astype(jnp.float32) for part in spectrum_of(polar, table)
        )
        rows = pl.ds(c, ANGLES, stride=CLS_GRP)
        ref_real[rows, :], ref_imag[rows, :] = real, imag
        power[c : c + 1, :] = jnp.sum(real * real + imag * imag, axis=0, keepdims=True)
    square = square_ref[...]
    across = (((1,), (1,)), ((), ()))
    energy = 0.5 * lax.dot_general(
        power[...], square, across, precision=TOP_PRECISION, preferred_element_type=jnp.float32
    )
    for m in range(ANGLES):
        if m % depth == 0:
            for copy in arriving[m // depth * 2 : m // depth * 2 + 2]:
                copy.wait()
        rows = slice(m * CLS_GRP, (m + 1) * CLS_GRP)
        real, imag = ref_real[rows, :], ref_imag[rows, :]
        both = jnp.concatenate(
            [jnp.concatenate([real, -imag], axis=0), jnp.concatenate([imag, real], axis=0)],
            axis=-1,
        ).astype(jnp.bfloat16)
        corr[m * 2 * CLS_GRP : (m + 1) * 2 * CLS_GRP, :] = lax.dot_general(
            both, spectra_ref[m], across, preferred_element_type=jnp.float32
        )
    turn, prior = turn_ref[...], prior_ref[...]
    best = jnp.full((ANGLES, particles), -jnp.inf, jnp.float32)
    own = jnp.zeros((ANGLES, particles), jnp.float32)
    for c in range(0, CLS_GRP, 2):
        pair = [
            jnp.concatenate(
                [
                    corr[pl.ds(k, ANGLES, stride=2 * CLS_GRP), :],
                    corr[pl.ds(CLS_GRP + k, ANGLES, stride=2 * CLS_GRP), :],
                ],
                axis=0,
            )
            for k in (c, c + 1)
        ]
        rotated = jnp.dot(
            turn,
            jnp.concatenate(pair, axis=-1),
            precision=TOP_PRECISION,
            preferred_element_type=jnp.float32,
        )
        for k in range(2):
            value = rotated[:, k * particles : (k + 1) * particles]
            value = (value - energy[c + k : c + k + 1, :]) * (1.0 / ANGLES) + prior
            scores[c + k] = value
            best = jnp.maximum(best, value)
            own = own + jnp.where(member_ref[c + k : c + k + 1, :] > 0, value, 0.0)
    top = jnp.max(best, axis=0, keepdims=True)
    total = jnp.zeros((ANGLES, particles), jnp.float32)
    for c in range(CLS_GRP):
        total = total + jnp.exp(scores[c] - top)
    evidence_ref[0:1, :] = top
    evidence_ref[1:2, :] = jnp.sum(total, axis=0, keepdims=True)
    weight = jnp.exp(own - jnp.max(own, axis=0, keepdims=True))
    weight = weight / jnp.sum(weight, axis=0, keepdims=True)
    turned_back = jnp.dot(
        back_ref[...], weight, precision=TOP_PRECISION, preferred_element_type=jnp.float32
    )
    h_real = turned_back[:particles].T
    h_imag = turned_back[particles:].T
    member = member_ref[...]
    chosen = member.astype(jnp.bfloat16)
    for m in range(ANGLES):
        x_real = spectra_ref[m, :, :CYCLES].astype(jnp.float32)
        x_imag = spectra_ref[m, :, CYCLES:].astype(jnp.float32)
        hr, hi = h_real[:, m : m + 1], h_imag[:, m : m + 1]
        aligned = jnp.concatenate(
            [x_real * hr - x_imag * hi, x_real * hi + x_imag * hr], axis=-1
        ).astype(jnp.bfloat16)
        sums = jnp.dot(chosen, aligned, preferred_element_type=jnp.float32)
        real_sum, imag_sum = sums[:, :CYCLES], sums[:, CYCLES:]
        keep_ref[m] = jnp.where(first, real_sum, imag_sum)
        send_ref[m] = jnp.where(first, imag_sum, real_sum)
    denom = jnp.dot(
        member, square, precision=TOP_PRECISION, preferred_element_type=jnp.float32
    )
    keep_ref[ANGLES] = denom
    send_ref[ANGLES] = denom


def score(core, mine, other, early, late, low_table, turn, back, square, prior, member):
    particles = 2 * early.shape[1]
    sums = jax.ShapeDtypeStruct((ANGLES + 1, CLS_GRP, CYCLES), jnp.float32)
    evidence = jax.ShapeDtypeStruct((2, particles), jnp.float32)
    vmem = pl.BlockSpec(memory_space=pltpu.VMEM)
    return pl.pallas_call(
        score_kernel,
        in_specs=[pl.BlockSpec(memory_space=pltpu.SMEM), vmem, vmem]
        + [pl.BlockSpec(memory_space=pltpu.HBM)] * 2
        + [vmem] * 6,
        out_specs=(vmem, vmem, vmem),
        out_shape=(sums, sums, evidence),
        scratch_shapes=[
            pltpu.VMEM((ANGLES * CLS_GRP, CYCLES), jnp.float32),
            pltpu.VMEM((ANGLES * CLS_GRP, CYCLES), jnp.float32),
            pltpu.VMEM((ANGLES * 2 * CLS_GRP, particles), jnp.float32),
            pltpu.VMEM((CLS_GRP, ANGLES, particles), jnp.float32),
            pltpu.VMEM((CLS_GRP, CYCLES), jnp.float32),
            pltpu.VMEM((ANGLES, particles, 2 * CYCLES), jnp.bfloat16),
            pltpu.SemaphoreType.DMA((CHUNKS, 2)),
        ],
        compiler_params=pltpu.CompilerParams(vmem_limit_bytes=50 * 1024 * 1024),
    )(core, mine, other, early, late, low_table, turn, back, square, prior, member)


def pack_kernel(keep_ref, got_ref, out_ref):
    denom = keep_ref[ANGLES] + got_ref[ANGLES]
    high = denom.astype(jnp.bfloat16)
    low = (denom - high.astype(jnp.float32)).astype(jnp.bfloat16)
    for z in range(out_ref.shape[0]):
        at = pl.ds(z * ROWS, ROWS)
        out_ref[z, :ROWS] = (keep_ref[at] + got_ref[at]).astype(jnp.bfloat16)
        out_ref[z, ROWS] = high if z == 0 else low


def pack(keep, got):
    vmem = pl.BlockSpec(memory_space=pltpu.VMEM)
    return pl.pallas_call(
        pack_kernel,
        in_specs=[vmem, vmem],
        out_specs=vmem,
        out_shape=jax.ShapeDtypeStruct((8, ROWS + 1, CLS_GRP, CYCLES), jnp.bfloat16),
        compiler_params=pltpu.CompilerParams(vmem_limit_bytes=4 * 1024 * 1024),
    )(keep, got)


def rotation_prior(rotation_rows):
    counting = jnp.arange(ANGLES, dtype=jnp.int32)
    distance = jnp.abs(counting[None, :] - rotation_rows[:, None])
    distance = jnp.minimum(distance, ANGLES - distance).astype(jnp.float32)
    return -0.5 * (distance / SIGMA_ROT) ** 2


def halve_kernel(blocks_ref, out_ref, sems):
    copies = [
        pltpu.make_async_copy(
            blocks_ref.at[:, :, half * CYCLES : (half + 1) * CYCLES], out_ref.at[:, half], sems.at[half]
        )
        for half in range(2)
    ]
    for copy in copies:
        copy.start()
    for copy in copies:
        copy.wait()


def halve(blocks):
    return pl.pallas_call(
        halve_kernel,
        in_specs=[pl.BlockSpec(memory_space=pl.ANY)],
        out_specs=pl.BlockSpec(memory_space=pl.ANY),
        out_shape=jax.ShapeDtypeStruct((BLOCK, 2, ANGLES, CYCLES), jnp.bfloat16),
        scratch_shapes=[pltpu.SemaphoreType.DMA((2,))],
        compiler_params=pltpu.CompilerParams(vmem_limit_bytes=1024 * 1024),
    )(blocks)


def route_kernel(core_ref, place_ref, got_ref, out_ref):
    total = got_ref[0].astype(jnp.float32)
    for z in range(1, got_ref.shape[0]):
        total = total + got_ref[z].astype(jnp.float32)
    denom = total[ROWS * CLS_GRP :]
    high = denom.astype(jnp.bfloat16).astype(jnp.float32)
    denom = jnp.where(core_ref[0] == 0, high, denom - high)
    share = jnp.concatenate([total[: ROWS * CLS_GRP], denom], axis=0).astype(jnp.bfloat16)
    rows, columns = (ROWS + 1) * OWN_MAX, (ROWS + 1) * CLS_GRP
    place = place_ref[...]
    line = lax.broadcasted_iota(jnp.int32, (rows, columns), 0)
    line = (line // OWN_MAX) * 1024 + line % OWN_MAX - place
    for owner in range(0, 64, 8):
        chosen = jnp.concatenate(
            [jnp.where(line == -OWN_MAX * (owner + k), 1.0, 0.0) for k in range(8)], axis=0
        ).astype(jnp.bfloat16)
        out_ref[owner * rows : (owner + 8) * rows, :] = jnp.dot(
            chosen, share, preferred_element_type=jnp.float32
        ).astype(jnp.bfloat16)


def route(core, place, got):
    vmem = pl.BlockSpec(memory_space=pltpu.VMEM)
    return pl.pallas_call(
        route_kernel,
        in_specs=[pl.BlockSpec(memory_space=pltpu.SMEM), vmem, vmem],
        out_specs=vmem,
        out_shape=jax.ShapeDtypeStruct((64 * (ROWS + 1) * OWN_MAX, CYCLES), jnp.bfloat16),
        compiler_params=pltpu.CompilerParams(vmem_limit_bytes=6 * 1024 * 1024),
    )(core, place, got)


def finish_kernel(table_ref, got_ref, out_ref, held):
    total = got_ref[0].astype(jnp.float32)
    for plane in range(1, got_ref.shape[0]):
        total = total + got_ref[plane].astype(jnp.float32)
    held[...] = total
    rows = (ROWS + 1) * OWN_MAX
    at = ROWS * OWN_MAX
    denom = total[at : at + OWN_MAX] + total[rows + at : rows + at + OWN_MAX]
    denom = denom + total[2 * rows + at : 2 * rows + at + OWN_MAX]
    scale = (1.0 / ANGLES) / (denom + TAU)
    for slot in range(0, OWN_MAX, 2):
        pair = [
            held[pl.ds(k, 16 * (ROWS + 1), stride=OWN_MAX), :] * scale[k : k + 1]
            for k in (slot, slot + 1)
        ]
        polar = jnp.dot(
            table_ref[...],
            jnp.concatenate(pair, axis=-1),
            precision=TOP_PRECISION,
            preferred_element_type=jnp.float32,
        ).astype(jnp.bfloat16)
        for k in range(2):
            columns = slice(k * CYCLES, (k + 1) * CYCLES)
            out_ref[slot + k, :, :CYCLES] = polar[:ANGLES, columns]
            out_ref[slot + k, :, CYCLES:] = polar[ANGLES:, columns]


def finish(table, got):
    vmem = pl.BlockSpec(memory_space=pltpu.VMEM)
    return pl.pallas_call(
        finish_kernel,
        in_specs=[vmem, vmem],
        out_specs=vmem,
        out_shape=jax.ShapeDtypeStruct((OWN_MAX, ANGLES, 2 * CYCLES), jnp.bfloat16),
        scratch_shapes=[pltpu.VMEM((16 * (ROWS + 1) * OWN_MAX, CYCLES), jnp.float32)],
        compiler_params=pltpu.CompilerParams(vmem_limit_bytes=6 * 1024 * 1024),
    )(table, got)


def finish_table(cosine_table, sine_table):
    def laid(table):
        table = table.reshape(ANGLES, 8, 1, ROWS)
        return jnp.pad(table, ((0, 0), (0, 0), (0, 0), (0, 1)))

    cosine, sine = laid(cosine_table), laid(sine_table)
    real = jnp.concatenate([cosine, -sine], axis=2).reshape(ANGLES, 16 * (ROWS + 1))
    imag = jnp.concatenate([sine, cosine], axis=2).reshape(ANGLES, 16 * (ROWS + 1))
    return jnp.concatenate([real, imag])


def fetch(blocks, holders, images, contrast_rows, table, small):
    half = contrast_rows.shape[0] // 2
    halves = halve(blocks).reshape(BLOCK * 2, ANGLES, CYCLES)
    sliced = lax.all_to_all(halves, ("wide_1", "wide_2"), 0, 0, tiled=True)
    early = image_spectra(images, 0, contrast_rows[:half], table)
    sliced, early, later = lax.optimization_barrier((sliced, early, contrast_rows[half:]))
    picked = pick(sliced[:, None], holders % 16, 4)
    planes = lax.all_to_all(picked, "wide_0", 0, 0, tiled=True)
    late = image_spectra(images, 1, later, table)
    planes, late, small = lax.optimization_barrier((planes, late, small))
    picked = pick(planes, holders // 16, 8)
    mine = lax.all_to_all(picked, "wide_1", 0, 0, tiled=True).reshape(CLS_GRP, ANGLES, CYCLES)
    return mine, early, late, small


def exchanged_evidence(pair, bit):
    got = lax.ppermute(pair, "narrow", [(k, k ^ bit) for k in range(8)])
    top = jnp.maximum(pair[:1], got[:1])
    total = pair[1:] * jnp.exp(pair[:1] - top) + got[1:] * jnp.exp(got[:1] - top)
    return jnp.concatenate([top, total])


def per_device(images, defocus, class_index, rotation_index, owner_map, roster, ref_store):
    class_group = lax.axis_index("narrow")
    core = lax.axis_index("wide_2")
    cosine_table, sine_table = angle_tables(ANGLES)
    cosines_low = cosine_table.astype(jnp.bfloat16)
    sines_low = sine_table.astype(jnp.bfloat16)
    leading_class = class_group * CLS_GRP
    arrival = jnp.arange(CLS_GRP, dtype=jnp.int32)
    within = arrival % STEPS * BLOCK + arrival // STEPS
    class_ids = leading_class + within
    holders = lax.dynamic_index_in_dim(roster, class_group, 0, keepdims=False)

    low_table = jnp.concatenate([cosines_low, sines_low])
    turn = jnp.concatenate([cosine_table, -sine_table], axis=-1)
    filled = ((0, CYCLES - ANGLES), (0, 0))
    back = jnp.concatenate([jnp.pad(cosine_table, filled), jnp.pad(sine_table, filled)])
    contrast_rows = contrast(defocus)
    square = contrast_rows * contrast_rows
    prior = rotation_prior(rotation_index).T
    member = (class_index[None, :] == class_ids[:, None]).astype(jnp.float32)
    owners = lax.dynamic_slice_in_dim(owner_map, leading_class, CLS_GRP)
    owners = owners.reshape(STEPS, BLOCK).T.reshape(CLS_GRP)
    same = owners[:, None] == owners[None, :]
    ranking = jnp.sum(same & (within[None, :] < within[:, None]), axis=1)
    place = owners * OWN_MAX + ranking
    place = jnp.arange(ROWS + 1, dtype=jnp.int32)[:, None] * 1024 + place[None, :]
    place = place.reshape(1, (ROWS + 1) * CLS_GRP)
    table = finish_table(cosine_table, sine_table)
    small = (turn, back, square, prior, member, place, table)

    mine, early, late, small = fetch(
        ref_store[0, 0], holders, images, contrast_rows, low_table, small
    )
    turn, back, square, prior, member, place, table = small
    other = swapped(mine)
    keep, send, evidence = score(
        core.reshape(1), mine, other, early, late, low_table, turn, back, square, prior, member
    )
    got, evidence = lax.optimization_barrier((swapped(send), exchanged_evidence(evidence, 1)))
    share = pack(keep, got).reshape(8, (ROWS + 1) * CLS_GRP, CYCLES)
    share = lax.all_to_all(share, "wide_1", 0, 0, tiled=True)
    sent = route(core.reshape(1), place, share).reshape(64, (ROWS + 1) * OWN_MAX, CYCLES)
    sent, evidence = lax.optimization_barrier((sent, evidence))
    got = lax.all_to_all(sent, WIDE, 0, 0, tiled=True)
    evidence = exchanged_evidence(exchanged_evidence(evidence, 2), 4)
    log_evidence = evidence[0] + jnp.log(evidence[1])
    got = got.reshape(4, 16 * (ROWS + 1) * OWN_MAX, CYCLES)
    new_references = finish(table, got).reshape(1, 1, OWN_MAX, ANGLES, 2 * CYCLES)
    return (new_references, log_evidence)


def solution(mesh):
    split = Mesh(
        mesh.devices.reshape(4, 8, 2, mesh.shape["narrow"]),
        ("wide_0", "wide_1", "wide_2", "narrow"),
    )
    placed = (
        P(WIDE, None, None),
        P(WIDE),
        P(WIDE),
        P(WIDE),
        P(),
        P(),
        P(WIDE, "narrow", None, None, None),
    )
    return jax.shard_map(
        per_device,
        mesh=split,
        in_specs=placed,
        out_specs=(P(WIDE, "narrow", None, None, None), P(WIDE)),
        check_vma=False,
    )
```

```python
import math

import jax
import jax.numpy as jnp
import numpy as np
from jax import lax
from jax.experimental import pallas as pl
from jax.experimental.pallas import tpu as pltpu
from jax.sharding import Mesh
from jax.sharding import PartitionSpec as P

CYCLES = 128
ANGLES = 72
STEPS = 3
BLOCK = 8
OWN_MAX = 4
CLS_GRP = 24
SIGMA_ROT = 8
ROWS = 9
CHUNKS = 4
WIDE = ("wide_0", "wide_1", "wide_2")


TAU = 1.0
CONTRAST = 0.1
TOP_PRECISION = lax.Precision.HIGHEST


def swapped(x):
    return lax.ppermute(x, "wide_2", [(0, 1), (1, 0)])


def angle_tables(length):
    counting = np.arange(length)
    products = counting[:, None] * counting[None, :] % length
    phase_angle = products.astype(np.float64) * (2.0 * math.pi / length)
    return (np.cos(phase_angle).astype(np.float32), np.sin(phase_angle).astype(np.float32))


def contrast(defocus_rows):
    cycle_freq = (jnp.arange(CYCLES, dtype=jnp.float32) + 1.0) / CYCLES
    phase_angle = 8.0 * math.pi * defocus_rows[:, None] * cycle_freq[None, :] ** 2
    return -jnp.sin(phase_angle) - CONTRAST * jnp.cos(phase_angle)


def spectrum_of(polar, table):
    both = jnp.dot(table, polar, preferred_element_type=jnp.float32)
    cos_part, sin_part = both[:ANGLES], both[ANGLES:]
    real_part = cos_part[:, :CYCLES] + sin_part[:, CYCLES:]
    imag_part = cos_part[:, CYCLES:] - sin_part[:, :CYCLES]
    return real_part, imag_part


def spectra_kernel(table_ref, contrast_ref, image_ref, out_ref, held_real, held_imag):
    table = table_ref[...]
    count = image_ref.shape[0]
    for row in range(count):
        factor = contrast_ref[row : row + 1, :]
        factor = jnp.concatenate([factor, factor], axis=-1)
        weighted = (image_ref[row].astype(jnp.float32) * factor).astype(jnp.bfloat16)
        rows = pl.ds(row, ANGLES, stride=count)
        held_real[rows, :], held_imag[rows, :] = spectrum_of(weighted, table)
    shape = (ANGLES, count, CYCLES)
    out_ref[:, :, :CYCLES] = held_real[...].reshape(shape).astype(jnp.bfloat16)
    out_ref[:, :, CYCLES:] = held_imag[...].reshape(shape).astype(jnp.bfloat16)


def image_spectra(images, half, contrast_rows, table):
    particles = contrast_rows.shape[0]
    count = 16
    skipped = half * particles // count
    return pl.pallas_call(
        spectra_kernel,
        grid=(particles // count,),
        in_specs=[
            pl.BlockSpec((2 * ANGLES, ANGLES), lambda i: (0, 0)),
            pl.BlockSpec((count, CYCLES), lambda i: (i, 0)),
            pl.BlockSpec((count, ANGLES, 2 * CYCLES), lambda i: (i + skipped, 0, 0)),
        ],
        out_specs=pl.BlockSpec((ANGLES, count, 2 * CYCLES), lambda i: (0, i, 0)),
        out_shape=jax.ShapeDtypeStruct((ANGLES, particles, 2 * CYCLES), jnp.bfloat16),
        scratch_shapes=[pltpu.VMEM((ANGLES * count, CYCLES), jnp.float32)] * 2,
        compiler_params=pltpu.CompilerParams(vmem_limit_bytes=56 * 1024 * 1024),
        cost_estimate=pl.CostEstimate(
            flops=particles * 4 * ANGLES * ANGLES * 2 * CYCLES,
            bytes_accessed=4 * particles * ANGLES * 2 * CYCLES,
            transcendentals=0,
        ),
    )(table, contrast_rows, images)


def pick_kernel(index_ref, source_ref, out_ref):
    for step in range(STEPS):
        at = index_ref[step]
        value = source_ref[at, step if source_ref.shape[1] == STEPS else 0]
        for copy in range(out_ref.shape[0]):
            out_ref[copy, step] = value


def pick(source, index, copies):
    return pl.pallas_call(
        pick_kernel,
        in_specs=[
            pl.BlockSpec(memory_space=pltpu.SMEM),
            pl.BlockSpec(memory_space=pltpu.VMEM),
        ],
        out_specs=pl.BlockSpec(memory_space=pltpu.VMEM),
        out_shape=jax.ShapeDtypeStruct((copies, STEPS, ANGLES, CYCLES), jnp.bfloat16),
        compiler_params=pltpu.CompilerParams(vmem_limit_bytes=2 * 1024 * 1024),
    )(index, source)


def score_kernel(
    core_ref,
    mine_ref,
    other_ref,
    early_ref,
    late_ref,
    low_ref,
    turn_ref,
    back_ref,
    square_ref,
    prior_ref,
    member_ref,
    keep_ref,
    send_ref,
    evidence_ref,
    ref_real,
    ref_imag,
    corr,
    scores,
    power,
    spectra_ref,
    sem,
):
    particles = spectra_ref.shape[1]
    depth, half = ANGLES // CHUNKS, particles // 2
    arriving = [
        pltpu.make_async_copy(
            source.at[pl.ds(n * depth, depth)],
            spectra_ref.at[pl.ds(n * depth, depth), pl.ds(k * half, half)],
            sem.at[n, k],
        )
        for n in range(CHUNKS)
        for k, source in enumerate((early_ref, late_ref))
    ]
    for copy in arriving:
        copy.start()
    first = core_ref[0] == 0
    table = low_ref[...]
    for c in range(CLS_GRP):
        mine, other = mine_ref[c], other_ref[c]
        polar = jnp.concatenate(
            [jnp.where(first, mine, other), jnp.where(first, other, mine)], axis=-1
        )
        real, imag = (
            part.astype(jnp.bfloat16).astype(jnp.float32) for part in spectrum_of(polar, table)
        )
        rows = pl.ds(c, ANGLES, stride=CLS_GRP)
        ref_real[rows, :], ref_imag[rows, :] = real, imag
        power[c : c + 1, :] = jnp.sum(real * real + imag * imag, axis=0, keepdims=True)
    square = square_ref[...]
    across = (((1,), (1,)), ((), ()))
    energy = 0.5 * lax.dot_general(
        power[...], square, across, precision=TOP_PRECISION, preferred_element_type=jnp.float32
    )
    for m in range(ANGLES):
        if m % depth == 0:
            for copy in arriving[m // depth * 2 : m // depth * 2 + 2]:
                copy.wait()
        rows = slice(m * CLS_GRP, (m + 1) * CLS_GRP)
        real, imag = ref_real[rows, :], ref_imag[rows, :]
        both = jnp.concatenate(
            [jnp.concatenate([real, -imag], axis=0), jnp.concatenate([imag, real], axis=0)],
            axis=-1,
        ).astype(jnp.bfloat16)
        corr[m * 2 * CLS_GRP : (m + 1) * 2 * CLS_GRP, :] = lax.dot_general(
            both, spectra_ref[m], across, preferred_element_type=jnp.float32
        )
    turn, prior = turn_ref[...], prior_ref[...]
    best = jnp.full((ANGLES, particles), -jnp.inf, jnp.float32)
    own = jnp.zeros((ANGLES, particles), jnp.float32)
    for c in range(0, CLS_GRP, 2):
        pair = [
            jnp.concatenate(
                [
                    corr[pl.ds(k, ANGLES, stride=2 * CLS_GRP), :],
                    corr[pl.ds(CLS_GRP + k, ANGLES, stride=2 * CLS_GRP), :],
                ],
                axis=0,
            )
            for k in (c, c + 1)
        ]
        rotated = jnp.dot(
            turn,
            jnp.concatenate(pair, axis=-1),
            precision=TOP_PRECISION,
            preferred_element_type=jnp.float32,
        )
        for k in range(2):
            value = rotated[:, k * particles : (k + 1) * particles]
            value = (value - energy[c + k : c + k + 1, :]) * (1.0 / ANGLES) + prior
            scores[c + k] = value
            best = jnp.maximum(best, value)
            own = own + jnp.where(member_ref[c + k : c + k + 1, :] > 0, value, 0.0)
    top = jnp.max(best, axis=0, keepdims=True)
    total = jnp.zeros((ANGLES, particles), jnp.float32)
    for c in range(CLS_GRP):
        total = total + jnp.exp(scores[c] - top)
    evidence_ref[0:1, :] = top
    evidence_ref[1:2, :] = jnp.sum(total, axis=0, keepdims=True)
    weight = jnp.exp(own - jnp.max(own, axis=0, keepdims=True))
    weight = weight / jnp.sum(weight, axis=0, keepdims=True)
    turned_back = jnp.dot(
        back_ref[...], weight, precision=TOP_PRECISION, preferred_element_type=jnp.float32
    )
    h_real = turned_back[:particles].T
    h_imag = turned_back[particles:].T
    member = member_ref[...]
    chosen = member.astype(jnp.bfloat16)
    for m in range(ANGLES):
        x_real = spectra_ref[m, :, :CYCLES].astype(jnp.float32)
        x_imag = spectra_ref[m, :, CYCLES:].astype(jnp.float32)
        hr, hi = h_real[:, m : m + 1], h_imag[:, m : m + 1]
        aligned = jnp.concatenate(
            [x_real * hr - x_imag * hi, x_real * hi + x_imag * hr], axis=-1
        ).astype(jnp.bfloat16)
        sums = jnp.dot(chosen, aligned, preferred_element_type=jnp.float32)
        real_sum, imag_sum = sums[:, :CYCLES], sums[:, CYCLES:]
        keep_ref[m] = jnp.where(first, real_sum, imag_sum)
        send_ref[m] = jnp.where(first, imag_sum, real_sum)
    denom = jnp.dot(
        member, square, precision=TOP_PRECISION, preferred_element_type=jnp.float32
    )
    keep_ref[ANGLES] = denom
    send_ref[ANGLES] = denom


def score(core, mine, other, early, late, low_table, turn, back, square, prior, member):
    particles = 2 * early.shape[1]
    sums = jax.ShapeDtypeStruct((ANGLES + 1, CLS_GRP, CYCLES), jnp.float32)
    evidence = jax.ShapeDtypeStruct((2, particles), jnp.float32)
    vmem = pl.BlockSpec(memory_space=pltpu.VMEM)
    return pl.pallas_call(
        score_kernel,
        in_specs=[pl.BlockSpec(memory_space=pltpu.SMEM), vmem, vmem]
        + [pl.BlockSpec(memory_space=pltpu.HBM)] * 2
        + [vmem] * 6,
        out_specs=(vmem, vmem, vmem),
        out_shape=(sums, sums, evidence),
        scratch_shapes=[
            pltpu.VMEM((ANGLES * CLS_GRP, CYCLES), jnp.float32),
            pltpu.VMEM((ANGLES * CLS_GRP, CYCLES), jnp.float32),
            pltpu.VMEM((ANGLES * 2 * CLS_GRP, particles), jnp.float32),
            pltpu.VMEM((CLS_GRP, ANGLES, particles), jnp.float32),
            pltpu.VMEM((CLS_GRP, CYCLES), jnp.float32),
            pltpu.VMEM((ANGLES, particles, 2 * CYCLES), jnp.bfloat16),
            pltpu.SemaphoreType.DMA((CHUNKS, 2)),
        ],
        compiler_params=pltpu.CompilerParams(vmem_limit_bytes=50 * 1024 * 1024),
    )(core, mine, other, early, late, low_table, turn, back, square, prior, member)


def pack_kernel(keep_ref, got_ref, out_ref):
    denom = keep_ref[ANGLES] + got_ref[ANGLES]
    high = denom.astype(jnp.bfloat16)
    low = (denom - high.astype(jnp.float32)).astype(jnp.bfloat16)
    for z in range(out_ref.shape[0]):
        at = pl.ds(z * ROWS, ROWS)
        out_ref[z, :ROWS] = (keep_ref[at] + got_ref[at]).astype(jnp.bfloat16)
        out_ref[z, ROWS] = high if z == 0 else low


def pack(keep, got):
    vmem = pl.BlockSpec(memory_space=pltpu.VMEM)
    return pl.pallas_call(
        pack_kernel,
        in_specs=[vmem, vmem],
        out_specs=vmem,
        out_shape=jax.ShapeDtypeStruct((8, ROWS + 1, CLS_GRP, CYCLES), jnp.bfloat16),
        compiler_params=pltpu.CompilerParams(vmem_limit_bytes=4 * 1024 * 1024),
    )(keep, got)


def rotation_prior(rotation_rows):
    counting = jnp.arange(ANGLES, dtype=jnp.int32)
    distance = jnp.abs(counting[None, :] - rotation_rows[:, None])
    distance = jnp.minimum(distance, ANGLES - distance).astype(jnp.float32)
    return -0.5 * (distance / SIGMA_ROT) ** 2


def halve_kernel(blocks_ref, out_ref):
    for half in range(2):
        out_ref[:, half] = blocks_ref[:, :, half * CYCLES : (half + 1) * CYCLES]


def halve(blocks):
    count = 4
    return pl.pallas_call(
        halve_kernel,
        grid=(BLOCK // count,),
        in_specs=[pl.BlockSpec((count, ANGLES, 2 * CYCLES), lambda i: (i, 0, 0))],
        out_specs=pl.BlockSpec((count, 2, ANGLES, CYCLES), lambda i: (i, 0, 0, 0)),
        out_shape=jax.ShapeDtypeStruct((BLOCK, 2, ANGLES, CYCLES), jnp.bfloat16),
        compiler_params=pltpu.CompilerParams(vmem_limit_bytes=60 * 1024 * 1024),
    )(blocks)


def route_kernel(core_ref, place_ref, got_ref, out_ref):
    total = got_ref[0].astype(jnp.float32)
    for z in range(1, got_ref.shape[0]):
        total = total + got_ref[z].astype(jnp.float32)
    denom = total[ROWS * CLS_GRP :]
    high = denom.astype(jnp.bfloat16).astype(jnp.float32)
    denom = jnp.where(core_ref[0] == 0, high, denom - high)
    share = jnp.concatenate([total[: ROWS * CLS_GRP], denom], axis=0).astype(jnp.bfloat16)
    rows, columns = (ROWS + 1) * OWN_MAX, (ROWS + 1) * CLS_GRP
    place = place_ref[...]
    line = lax.broadcasted_iota(jnp.int32, (rows, columns), 0)
    line = (line // OWN_MAX) * 1024 + line % OWN_MAX - place
    for owner in range(0, 64, 8):
        chosen = jnp.concatenate(
            [jnp.where(line == -OWN_MAX * (owner + k), 1.0, 0.0) for k in range(8)], axis=0
        ).astype(jnp.bfloat16)
        out_ref[owner * rows : (owner + 8) * rows, :] = jnp.dot(
            chosen, share, preferred_element_type=jnp.float32
        ).astype(jnp.bfloat16)


def route(core, place, got):
    vmem = pl.BlockSpec(memory_space=pltpu.VMEM)
    return pl.pallas_call(
        route_kernel,
        in_specs=[pl.BlockSpec(memory_space=pltpu.SMEM), vmem, vmem],
        out_specs=vmem,
        out_shape=jax.ShapeDtypeStruct((64 * (ROWS + 1) * OWN_MAX, CYCLES), jnp.bfloat16),
        compiler_params=pltpu.CompilerParams(vmem_limit_bytes=6 * 1024 * 1024),
    )(core, place, got)


def finish_kernel(table_ref, got_ref, out_ref, held):
    total = got_ref[0].astype(jnp.float32)
    for plane in range(1, got_ref.shape[0]):
        total = total + got_ref[plane].astype(jnp.float32)
    held[...] = total
    rows = (ROWS + 1) * OWN_MAX
    at = ROWS * OWN_MAX
    denom = total[at : at + OWN_MAX] + total[rows + at : rows + at + OWN_MAX]
    denom = denom + total[2 * rows + at : 2 * rows + at + OWN_MAX]
    scale = (1.0 / ANGLES) / (denom + TAU)
    for slot in range(0, OWN_MAX, 2):
        pair = [
            held[pl.ds(k, 16 * (ROWS + 1), stride=OWN_MAX), :] * scale[k : k + 1]
            for k in (slot, slot + 1)
        ]
        polar = jnp.dot(
            table_ref[...],
            jnp.concatenate(pair, axis=-1),
            precision=TOP_PRECISION,
            preferred_element_type=jnp.float32,
        ).astype(jnp.bfloat16)
        for k in range(2):
            columns = slice(k * CYCLES, (k + 1) * CYCLES)
            out_ref[slot + k, :, :CYCLES] = polar[:ANGLES, columns]
            out_ref[slot + k, :, CYCLES:] = polar[ANGLES:, columns]


def finish(table, got):
    vmem = pl.BlockSpec(memory_space=pltpu.VMEM)
    return pl.pallas_call(
        finish_kernel,
        in_specs=[vmem, vmem],
        out_specs=vmem,
        out_shape=jax.ShapeDtypeStruct((OWN_MAX, ANGLES, 2 * CYCLES), jnp.bfloat16),
        scratch_shapes=[pltpu.VMEM((16 * (ROWS + 1) * OWN_MAX, CYCLES), jnp.float32)],
        compiler_params=pltpu.CompilerParams(vmem_limit_bytes=6 * 1024 * 1024),
    )(table, got)


def finish_table(cosine_table, sine_table):
    def laid(table):
        table = table.reshape(ANGLES, 8, 1, ROWS)
        return np.pad(table, ((0, 0), (0, 0), (0, 0), (0, 1)))

    cosine, sine = laid(cosine_table), laid(sine_table)
    real = np.concatenate([cosine, -sine], axis=2).reshape(ANGLES, 16 * (ROWS + 1))
    imag = np.concatenate([sine, cosine], axis=2).reshape(ANGLES, 16 * (ROWS + 1))
    return np.concatenate([real, imag])


def fetch(blocks, holders, images, contrast_rows, table, small):
    half = contrast_rows.shape[0] // 2
    halves = halve(blocks).reshape(BLOCK * 2, ANGLES, CYCLES)
    sliced = lax.all_to_all(halves, ("wide_1", "wide_2"), 0, 0, tiled=True)
    early = image_spectra(images, 0, contrast_rows[:half], table)
    sliced, early, later = lax.optimization_barrier((sliced, early, contrast_rows[half:]))
    picked = pick(sliced[:, None], holders % 16, 4)
    planes = lax.all_to_all(picked, "wide_0", 0, 0, tiled=True)
    late = image_spectra(images, 1, later, table)
    planes, late, small = lax.optimization_barrier((planes, late, small))
    picked = pick(planes, holders // 16, 8)
    mine = lax.all_to_all(picked, "wide_1", 0, 0, tiled=True).reshape(CLS_GRP, ANGLES, CYCLES)
    return mine, early, late, small


def exchanged_evidence(pair, bit):
    got = lax.ppermute(pair, "narrow", [(k, k ^ bit) for k in range(8)])
    top = jnp.maximum(pair[:1], got[:1])
    total = pair[1:] * jnp.exp(pair[:1] - top) + got[1:] * jnp.exp(got[:1] - top)
    return jnp.concatenate([top, total])


def per_device(images, defocus, class_index, rotation_index, owner_map, roster, ref_store):
    class_group = lax.axis_index("narrow")
    core = lax.axis_index("wide_2")
    cosine_table, sine_table = angle_tables(ANGLES)
    leading_class = class_group * CLS_GRP
    arrival = jnp.arange(CLS_GRP, dtype=jnp.int32)
    within = arrival % STEPS * BLOCK + arrival // STEPS
    class_ids = leading_class + within
    mine_group = jnp.arange(8, dtype=jnp.int32)[:, None] == class_group
    holders = jnp.sum(jnp.where(mine_group, roster, 0), axis=0)

    low_table = np.concatenate([cosine_table, sine_table]).astype(jnp.bfloat16)
    turn = np.concatenate([cosine_table, -sine_table], axis=-1)
    filled = ((0, CYCLES - ANGLES), (0, 0))
    back = np.concatenate([np.pad(cosine_table, filled), np.pad(sine_table, filled)])
    contrast_rows = contrast(defocus)
    square = contrast_rows * contrast_rows
    prior = rotation_prior(rotation_index).T
    member = (class_index[None, :] == class_ids[:, None]).astype(jnp.float32)
    owners = jnp.sum(jnp.where(mine_group, owner_map.reshape(8, CLS_GRP), 0), axis=0)
    owners = owners.reshape(STEPS, BLOCK).T.reshape(CLS_GRP)
    same = owners[:, None] == owners[None, :]
    ranking = jnp.sum(same & (within[None, :] < within[:, None]), axis=1)
    place = owners * OWN_MAX + ranking
    place = jnp.arange(ROWS + 1, dtype=jnp.int32)[:, None] * 1024 + place[None, :]
    place = place.reshape(1, (ROWS + 1) * CLS_GRP)
    table = finish_table(cosine_table, sine_table)
    small = (square, prior, member, place)

    mine, early, late, small = fetch(
        ref_store[0, 0], holders, images, contrast_rows, low_table, small
    )
    square, prior, member, place = small
    other = swapped(mine)
    keep, send, evidence = score(
        core.reshape(1), mine, other, early, late, low_table, turn, back, square, prior, member
    )
    share = pack(keep, swapped(send)).reshape(8, (ROWS + 1) * CLS_GRP, CYCLES)
    share = lax.all_to_all(share, "wide_1", 0, 0, tiled=True)
    sent = route(core.reshape(1), place, share).reshape(64, (ROWS + 1) * OWN_MAX, CYCLES)
    sent, evidence = lax.optimization_barrier((sent, evidence))
    got = lax.all_to_all(sent, WIDE, 0, 0, tiled=True)
    for bit in (2, 4, 1):
        evidence = exchanged_evidence(evidence, bit)
    log_evidence = evidence[0] + jnp.log(evidence[1])
    got = got.reshape(4, 16 * (ROWS + 1) * OWN_MAX, CYCLES)
    new_references = finish(table, got).reshape(1, 1, OWN_MAX, ANGLES, 2 * CYCLES)
    return (new_references, log_evidence)


def solution(mesh):
    split = Mesh(
        mesh.devices.reshape(4, 8, 2, mesh.shape["narrow"]),
        ("wide_0", "wide_1", "wide_2", "narrow"),
    )
    placed = (
        P(WIDE, None, None),
        P(WIDE),
        P(WIDE),
        P(WIDE),
        P(),
        P(),
        P(WIDE, "narrow", None, None, None),
    )
    return jax.shard_map(
        per_device,
        mesh=split,
        in_specs=placed,
        out_specs=(P(WIDE, "narrow", None, None, None), P(WIDE)),
        check_vma=False,
    )
```

```python
import math

import jax
import jax.numpy as jnp
import numpy as np
from jax import lax
from jax.experimental import pallas as pl
from jax.experimental.pallas import tpu as pltpu
from jax.sharding import Mesh
from jax.sharding import PartitionSpec as P

CYCLES = 128
ANGLES = 72
STEPS = 3
BLOCK = 8
OWN_MAX = 4
CLS_GRP = 24
SIGMA_ROT = 8
ROWS = 9
CHUNKS = 4
WIDE = ("wide_0", "wide_1", "wide_2")


TAU = 1.0
CONTRAST = 0.1
TOP_PRECISION = lax.Precision.HIGHEST


def swapped(x):
    return lax.ppermute(x, "wide_2", [(0, 1), (1, 0)])


def stepped(classes):
    length = lax.axis_size("wide_1")
    got = lax.ppermute(classes, "wide_1", [(k, (k + 1) % length) for k in range(length)])
    return got[:, :1] >> 8


def angle_tables(length):
    counting = np.arange(length)
    products = counting[:, None] * counting[None, :] % length
    phase_angle = products.astype(np.float32) * np.float32(2.0 * math.pi / length)
    return (np.cos(phase_angle), np.sin(phase_angle))


def contrast(defocus_rows):
    cycle_freq = (jnp.arange(CYCLES, dtype=jnp.float32) + 1.0) / CYCLES
    phase_angle = 8.0 * math.pi * defocus_rows[:, None] * cycle_freq[None, :] ** 2
    return -jnp.sin(phase_angle) - CONTRAST * jnp.cos(phase_angle)


def spectrum_of(polar, table):
    both = jnp.dot(table, polar, preferred_element_type=jnp.float32)
    cos_part, sin_part = both[:ANGLES], both[ANGLES:]
    real_part = cos_part[:, :CYCLES] + sin_part[:, CYCLES:]
    imag_part = cos_part[:, CYCLES:] - sin_part[:, :CYCLES]
    return real_part, imag_part


def spectra_kernel(table_ref, contrast_ref, image_ref, out_ref, held_real, held_imag):
    table = table_ref[...]
    count = image_ref.shape[0]
    for row in range(count):
        factor = contrast_ref[row : row + 1, :]
        factor = jnp.concatenate([factor, factor], axis=-1)
        weighted = (image_ref[row].astype(jnp.float32) * factor).astype(jnp.bfloat16)
        rows = pl.ds(row, ANGLES, stride=count)
        held_real[rows, :], held_imag[rows, :] = spectrum_of(weighted, table)
    shape = (ANGLES, count, CYCLES)
    out_ref[:, :, :CYCLES] = held_real[...].reshape(shape).astype(jnp.bfloat16)
    out_ref[:, :, CYCLES:] = held_imag[...].reshape(shape).astype(jnp.bfloat16)


def image_spectra(images, half, contrast_rows, table):
    particles = contrast_rows.shape[0]
    count = 16
    skipped = half * particles // count
    return pl.pallas_call(
        spectra_kernel,
        grid=(particles // count,),
        in_specs=[
            pl.BlockSpec((2 * ANGLES, ANGLES), lambda i: (0, 0)),
            pl.BlockSpec((count, CYCLES), lambda i: (i, 0)),
            pl.BlockSpec((count, ANGLES, 2 * CYCLES), lambda i: (i + skipped, 0, 0)),
        ],
        out_specs=pl.BlockSpec((ANGLES, count, 2 * CYCLES), lambda i: (0, i, 0)),
        out_shape=jax.ShapeDtypeStruct((ANGLES, particles, 2 * CYCLES), jnp.bfloat16),
        scratch_shapes=[pltpu.VMEM((ANGLES * count, CYCLES), jnp.float32)] * 2,
        compiler_params=pltpu.CompilerParams(vmem_limit_bytes=56 * 1024 * 1024),
        cost_estimate=pl.CostEstimate(
            flops=particles * 4 * ANGLES * ANGLES * 2 * CYCLES,
            bytes_accessed=4 * particles * ANGLES * 2 * CYCLES,
            transcendentals=0,
        ),
    )(table, contrast_rows, images)


def pick_kernel(index_ref, source_ref, out_ref):
    for step in range(STEPS):
        at = index_ref[step]
        value = source_ref[at, step if source_ref.shape[1] == STEPS else 0]
        for copy in range(out_ref.shape[0]):
            out_ref[copy, step] = value


def pick(source, index, copies):
    return pl.pallas_call(
        pick_kernel,
        in_specs=[
            pl.BlockSpec(memory_space=pltpu.SMEM),
            pl.BlockSpec(memory_space=pltpu.VMEM),
        ],
        out_specs=pl.BlockSpec(memory_space=pltpu.VMEM),
        out_shape=jax.ShapeDtypeStruct((copies, STEPS, ANGLES, CYCLES), jnp.bfloat16),
        compiler_params=pltpu.CompilerParams(vmem_limit_bytes=2 * 1024 * 1024),
    )(index, source)


def score_kernel(
    core_ref,
    mine_ref,
    other_ref,
    early_ref,
    late_ref,
    low_ref,
    turn_ref,
    back_ref,
    square_ref,
    prior_ref,
    member_ref,
    keep_ref,
    send_ref,
    evidence_ref,
    ref_real,
    ref_imag,
    corr,
    scores,
    power,
    spectra_ref,
    sem,
):
    particles = spectra_ref.shape[1]
    depth, half = ANGLES // CHUNKS, particles // 2
    arriving = [
        pltpu.make_async_copy(
            source.at[pl.ds(n * depth, depth)],
            spectra_ref.at[pl.ds(n * depth, depth), pl.ds(k * half, half)],
            sem.at[n, k],
        )
        for n in range(CHUNKS)
        for k, source in enumerate((early_ref, late_ref))
    ]
    for copy in arriving:
        copy.start()
    first = core_ref[0] == 0
    table = low_ref[...]
    for c in range(CLS_GRP):
        mine, other = mine_ref[c], other_ref[c]
        polar = jnp.concatenate(
            [jnp.where(first, mine, other), jnp.where(first, other, mine)], axis=-1
        )
        real, imag = (
            part.astype(jnp.bfloat16).astype(jnp.float32) for part in spectrum_of(polar, table)
        )
        rows = pl.ds(c, ANGLES, stride=CLS_GRP)
        ref_real[rows, :], ref_imag[rows, :] = real, imag
        power[c : c + 1, :] = jnp.sum(real * real + imag * imag, axis=0, keepdims=True)
    square = square_ref[...]
    across = (((1,), (1,)), ((), ()))
    energy = 0.5 * lax.dot_general(
        power[...], square, across, precision=TOP_PRECISION, preferred_element_type=jnp.float32
    )
    for m in range(ANGLES):
        if m % depth == 0:
            for copy in arriving[m // depth * 2 : m // depth * 2 + 2]:
                copy.wait()
        rows = slice(m * CLS_GRP, (m + 1) * CLS_GRP)
        real, imag = ref_real[rows, :], ref_imag[rows, :]
        both = jnp.concatenate(
            [jnp.concatenate([real, -imag], axis=0), jnp.concatenate([imag, real], axis=0)],
            axis=-1,
        ).astype(jnp.bfloat16)
        corr[m * 2 * CLS_GRP : (m + 1) * 2 * CLS_GRP, :] = lax.dot_general(
            both, spectra_ref[m], across, preferred_element_type=jnp.float32
        )
    turn, prior = turn_ref[...], prior_ref[...]
    best = jnp.full((ANGLES, particles), -jnp.inf, jnp.float32)
    own = jnp.zeros((ANGLES, particles), jnp.float32)
    for c in range(0, CLS_GRP, 2):
        pair = [
            jnp.concatenate(
                [
                    corr[pl.ds(k, ANGLES, stride=2 * CLS_GRP), :],
                    corr[pl.ds(CLS_GRP + k, ANGLES, stride=2 * CLS_GRP), :],
                ],
                axis=0,
            )
            for k in (c, c + 1)
        ]
        rotated = jnp.dot(
            turn,
            jnp.concatenate(pair, axis=-1),
            precision=TOP_PRECISION,
            preferred_element_type=jnp.float32,
        )
        for k in range(2):
            value = rotated[:, k * particles : (k + 1) * particles]
            value = (value - energy[c + k : c + k + 1, :]) * (1.0 / ANGLES) + prior
            scores[c + k] = value
            best = jnp.maximum(best, value)
            own = own + jnp.where(member_ref[c + k : c + k + 1, :] > 0, value, 0.0)
    top = jnp.max(best, axis=0, keepdims=True)
    total = jnp.zeros((ANGLES, particles), jnp.float32)
    for c in range(CLS_GRP):
        total = total + jnp.exp(scores[c] - top)
    evidence_ref[0:1, :] = top
    evidence_ref[1:2, :] = jnp.sum(total, axis=0, keepdims=True)
    weight = jnp.exp(own - jnp.max(own, axis=0, keepdims=True))
    weight = weight / jnp.sum(weight, axis=0, keepdims=True)
    turned_back = jnp.dot(
        back_ref[...], weight, precision=TOP_PRECISION, preferred_element_type=jnp.float32
    )
    h_real = turned_back[:particles].T
    h_imag = turned_back[particles:].T
    member = member_ref[...]
    chosen = member.astype(jnp.bfloat16)
    for m in range(ANGLES):
        x_real = spectra_ref[m, :, :CYCLES].astype(jnp.float32)
        x_imag = spectra_ref[m, :, CYCLES:].astype(jnp.float32)
        hr, hi = h_real[:, m : m + 1], h_imag[:, m : m + 1]
        aligned = jnp.concatenate(
            [x_real * hr - x_imag * hi, x_real * hi + x_imag * hr], axis=-1
        ).astype(jnp.bfloat16)
        sums = jnp.dot(chosen, aligned, preferred_element_type=jnp.float32)
        real_sum, imag_sum = sums[:, :CYCLES], sums[:, CYCLES:]
        keep_ref[m] = jnp.where(first, real_sum, imag_sum)
        send_ref[m] = jnp.where(first, imag_sum, real_sum)
    denom = jnp.dot(
        member, square, precision=TOP_PRECISION, preferred_element_type=jnp.float32
    )
    keep_ref[ANGLES] = denom
    send_ref[ANGLES] = denom


def score(core, mine, other, early, late, low_table, turn, back, square, prior, member):
    particles = 2 * early.shape[1]
    sums = jax.ShapeDtypeStruct((ANGLES + 1, CLS_GRP, CYCLES), jnp.float32)
    evidence = jax.ShapeDtypeStruct((2, particles), jnp.float32)
    vmem = pl.BlockSpec(memory_space=pltpu.VMEM)
    return pl.pallas_call(
        score_kernel,
        in_specs=[pl.BlockSpec(memory_space=pltpu.SMEM), vmem, vmem]
        + [pl.BlockSpec(memory_space=pltpu.HBM)] * 2
        + [vmem] * 6,
        out_specs=(vmem, vmem, vmem),
        out_shape=(sums, sums, evidence),
        scratch_shapes=[
            pltpu.VMEM((ANGLES * CLS_GRP, CYCLES), jnp.float32),
            pltpu.VMEM((ANGLES * CLS_GRP, CYCLES), jnp.float32),
            pltpu.VMEM((ANGLES * 2 * CLS_GRP, particles), jnp.float32),
            pltpu.VMEM((CLS_GRP, ANGLES, particles), jnp.float32),
            pltpu.VMEM((CLS_GRP, CYCLES), jnp.float32),
            pltpu.VMEM((ANGLES, particles, 2 * CYCLES), jnp.bfloat16),
            pltpu.SemaphoreType.DMA((CHUNKS, 2)),
        ],
        compiler_params=pltpu.CompilerParams(vmem_limit_bytes=50 * 1024 * 1024),
    )(core, mine, other, early, late, low_table, turn, back, square, prior, member)


def pack_kernel(keep_ref, got_ref, out_ref):
    denom = keep_ref[ANGLES] + got_ref[ANGLES]
    high = denom.astype(jnp.bfloat16)
    low = (denom - high.astype(jnp.float32)).astype(jnp.bfloat16)
    for z in range(out_ref.shape[0]):
        at = pl.ds(z * ROWS, ROWS)
        out_ref[z, :ROWS] = (keep_ref[at] + got_ref[at]).astype(jnp.bfloat16)
        out_ref[z, ROWS] = high if z == 0 else low


def pack(keep, got):
    vmem = pl.BlockSpec(memory_space=pltpu.VMEM)
    return pl.pallas_call(
        pack_kernel,
        in_specs=[vmem, vmem],
        out_specs=vmem,
        out_shape=jax.ShapeDtypeStruct((8, ROWS + 1, CLS_GRP, CYCLES), jnp.bfloat16),
        compiler_params=pltpu.CompilerParams(vmem_limit_bytes=4 * 1024 * 1024),
    )(keep, got)


def rotation_prior(rotation_rows):
    counting = jnp.arange(ANGLES, dtype=jnp.int32)
    distance = jnp.abs(counting[None, :] - rotation_rows[:, None])
    distance = jnp.minimum(distance, ANGLES - distance).astype(jnp.float32)
    return -0.5 * (distance / SIGMA_ROT) ** 2


def halve_kernel(blocks_ref, out_ref):
    for half in range(2):
        out_ref[:, half] = blocks_ref[:, :, half * CYCLES : (half + 1) * CYCLES]


def halve(blocks):
    count = 4
    return pl.pallas_call(
        halve_kernel,
        grid=(BLOCK // count,),
        in_specs=[pl.BlockSpec((count, ANGLES, 2 * CYCLES), lambda i: (i, 0, 0))],
        out_specs=pl.BlockSpec((count, 2, ANGLES, CYCLES), lambda i: (i, 0, 0, 0)),
        out_shape=jax.ShapeDtypeStruct((BLOCK, 2, ANGLES, CYCLES), jnp.bfloat16),
        compiler_params=pltpu.CompilerParams(vmem_limit_bytes=60 * 1024 * 1024),
    )(blocks)


def route_kernel(core_ref, place_ref, got_ref, out_ref):
    total = got_ref[0].astype(jnp.float32)
    for z in range(1, got_ref.shape[0]):
        total = total + got_ref[z].astype(jnp.float32)
    denom = total[ROWS * CLS_GRP :]
    high = denom.astype(jnp.bfloat16).astype(jnp.float32)
    denom = jnp.where(core_ref[0] == 0, high, denom - high)
    share = jnp.concatenate([total[: ROWS * CLS_GRP], denom], axis=0).astype(jnp.bfloat16)
    rows, columns = (ROWS + 1) * OWN_MAX, (ROWS + 1) * CLS_GRP
    place = place_ref[...]
    line = lax.broadcasted_iota(jnp.int32, (rows, columns), 0)
    line = (line // OWN_MAX) * 1024 + line % OWN_MAX - place
    for owner in range(0, 64, 8):
        chosen = jnp.concatenate(
            [jnp.where(line == -OWN_MAX * (owner + k), 1.0, 0.0) for k in range(8)], axis=0
        ).astype(jnp.bfloat16)
        out_ref[owner * rows : (owner + 8) * rows, :] = jnp.dot(
            chosen, share, preferred_element_type=jnp.float32
        ).astype(jnp.bfloat16)


def route(core, place, got):
    vmem = pl.BlockSpec(memory_space=pltpu.VMEM)
    return pl.pallas_call(
        route_kernel,
        in_specs=[pl.BlockSpec(memory_space=pltpu.SMEM), vmem, vmem],
        out_specs=vmem,
        out_shape=jax.ShapeDtypeStruct((64 * (ROWS + 1) * OWN_MAX, CYCLES), jnp.bfloat16),
        compiler_params=pltpu.CompilerParams(vmem_limit_bytes=6 * 1024 * 1024),
    )(core, place, got)


def finish_kernel(table_ref, got_ref, out_ref, held):
    total = got_ref[0].astype(jnp.float32)
    for plane in range(1, got_ref.shape[0]):
        total = total + got_ref[plane].astype(jnp.float32)
    held[...] = total
    rows = (ROWS + 1) * OWN_MAX
    at = ROWS * OWN_MAX
    denom = total[at : at + OWN_MAX] + total[rows + at : rows + at + OWN_MAX]
    denom = denom + total[2 * rows + at : 2 * rows + at + OWN_MAX]
    scale = (1.0 / ANGLES) / (denom + TAU)
    for slot in range(0, OWN_MAX, 2):
        pair = [
            held[pl.ds(k, 16 * (ROWS + 1), stride=OWN_MAX), :] * scale[k : k + 1]
            for k in (slot, slot + 1)
        ]
        polar = jnp.dot(
            table_ref[...],
            jnp.concatenate(pair, axis=-1),
            precision=TOP_PRECISION,
            preferred_element_type=jnp.float32,
        ).astype(jnp.bfloat16)
        for k in range(2):
            columns = slice(k * CYCLES, (k + 1) * CYCLES)
            out_ref[slot + k, :, :CYCLES] = polar[:ANGLES, columns]
            out_ref[slot + k, :, CYCLES:] = polar[ANGLES:, columns]


def finish(table, got):
    vmem = pl.BlockSpec(memory_space=pltpu.VMEM)
    return pl.pallas_call(
        finish_kernel,
        in_specs=[vmem, vmem],
        out_specs=vmem,
        out_shape=jax.ShapeDtypeStruct((OWN_MAX, ANGLES, 2 * CYCLES), jnp.bfloat16),
        scratch_shapes=[pltpu.VMEM((16 * (ROWS + 1) * OWN_MAX, CYCLES), jnp.float32)],
        compiler_params=pltpu.CompilerParams(vmem_limit_bytes=6 * 1024 * 1024),
    )(table, got)


def finish_table(cosine_table, sine_table):
    def laid(table):
        table = table.reshape(ANGLES, 8, 1, ROWS)
        return np.pad(table, ((0, 0), (0, 0), (0, 0), (0, 1)))

    cosine, sine = laid(cosine_table), laid(sine_table)
    real = np.concatenate([cosine, -sine], axis=2).reshape(ANGLES, 16 * (ROWS + 1))
    imag = np.concatenate([sine, cosine], axis=2).reshape(ANGLES, 16 * (ROWS + 1))
    return np.concatenate([real, imag])


def fetch(blocks, holders, images, contrast_rows, table, classes, small):
    half = contrast_rows.shape[0] // 2
    halves = halve(blocks).reshape(BLOCK * 2, ANGLES, CYCLES)
    sliced = lax.all_to_all(halves, ("wide_1", "wide_2"), 0, 0, tiled=True)
    early = image_spectra(images, 0, contrast_rows[:half], table)
    sliced, early, later, classes, small = lax.optimization_barrier(
        (sliced, early, contrast_rows[half:], classes, small)
    )
    picked = pick(sliced[:, None], holders % 16, 4)
    planes = lax.all_to_all(picked, "wide_0", 0, 0, tiled=True)
    late = image_spectra(images, 1, later, table)
    planes, late, step = lax.optimization_barrier((planes, late, stepped(classes)))
    picked = pick(planes, holders // 16, 8)
    mine = lax.all_to_all(picked, "wide_1", 0, 0, tiled=True).reshape(CLS_GRP, ANGLES, CYCLES)
    return mine, early, late, (*small, step)


def exchanged_evidence(pair, bit):
    got = lax.ppermute(pair, "narrow", [(k, k ^ bit) for k in range(8)])
    top = jnp.maximum(pair[:1], got[:1])
    total = pair[1:] * jnp.exp(pair[:1] - top) + got[1:] * jnp.exp(got[:1] - top)
    return jnp.concatenate([top, total])


def per_device(images, defocus, class_index, rotation_index, owner_map, roster, ref_store):
    class_group = lax.axis_index("narrow")
    core = lax.axis_index("wide_2")
    cosine_table, sine_table = angle_tables(ANGLES)
    leading_class = class_group * CLS_GRP
    arrival = jnp.arange(CLS_GRP, dtype=jnp.int32)
    within = arrival % STEPS * BLOCK + arrival // STEPS
    class_ids = leading_class + within
    mine_group = jnp.arange(8, dtype=jnp.int32)[:, None] == class_group
    holders = jnp.sum(jnp.where(mine_group, roster, 0), axis=0)

    low_table = np.concatenate([cosine_table, sine_table]).astype(jnp.bfloat16)
    turn = np.concatenate([cosine_table, -sine_table], axis=-1)
    filled = ((0, CYCLES - ANGLES), (0, 0))
    back = np.concatenate([np.pad(cosine_table, filled), np.pad(sine_table, filled)])
    contrast_rows = contrast(defocus)
    square = contrast_rows * contrast_rows
    prior = rotation_prior(rotation_index).T
    member = (class_index[None, :] == class_ids[:, None]).astype(jnp.float32)
    owners = jnp.sum(jnp.where(mine_group, owner_map.reshape(8, CLS_GRP), 0), axis=0)
    owners = owners.reshape(STEPS, BLOCK).T.reshape(CLS_GRP)
    same = owners[:, None] == owners[None, :]
    ranking = jnp.sum(same & (within[None, :] < within[:, None]), axis=1)
    place = owners * OWN_MAX + ranking
    place = jnp.arange(ROWS + 1, dtype=jnp.int32)[:, None] * 1024 + place[None, :]
    small = (square, prior, member, place.reshape(1, (ROWS + 1) * CLS_GRP))
    classes = class_index[None, :]
    table = finish_table(cosine_table, sine_table)
    mine, early, late, small = fetch(
        ref_store[0, 0], holders, images, contrast_rows, low_table, classes, small
    )
    square, prior, member, place, step = small
    mine, place = lax.optimization_barrier((mine, place + step))
    other = swapped(mine)
    keep, send, evidence = score(
        core.reshape(1), mine, other, early, late, low_table, turn, back, square, prior, member
    )
    share = pack(keep, swapped(send)).reshape(8, (ROWS + 1) * CLS_GRP, CYCLES)
    share = lax.all_to_all(share, "wide_1", 0, 0, tiled=True)
    sent = route(core.reshape(1), place, share).reshape(64, (ROWS + 1) * OWN_MAX, CYCLES)
    sent, evidence = lax.optimization_barrier((sent, evidence))
    got = lax.all_to_all(sent, WIDE, 0, 0, tiled=True)
    for bit in (2, 4, 1):
        evidence = exchanged_evidence(evidence, bit)
    log_evidence = evidence[0] + jnp.log(evidence[1])
    got = got.reshape(4, 16 * (ROWS + 1) * OWN_MAX, CYCLES)
    new_references = finish(table, got).reshape(1, 1, OWN_MAX, ANGLES, 2 * CYCLES)
    return (new_references, log_evidence)


def solution(mesh):
    split = Mesh(
        mesh.devices.reshape(4, 8, 2, mesh.shape["narrow"]),
        ("wide_0", "wide_1", "wide_2", "narrow"),
    )
    placed = (
        P(WIDE, None, None),
        P(WIDE),
        P(WIDE),
        P(WIDE),
        P(),
        P(),
        P(WIDE, "narrow", None, None, None),
    )
    return jax.shard_map(
        per_device,
        mesh=split,
        in_specs=placed,
        out_specs=(P(WIDE, "narrow", None, None, None), P(WIDE)),
        check_vma=False,
    )
```

```python
import math

import jax
import jax.numpy as jnp
import numpy as np
from jax import lax
from jax.experimental import pallas as pl
from jax.experimental.pallas import tpu as pltpu
from jax.sharding import Mesh
from jax.sharding import PartitionSpec as P

CYCLES = 128
ANGLES = 72
STEPS = 3
BLOCK = 8
OWN_MAX = 4
CLS_GRP = 24
SIGMA_ROT = 8
ROWS = 9
CHUNKS = 4
WIDE = ("wide_0", "wide_1", "wide_2")


TAU = 1.0
CONTRAST = 0.1
TOP_PRECISION = lax.Precision.HIGHEST


def swapped(x):
    return lax.ppermute(x, "wide_2", [(0, 1), (1, 0)])


def angle_tables(length):
    counting = np.arange(length)
    products = counting[:, None] * counting[None, :] % length
    phase_angle = products.astype(np.float32) * np.float32(2.0 * math.pi / length)
    return (np.cos(phase_angle), np.sin(phase_angle))


def contrast(defocus_rows):
    cycle_freq = (jnp.arange(CYCLES, dtype=jnp.float32) + 1.0) / CYCLES
    phase_angle = 8.0 * math.pi * defocus_rows[:, None] * cycle_freq[None, :] ** 2
    return -jnp.sin(phase_angle) - CONTRAST * jnp.cos(phase_angle)


def spectrum_of(polar, table):
    both = jnp.dot(table, polar, preferred_element_type=jnp.float32)
    cos_part, sin_part = both[:ANGLES], both[ANGLES:]
    real_part = cos_part[:, :CYCLES] + sin_part[:, CYCLES:]
    imag_part = cos_part[:, CYCLES:] - sin_part[:, :CYCLES]
    return real_part, imag_part


def spectra_kernel(table_ref, contrast_ref, image_ref, out_ref, held_real, held_imag):
    table = table_ref[...]
    count = image_ref.shape[0]
    for row in range(count):
        factor = contrast_ref[row : row + 1, :]
        factor = jnp.concatenate([factor, factor], axis=-1)
        weighted = (image_ref[row].astype(jnp.float32) * factor).astype(jnp.bfloat16)
        rows = pl.ds(row, ANGLES, stride=count)
        held_real[rows, :], held_imag[rows, :] = spectrum_of(weighted, table)
    shape = (ANGLES, count, CYCLES)
    out_ref[:, :, :CYCLES] = held_real[...].reshape(shape).astype(jnp.bfloat16)
    out_ref[:, :, CYCLES:] = held_imag[...].reshape(shape).astype(jnp.bfloat16)


def image_spectra(images, half, contrast_rows, table):
    particles = contrast_rows.shape[0] // 2
    count = 16
    skipped = half * particles // count
    return pl.pallas_call(
        spectra_kernel,
        grid=(particles // count,),
        in_specs=[
            pl.BlockSpec((2 * ANGLES, ANGLES), lambda i: (0, 0)),
            pl.BlockSpec((count, CYCLES), lambda i: (i + skipped, 0)),
            pl.BlockSpec((count, ANGLES, 2 * CYCLES), lambda i: (i + skipped, 0, 0)),
        ],
        out_specs=pl.BlockSpec((ANGLES, count, 2 * CYCLES), lambda i: (0, i, 0)),
        out_shape=jax.ShapeDtypeStruct((ANGLES, particles, 2 * CYCLES), jnp.bfloat16),
        scratch_shapes=[pltpu.VMEM((ANGLES * count, CYCLES), jnp.float32)] * 2,
        compiler_params=pltpu.CompilerParams(vmem_limit_bytes=56 * 1024 * 1024),
        cost_estimate=pl.CostEstimate(
            flops=particles * 4 * ANGLES * ANGLES * 2 * CYCLES,
            bytes_accessed=4 * particles * ANGLES * 2 * CYCLES,
            transcendentals=0,
        ),
    )(table, contrast_rows, images)


def pick_kernel(group_ref, roster_ref, source_ref, out_ref):
    planes = source_ref.shape[1] == STEPS
    for step in range(STEPS):
        holder = roster_ref[group_ref[0], step]
        value = source_ref[holder >> 4, step] if planes else source_ref[holder & 15, 0]
        for copy in range(out_ref.shape[0]):
            out_ref[copy, step] = value


def pick(group, roster, source, copies):
    smem = pl.BlockSpec(memory_space=pltpu.SMEM)
    vmem = pl.BlockSpec(memory_space=pltpu.VMEM)
    return pl.pallas_call(
        pick_kernel,
        in_specs=[smem, smem, vmem],
        out_specs=vmem,
        out_shape=jax.ShapeDtypeStruct((copies, STEPS, ANGLES, CYCLES), jnp.bfloat16),
        compiler_params=pltpu.CompilerParams(vmem_limit_bytes=2 * 1024 * 1024),
    )(group, roster, source)


def score_kernel(
    core_ref,
    mine_ref,
    other_ref,
    early_ref,
    late_ref,
    low_ref,
    turn_ref,
    back_ref,
    square_ref,
    prior_ref,
    member_ref,
    sums_ref,
    evidence_ref,
    ref_real,
    ref_imag,
    corr,
    scores,
    power,
    spectra_ref,
    sem,
):
    particles = spectra_ref.shape[1]
    depth, half = ANGLES // CHUNKS, particles // 2
    arriving = [
        pltpu.make_async_copy(
            source.at[pl.ds(n * depth, depth)],
            spectra_ref.at[pl.ds(n * depth, depth), pl.ds(k * half, half)],
            sem.at[n, k],
        )
        for n in range(CHUNKS)
        for k, source in enumerate((early_ref, late_ref))
    ]
    for copy in arriving:
        copy.start()
    first = core_ref[0] == 0
    table = low_ref[...]
    for c in range(CLS_GRP):
        mine, other = mine_ref[c], other_ref[c]
        polar = jnp.concatenate(
            [jnp.where(first, mine, other), jnp.where(first, other, mine)], axis=-1
        )
        real, imag = (
            part.astype(jnp.bfloat16).astype(jnp.float32) for part in spectrum_of(polar, table)
        )
        rows = pl.ds(c, ANGLES, stride=CLS_GRP)
        ref_real[rows, :], ref_imag[rows, :] = real, imag
        power[c : c + 1, :] = jnp.sum(real * real + imag * imag, axis=0, keepdims=True)
    square = square_ref[...]
    across = (((1,), (1,)), ((), ()))
    energy = 0.5 * lax.dot_general(
        power[...], square, across, precision=TOP_PRECISION, preferred_element_type=jnp.float32
    )
    for m in range(ANGLES):
        if m % depth == 0:
            for copy in arriving[m // depth * 2 : m // depth * 2 + 2]:
                copy.wait()
        rows = slice(m * CLS_GRP, (m + 1) * CLS_GRP)
        real, imag = ref_real[rows, :], ref_imag[rows, :]
        both = jnp.concatenate(
            [jnp.concatenate([real, -imag], axis=0), jnp.concatenate([imag, real], axis=0)],
            axis=-1,
        ).astype(jnp.bfloat16)
        corr[m * 2 * CLS_GRP : (m + 1) * 2 * CLS_GRP, :] = lax.dot_general(
            both, spectra_ref[m], across, preferred_element_type=jnp.float32
        )
    turn, prior = turn_ref[...], prior_ref[...]
    best = jnp.full((ANGLES, particles), -jnp.inf, jnp.float32)
    own = jnp.zeros((ANGLES, particles), jnp.float32)
    for c in range(0, CLS_GRP, 2):
        pair = [
            jnp.concatenate(
                [
                    corr[pl.ds(k, ANGLES, stride=2 * CLS_GRP), :],
                    corr[pl.ds(CLS_GRP + k, ANGLES, stride=2 * CLS_GRP), :],
                ],
                axis=0,
            )
            for k in (c, c + 1)
        ]
        rotated = jnp.dot(
            turn,
            jnp.concatenate(pair, axis=-1),
            precision=TOP_PRECISION,
            preferred_element_type=jnp.float32,
        )
        for k in range(2):
            value = rotated[:, k * particles : (k + 1) * particles]
            value = (value - energy[c + k : c + k + 1, :]) * (1.0 / ANGLES) + prior
            scores[c + k] = value
            best = jnp.maximum(best, value)
            own = own + jnp.where(member_ref[c + k : c + k + 1, :] > 0, value, 0.0)
    top = jnp.max(best, axis=0, keepdims=True)
    total = jnp.zeros((ANGLES, particles), jnp.float32)
    for c in range(CLS_GRP):
        total = total + jnp.exp(scores[c] - top)
    evidence_ref[0:1, :] = top
    evidence_ref[1:2, :] = jnp.sum(total, axis=0, keepdims=True)
    weight = jnp.exp(own - jnp.max(own, axis=0, keepdims=True))
    weight = weight / jnp.sum(weight, axis=0, keepdims=True)
    turned_back = jnp.dot(
        back_ref[...], weight, precision=TOP_PRECISION, preferred_element_type=jnp.float32
    )
    h_real = turned_back[:particles].T
    h_imag = turned_back[particles:].T
    member = member_ref[...]
    chosen = member.astype(jnp.bfloat16)
    for m in range(ANGLES):
        x_real = spectra_ref[m, :, :CYCLES].astype(jnp.float32)
        x_imag = spectra_ref[m, :, CYCLES:].astype(jnp.float32)
        hr, hi = h_real[:, m : m + 1], h_imag[:, m : m + 1]
        aligned = jnp.concatenate(
            [x_real * hr - x_imag * hi, x_real * hi + x_imag * hr], axis=-1
        ).astype(jnp.bfloat16)
        sums = jnp.dot(chosen, aligned, preferred_element_type=jnp.float32)
        sums_ref[0, m] = sums[:, :CYCLES]
        sums_ref[1, m] = sums[:, CYCLES:]
    denom = jnp.dot(
        member, square, precision=TOP_PRECISION, preferred_element_type=jnp.float32
    )
    sums_ref[0, ANGLES] = denom
    sums_ref[1, ANGLES] = denom


def score(core, mine, other, early, late, low_table, turn, back, square, prior, member):
    particles = 2 * early.shape[1]
    sums = jax.ShapeDtypeStruct((2, ANGLES + 1, CLS_GRP, CYCLES), jnp.float32)
    evidence = jax.ShapeDtypeStruct((2, particles), jnp.float32)
    vmem = pl.BlockSpec(memory_space=pltpu.VMEM)
    return pl.pallas_call(
        score_kernel,
        in_specs=[pl.BlockSpec(memory_space=pltpu.SMEM), vmem, vmem]
        + [pl.BlockSpec(memory_space=pltpu.HBM)] * 2
        + [vmem] * 6,
        out_specs=(vmem, vmem),
        out_shape=(sums, evidence),
        scratch_shapes=[
            pltpu.VMEM((ANGLES * CLS_GRP, CYCLES), jnp.float32),
            pltpu.VMEM((ANGLES * CLS_GRP, CYCLES), jnp.float32),
            pltpu.VMEM((ANGLES * 2 * CLS_GRP, particles), jnp.float32),
            pltpu.VMEM((CLS_GRP, ANGLES, particles), jnp.float32),
            pltpu.VMEM((CLS_GRP, CYCLES), jnp.float32),
            pltpu.VMEM((ANGLES, particles, 2 * CYCLES), jnp.bfloat16),
            pltpu.SemaphoreType.DMA((CHUNKS, 2)),
        ],
        compiler_params=pltpu.CompilerParams(vmem_limit_bytes=50 * 1024 * 1024),
    )(core, mine, other, early, late, low_table, turn, back, square, prior, member)


def pack_kernel(got_ref, out_ref):
    denom = got_ref[0, ANGLES] + got_ref[1, ANGLES]
    high = denom.astype(jnp.bfloat16)
    low = (denom - high.astype(jnp.float32)).astype(jnp.bfloat16)
    for z in range(out_ref.shape[0]):
        at = pl.ds(z * ROWS, ROWS)
        out_ref[z, :ROWS] = (got_ref[0, at] + got_ref[1, at]).astype(jnp.bfloat16)
        out_ref[z, ROWS] = high if z == 0 else low


def pack(got):
    vmem = pl.BlockSpec(memory_space=pltpu.VMEM)
    return pl.pallas_call(
        pack_kernel,
        in_specs=[vmem],
        out_specs=vmem,
        out_shape=jax.ShapeDtypeStruct((8, ROWS + 1, CLS_GRP, CYCLES), jnp.bfloat16),
        compiler_params=pltpu.CompilerParams(vmem_limit_bytes=4 * 1024 * 1024),
    )(got)


def rotation_prior(rotation_rows):
    counting = jnp.arange(ANGLES, dtype=jnp.int32)
    distance = jnp.abs(counting[None, :] - rotation_rows[:, None])
    distance = jnp.minimum(distance, ANGLES - distance).astype(jnp.float32)
    return -0.5 * (distance / SIGMA_ROT) ** 2


def halve_kernel(blocks_ref, out_ref):
    for half in range(2):
        out_ref[:, half] = blocks_ref[:, :, half * CYCLES : (half + 1) * CYCLES]


def halve(blocks):
    count = 4
    return pl.pallas_call(
        halve_kernel,
        grid=(BLOCK // count,),
        in_specs=[pl.BlockSpec((count, ANGLES, 2 * CYCLES), lambda i: (i, 0, 0))],
        out_specs=pl.BlockSpec((count, 2, ANGLES, CYCLES), lambda i: (i, 0, 0, 0)),
        out_shape=jax.ShapeDtypeStruct((BLOCK, 2, ANGLES, CYCLES), jnp.bfloat16),
        compiler_params=pltpu.CompilerParams(vmem_limit_bytes=60 * 1024 * 1024),
    )(blocks)


def route_kernel(core_ref, place_ref, got_ref, out_ref):
    total = got_ref[0].astype(jnp.float32)
    for z in range(1, got_ref.shape[0]):
        total = total + got_ref[z].astype(jnp.float32)
    denom = total[ROWS * CLS_GRP :]
    high = denom.astype(jnp.bfloat16).astype(jnp.float32)
    denom = jnp.where(core_ref[0] == 0, high, denom - high)
    share = jnp.concatenate([total[: ROWS * CLS_GRP], denom], axis=0).astype(jnp.bfloat16)
    rows, columns = (ROWS + 1) * OWN_MAX, (ROWS + 1) * CLS_GRP
    place = place_ref[...]
    line = lax.broadcasted_iota(jnp.int32, (rows, columns), 0)
    line = (line // OWN_MAX) * 1024 + line % OWN_MAX - place
    for owner in range(0, 64, 8):
        chosen = jnp.concatenate(
            [jnp.where(line == -OWN_MAX * (owner + k), 1.0, 0.0) for k in range(8)], axis=0
        ).astype(jnp.bfloat16)
        out_ref[owner * rows : (owner + 8) * rows, :] = jnp.dot(
            chosen, share, preferred_element_type=jnp.float32
        ).astype(jnp.bfloat16)


def route(core, place, got):
    vmem = pl.BlockSpec(memory_space=pltpu.VMEM)
    return pl.pallas_call(
        route_kernel,
        in_specs=[pl.BlockSpec(memory_space=pltpu.SMEM), vmem, vmem],
        out_specs=vmem,
        out_shape=jax.ShapeDtypeStruct((64 * (ROWS + 1) * OWN_MAX, CYCLES), jnp.bfloat16),
        compiler_params=pltpu.CompilerParams(vmem_limit_bytes=6 * 1024 * 1024),
    )(core, place, got)


def finish_kernel(table_ref, got_ref, out_ref, held):
    total = got_ref[0].astype(jnp.float32)
    for plane in range(1, got_ref.shape[0]):
        total = total + got_ref[plane].astype(jnp.float32)
    held[...] = total
    rows = (ROWS + 1) * OWN_MAX
    at = ROWS * OWN_MAX
    denom = total[at : at + OWN_MAX] + total[rows + at : rows + at + OWN_MAX]
    denom = denom + total[2 * rows + at : 2 * rows + at + OWN_MAX]
    scale = (1.0 / ANGLES) / (denom + TAU)
    for slot in range(0, OWN_MAX, 2):
        pair = [
            held[pl.ds(k, 16 * (ROWS + 1), stride=OWN_MAX), :] * scale[k : k + 1]
            for k in (slot, slot + 1)
        ]
        polar = jnp.dot(
            table_ref[...],
            jnp.concatenate(pair, axis=-1),
            precision=TOP_PRECISION,
            preferred_element_type=jnp.float32,
        ).astype(jnp.bfloat16)
        for k in range(2):
            columns = slice(k * CYCLES, (k + 1) * CYCLES)
            out_ref[slot + k, :, :CYCLES] = polar[:ANGLES, columns]
            out_ref[slot + k, :, CYCLES:] = polar[ANGLES:, columns]


def finish(table, got):
    vmem = pl.BlockSpec(memory_space=pltpu.VMEM)
    return pl.pallas_call(
        finish_kernel,
        in_specs=[vmem, vmem],
        out_specs=vmem,
        out_shape=jax.ShapeDtypeStruct((OWN_MAX, ANGLES, 2 * CYCLES), jnp.bfloat16),
        scratch_shapes=[pltpu.VMEM((16 * (ROWS + 1) * OWN_MAX, CYCLES), jnp.float32)],
        compiler_params=pltpu.CompilerParams(vmem_limit_bytes=6 * 1024 * 1024),
    )(table, got)


def finish_table(cosine_table, sine_table):
    def laid(table):
        table = table.reshape(ANGLES, 8, 1, ROWS)
        return np.pad(table, ((0, 0), (0, 0), (0, 0), (0, 1)))

    cosine, sine = laid(cosine_table), laid(sine_table)
    real = np.concatenate([cosine, -sine], axis=2).reshape(ANGLES, 16 * (ROWS + 1))
    imag = np.concatenate([sine, cosine], axis=2).reshape(ANGLES, 16 * (ROWS + 1))
    return np.concatenate([real, imag])


def fetch(blocks, group, roster, images, contrast_rows, table, small):
    halves = halve(blocks).reshape(BLOCK * 2, ANGLES, CYCLES)
    sliced = lax.all_to_all(halves, ("wide_1", "wide_2"), 0, 0, tiled=True)
    early = image_spectra(images, 0, contrast_rows, table)
    sliced, early, later = lax.optimization_barrier((sliced, early, contrast_rows))
    picked = pick(group, roster, sliced[:, None], 4)
    planes = lax.all_to_all(picked, "wide_0", 0, 0, tiled=True)
    late = image_spectra(images, 1, later, table)
    planes, late, small = lax.optimization_barrier((planes, late, small))
    picked = pick(group, roster, planes, 8)
    mine = lax.all_to_all(picked, "wide_1", 0, 0, tiled=True).reshape(CLS_GRP, ANGLES, CYCLES)
    return mine, early, late, small


def exchanged_evidence(pair, bit):
    got = lax.ppermute(pair, "narrow", [(k, k ^ bit) for k in range(8)])
    top = jnp.maximum(pair[:1], got[:1])
    total = pair[1:] * jnp.exp(pair[:1] - top) + got[1:] * jnp.exp(got[:1] - top)
    return jnp.concatenate([top, total])


def per_device(images, defocus, class_index, rotation_index, owner_map, roster, ref_store):
    class_group = lax.axis_index("narrow")
    core = lax.axis_index("wide_2")
    cosine_table, sine_table = angle_tables(ANGLES)
    leading_class = class_group * CLS_GRP
    arrival = jnp.arange(CLS_GRP, dtype=jnp.int32)
    within = arrival % STEPS * BLOCK + arrival // STEPS
    class_ids = leading_class + within
    mine_group = jnp.arange(8, dtype=jnp.int32)[:, None] == class_group

    low_table = np.concatenate([cosine_table, sine_table]).astype(jnp.bfloat16)
    turn = np.concatenate([cosine_table, -sine_table], axis=-1)
    filled = ((0, CYCLES - ANGLES), (0, 0))
    back = np.concatenate([np.pad(cosine_table, filled), np.pad(sine_table, filled)])
    contrast_rows = contrast(defocus)
    square = contrast_rows * contrast_rows
    prior = rotation_prior(rotation_index).T
    member = (class_index[None, :] == class_ids[:, None]).astype(jnp.float32)
    owners = jnp.sum(jnp.where(mine_group, owner_map.reshape(8, CLS_GRP), 0), axis=0)
    owners = owners.reshape(STEPS, BLOCK).T.reshape(CLS_GRP)
    same = owners[:, None] == owners[None, :]
    ranking = jnp.sum(same & (within[None, :] < within[:, None]), axis=1)
    place = owners * OWN_MAX + ranking
    place = jnp.arange(ROWS + 1, dtype=jnp.int32)[:, None] * 1024 + place[None, :]
    place = place.reshape(1, (ROWS + 1) * CLS_GRP)
    table = finish_table(cosine_table, sine_table)
    small = (square, prior, member, place)

    mine, early, late, small = fetch(
        ref_store[0, 0], class_group.reshape(1), roster, images, contrast_rows, low_table, small
    )
    square, prior, member, place = small
    other = swapped(mine)
    sums, evidence = score(
        core.reshape(1), mine, other, early, late, low_table, turn, back, square, prior, member
    )
    share = pack(lax.all_to_all(sums, "wide_2", 0, 0, tiled=True)).reshape(8, (ROWS + 1) * CLS_GRP, CYCLES)
    share = lax.all_to_all(share, "wide_1", 0, 0, tiled=True)
    sent = route(core.reshape(1), place, share).reshape(64, (ROWS + 1) * OWN_MAX, CYCLES)
    sent, evidence = lax.optimization_barrier((sent, evidence))
    got = lax.all_to_all(sent, WIDE, 0, 0, tiled=True)
    for bit in (2, 4, 1):
        evidence = exchanged_evidence(evidence, bit)
    log_evidence = evidence[0] + jnp.log(evidence[1])
    got = got.reshape(4, 16 * (ROWS + 1) * OWN_MAX, CYCLES)
    new_references = finish(table, got).reshape(1, 1, OWN_MAX, ANGLES, 2 * CYCLES)
    return (new_references, log_evidence)


def solution(mesh):
    split = Mesh(
        mesh.devices.reshape(4, 8, 2, mesh.shape["narrow"]),
        ("wide_0", "wide_1", "wide_2", "narrow"),
    )
    placed = (
        P(WIDE, None, None),
        P(WIDE),
        P(WIDE),
        P(WIDE),
        P(),
        P(),
        P(WIDE, "narrow", None, None, None),
    )
    return jax.shard_map(
        per_device,
        mesh=split,
        in_specs=placed,
        out_specs=(P(WIDE, "narrow", None, None, None), P(WIDE)),
        check_vma=False,
    )
```

```python
import math

import jax
import jax.numpy as jnp
import numpy as np
from jax import lax
from jax.experimental import pallas as pl
from jax.experimental.pallas import tpu as pltpu
from jax.sharding import Mesh
from jax.sharding import PartitionSpec as P

CYCLES = 128
ANGLES = 72
STEPS = 3
BLOCK = 8
OWN_MAX = 4
CLS_GRP = 24
SIGMA_ROT = 8
SHARES = 16
ROWS = 5
SLOT_ROWS = 24
DENOM_SHARE, DENOM_ROW = divmod(ANGLES, ROWS)
CHUNKS = 4
HIGH = ("wide_high", "wide_low")
WIDE = (*HIGH, "wide_1", "wide_2")


TAU = 1.0
CONTRAST = 0.1
TOP_PRECISION = lax.Precision.HIGHEST


def swapped(x):
    return lax.ppermute(x, "wide_2", [(0, 1), (1, 0)])


def angle_tables(length):
    counting = np.arange(length)
    products = counting[:, None] * counting[None, :] % length
    phase_angle = products.astype(np.float32) * np.float32(2.0 * math.pi / length)
    return (np.cos(phase_angle), np.sin(phase_angle))


def contrast(defocus_rows):
    cycle_freq = (jnp.arange(CYCLES, dtype=jnp.float32) + 1.0) / CYCLES
    phase_angle = 8.0 * math.pi * defocus_rows[:, None] * cycle_freq[None, :] ** 2
    return -jnp.sin(phase_angle) - CONTRAST * jnp.cos(phase_angle)


def spectrum_of(polar, table):
    both = jnp.dot(table, polar, preferred_element_type=jnp.float32)
    cos_part, sin_part = both[:ANGLES], both[ANGLES:]
    real_part = cos_part[:, :CYCLES] + sin_part[:, CYCLES:]
    imag_part = cos_part[:, CYCLES:] - sin_part[:, :CYCLES]
    return real_part, imag_part


def spectra_kernel(table_ref, contrast_ref, image_ref, out_ref, held_real, held_imag):
    table = table_ref[...]
    count = image_ref.shape[0]
    for row in range(count):
        factor = contrast_ref[row : row + 1, :]
        factor = jnp.concatenate([factor, factor], axis=-1)
        weighted = (image_ref[row].astype(jnp.float32) * factor).astype(jnp.bfloat16)
        rows = pl.ds(row, ANGLES, stride=count)
        held_real[rows, :], held_imag[rows, :] = spectrum_of(weighted, table)
    shape = (ANGLES, count, CYCLES)
    out_ref[:, :, :CYCLES] = held_real[...].reshape(shape).astype(jnp.bfloat16)
    out_ref[:, :, CYCLES:] = held_imag[...].reshape(shape).astype(jnp.bfloat16)


def image_spectra(images, half, contrast_rows, table):
    particles = contrast_rows.shape[0] // 2
    count = 16
    skipped = half * particles // count
    return pl.pallas_call(
        spectra_kernel,
        grid=(particles // count,),
        in_specs=[
            pl.BlockSpec((2 * ANGLES, ANGLES), lambda i: (0, 0)),
            pl.BlockSpec((count, CYCLES), lambda i: (i + skipped, 0)),
            pl.BlockSpec((count, ANGLES, 2 * CYCLES), lambda i: (i + skipped, 0, 0)),
        ],
        out_specs=pl.BlockSpec((ANGLES, count, 2 * CYCLES), lambda i: (0, i, 0)),
        out_shape=jax.ShapeDtypeStruct((ANGLES, particles, 2 * CYCLES), jnp.bfloat16),
        scratch_shapes=[pltpu.VMEM((ANGLES * count, CYCLES), jnp.float32)] * 2,
        compiler_params=pltpu.CompilerParams(vmem_limit_bytes=56 * 1024 * 1024),
        cost_estimate=pl.CostEstimate(
            flops=particles * 4 * ANGLES * ANGLES * 2 * CYCLES,
            bytes_accessed=4 * particles * ANGLES * 2 * CYCLES,
            transcendentals=0,
        ),
    )(table, contrast_rows, images)


def pick_kernel(group_ref, roster_ref, source_ref, out_ref):
    planes = source_ref.shape[1] == STEPS
    for step in range(STEPS):
        holder = roster_ref[group_ref[0], step]
        value = source_ref[holder >> 4, step] if planes else source_ref[holder & 15, 0]
        for copy in range(out_ref.shape[0]):
            out_ref[copy, step] = value


def pick(group, roster, source, copies):
    smem = pl.BlockSpec(memory_space=pltpu.SMEM)
    vmem = pl.BlockSpec(memory_space=pltpu.VMEM)
    return pl.pallas_call(
        pick_kernel,
        in_specs=[smem, smem, vmem],
        out_specs=vmem,
        out_shape=jax.ShapeDtypeStruct((copies, STEPS, ANGLES, CYCLES), jnp.bfloat16),
        compiler_params=pltpu.CompilerParams(vmem_limit_bytes=2 * 1024 * 1024),
    )(group, roster, source)


def score_kernel(
    core_ref,
    mine_ref,
    other_ref,
    early_ref,
    late_ref,
    low_ref,
    turn_ref,
    back_ref,
    square_ref,
    prior_ref,
    member_ref,
    sums_ref,
    evidence_ref,
    ref_real,
    ref_imag,
    corr,
    scores,
    power,
    spectra_ref,
    sem,
):
    particles = spectra_ref.shape[1]
    depth, half = ANGLES // CHUNKS, particles // 2
    arriving = [
        pltpu.make_async_copy(
            source.at[pl.ds(n * depth, depth)],
            spectra_ref.at[pl.ds(n * depth, depth), pl.ds(k * half, half)],
            sem.at[n, k],
        )
        for n in range(CHUNKS)
        for k, source in enumerate((early_ref, late_ref))
    ]
    for copy in arriving:
        copy.start()
    first = core_ref[0] == 0
    table = low_ref[...]
    for c in range(CLS_GRP):
        mine, other = mine_ref[c], other_ref[c]
        polar = jnp.concatenate(
            [jnp.where(first, mine, other), jnp.where(first, other, mine)], axis=-1
        )
        real, imag = (
            part.astype(jnp.bfloat16).astype(jnp.float32) for part in spectrum_of(polar, table)
        )
        rows = pl.ds(c, ANGLES, stride=CLS_GRP)
        ref_real[rows, :], ref_imag[rows, :] = real, imag
        power[c : c + 1, :] = jnp.sum(real * real + imag * imag, axis=0, keepdims=True)
    square = square_ref[...]
    across = (((1,), (1,)), ((), ()))
    energy = 0.5 * lax.dot_general(
        power[...], square, across, precision=TOP_PRECISION, preferred_element_type=jnp.float32
    )
    for m in range(ANGLES):
        if m % depth == 0:
            for copy in arriving[m // depth * 2 : m // depth * 2 + 2]:
                copy.wait()
        rows = slice(m * CLS_GRP, (m + 1) * CLS_GRP)
        real, imag = ref_real[rows, :], ref_imag[rows, :]
        both = jnp.concatenate(
            [jnp.concatenate([real, -imag], axis=0), jnp.concatenate([imag, real], axis=0)],
            axis=-1,
        ).astype(jnp.bfloat16)
        corr[m * 2 * CLS_GRP : (m + 1) * 2 * CLS_GRP, :] = lax.dot_general(
            both, spectra_ref[m], across, preferred_element_type=jnp.float32
        )
    turn, prior = turn_ref[...], prior_ref[...]
    best = jnp.full((ANGLES, particles), -jnp.inf, jnp.float32)
    own = jnp.zeros((ANGLES, particles), jnp.float32)
    for c in range(0, CLS_GRP, 2):
        pair = [
            jnp.concatenate(
                [
                    corr[pl.ds(k, ANGLES, stride=2 * CLS_GRP), :],
                    corr[pl.ds(CLS_GRP + k, ANGLES, stride=2 * CLS_GRP), :],
                ],
                axis=0,
            )
            for k in (c, c + 1)
        ]
        rotated = jnp.dot(
            turn,
            jnp.concatenate(pair, axis=-1),
            precision=TOP_PRECISION,
            preferred_element_type=jnp.float32,
        )
        for k in range(2):
            value = rotated[:, k * particles : (k + 1) * particles]
            value = (value - energy[c + k : c + k + 1, :]) * (1.0 / ANGLES) + prior
            scores[c + k] = value
            best = jnp.maximum(best, value)
            own = own + jnp.where(member_ref[c + k : c + k + 1, :] > 0, value, 0.0)
    top = jnp.max(best, axis=0, keepdims=True)
    total = jnp.zeros((ANGLES, particles), jnp.float32)
    for c in range(CLS_GRP):
        total = total + jnp.exp(scores[c] - top)
    evidence_ref[0:1, :] = top
    evidence_ref[1:2, :] = jnp.sum(total, axis=0, keepdims=True)
    weight = jnp.exp(own - jnp.max(own, axis=0, keepdims=True))
    weight = weight / jnp.sum(weight, axis=0, keepdims=True)
    turned_back = jnp.dot(
        back_ref[...], weight, precision=TOP_PRECISION, preferred_element_type=jnp.float32
    )
    h_real = turned_back[:particles].T
    h_imag = turned_back[particles:].T
    member = member_ref[...]
    chosen = member.astype(jnp.bfloat16)
    for m in range(ANGLES):
        x_real = spectra_ref[m, :, :CYCLES].astype(jnp.float32)
        x_imag = spectra_ref[m, :, CYCLES:].astype(jnp.float32)
        hr, hi = h_real[:, m : m + 1], h_imag[:, m : m + 1]
        aligned = jnp.concatenate(
            [x_real * hr - x_imag * hi, x_real * hi + x_imag * hr], axis=-1
        ).astype(jnp.bfloat16)
        sums = jnp.dot(chosen, aligned, preferred_element_type=jnp.float32)
        sums_ref[0, m] = sums[:, :CYCLES]
        sums_ref[1, m] = sums[:, CYCLES:]
    denom = jnp.dot(
        member, square, precision=TOP_PRECISION, preferred_element_type=jnp.float32
    )
    sums_ref[0, ANGLES] = denom
    sums_ref[1, ANGLES] = denom


def score(core, mine, other, early, late, low_table, turn, back, square, prior, member):
    particles = 2 * early.shape[1]
    sums = jax.ShapeDtypeStruct((2, ANGLES + 1, CLS_GRP, CYCLES), jnp.float32)
    evidence = jax.ShapeDtypeStruct((2, particles), jnp.float32)
    vmem = pl.BlockSpec(memory_space=pltpu.VMEM)
    return pl.pallas_call(
        score_kernel,
        in_specs=[pl.BlockSpec(memory_space=pltpu.SMEM), vmem, vmem]
        + [pl.BlockSpec(memory_space=pltpu.HBM)] * 2
        + [vmem] * 6,
        out_specs=(vmem, vmem),
        out_shape=(sums, evidence),
        scratch_shapes=[
            pltpu.VMEM((ANGLES * CLS_GRP, CYCLES), jnp.float32),
            pltpu.VMEM((ANGLES * CLS_GRP, CYCLES), jnp.float32),
            pltpu.VMEM((ANGLES * 2 * CLS_GRP, particles), jnp.float32),
            pltpu.VMEM((CLS_GRP, ANGLES, particles), jnp.float32),
            pltpu.VMEM((CLS_GRP, CYCLES), jnp.float32),
            pltpu.VMEM((ANGLES, particles, 2 * CYCLES), jnp.bfloat16),
            pltpu.SemaphoreType.DMA((CHUNKS, 2)),
        ],
        compiler_params=pltpu.CompilerParams(vmem_limit_bytes=50 * 1024 * 1024),
    )(core, mine, other, early, late, low_table, turn, back, square, prior, member)


def pack_kernel(got_ref, out_ref):
    denom = got_ref[0, ANGLES] + got_ref[1, ANGLES]
    high = denom.astype(jnp.bfloat16)
    low = (denom - high.astype(jnp.float32)).astype(jnp.bfloat16)
    for m in range(SHARES * ROWS):
        if m < ANGLES:
            value = (got_ref[0, m] + got_ref[1, m]).astype(jnp.bfloat16)
        elif m < ANGLES + 2:
            value = (high, low)[m - ANGLES]
        else:
            value = jnp.zeros_like(high)
        out_ref[m // ROWS, m % ROWS] = value


def pack(got):
    vmem = pl.BlockSpec(memory_space=pltpu.VMEM)
    return pl.pallas_call(
        pack_kernel,
        in_specs=[vmem],
        out_specs=vmem,
        out_shape=jax.ShapeDtypeStruct((SHARES, ROWS, CLS_GRP, CYCLES), jnp.bfloat16),
        compiler_params=pltpu.CompilerParams(vmem_limit_bytes=4 * 1024 * 1024),
    )(got)


def rotation_prior(rotation_rows):
    counting = jnp.arange(ANGLES, dtype=jnp.int32)
    distance = jnp.abs(counting[None, :] - rotation_rows[:, None])
    distance = jnp.minimum(distance, ANGLES - distance).astype(jnp.float32)
    return -0.5 * (distance / SIGMA_ROT) ** 2


def halve_kernel(blocks_ref, out_ref):
    for half in range(2):
        out_ref[:, half] = blocks_ref[:, :, half * CYCLES : (half + 1) * CYCLES]


def halve(blocks):
    count = 4
    return pl.pallas_call(
        halve_kernel,
        grid=(BLOCK // count,),
        in_specs=[pl.BlockSpec((count, ANGLES, 2 * CYCLES), lambda i: (i, 0, 0))],
        out_specs=pl.BlockSpec((count, 2, ANGLES, CYCLES), lambda i: (i, 0, 0, 0)),
        out_shape=jax.ShapeDtypeStruct((BLOCK, 2, ANGLES, CYCLES), jnp.bfloat16),
        compiler_params=pltpu.CompilerParams(vmem_limit_bytes=60 * 1024 * 1024),
    )(blocks)


def route_kernel(share_ref, place_ref, got_ref, out_ref):
    total = got_ref[0].astype(jnp.float32)
    for peer in range(1, SHARES):
        total = total + got_ref[peer].astype(jnp.float32)
    start = DENOM_ROW * CLS_GRP
    first, second = total[start : start + CLS_GRP], total[start + CLS_GRP : start + 2 * CLS_GRP]
    denom = first + second
    high = denom.astype(jnp.bfloat16).astype(jnp.float32)
    has_denom = share_ref[0] == DENOM_SHARE
    empty = jnp.zeros((CYCLES - ROWS * CLS_GRP, CYCLES), jnp.float32)
    share = jnp.concatenate(
        [
            total[:start],
            jnp.where(has_denom, high, first),
            jnp.where(has_denom, denom - high, second),
            total[start + 2 * CLS_GRP :],
            empty,
        ],
        axis=0,
    ).astype(jnp.bfloat16)
    place = place_ref[...]
    line = lax.broadcasted_iota(jnp.int32, (SLOT_ROWS, CYCLES), 0)
    line = (line // OWN_MAX) * 1024 + line % OWN_MAX - place
    for owner in range(0, 64, 8):
        chosen = jnp.concatenate(
            [jnp.where(line == -OWN_MAX * (owner + k), 1.0, 0.0) for k in range(8)], axis=0
        ).astype(jnp.bfloat16)
        out_ref[owner * SLOT_ROWS : (owner + 8) * SLOT_ROWS, :] = jnp.dot(
            chosen, share, preferred_element_type=jnp.float32
        ).astype(jnp.bfloat16)


def route(share, place, got):
    vmem = pl.BlockSpec(memory_space=pltpu.VMEM)
    return pl.pallas_call(
        route_kernel,
        in_specs=[pl.BlockSpec(memory_space=pltpu.SMEM), vmem, vmem],
        out_specs=vmem,
        out_shape=jax.ShapeDtypeStruct((64 * SLOT_ROWS, CYCLES), jnp.bfloat16),
        compiler_params=pltpu.CompilerParams(vmem_limit_bytes=6 * 1024 * 1024),
    )(share, place, got)


def finish_kernel(table_ref, got_ref, out_ref, held):
    total = got_ref[0].astype(jnp.float32) + got_ref[1].astype(jnp.float32)
    held[...] = total
    at = DENOM_SHARE * 2 * SLOT_ROWS + DENOM_ROW * OWN_MAX
    denom = total[at : at + OWN_MAX] + total[at + OWN_MAX : at + 2 * OWN_MAX]
    scale = (1.0 / ANGLES) / (denom + TAU)
    for slot in range(0, OWN_MAX, 2):
        pair = [
            held[pl.ds(k, held.shape[0] // OWN_MAX, stride=OWN_MAX), :] * scale[k : k + 1]
            for k in (slot, slot + 1)
        ]
        polar = jnp.dot(
            table_ref[...],
            jnp.concatenate(pair, axis=-1),
            precision=TOP_PRECISION,
            preferred_element_type=jnp.float32,
        ).astype(jnp.bfloat16)
        for k in range(2):
            columns = slice(k * CYCLES, (k + 1) * CYCLES)
            out_ref[slot + k, :, :CYCLES] = polar[:ANGLES, columns]
            out_ref[slot + k, :, CYCLES:] = polar[ANGLES:, columns]


def finish(table, got):
    vmem = pl.BlockSpec(memory_space=pltpu.VMEM)
    return pl.pallas_call(
        finish_kernel,
        in_specs=[vmem, vmem],
        out_specs=vmem,
        out_shape=jax.ShapeDtypeStruct((OWN_MAX, ANGLES, 2 * CYCLES), jnp.bfloat16),
        scratch_shapes=[pltpu.VMEM((2 * SHARES * SLOT_ROWS, CYCLES), jnp.float32)],
        compiler_params=pltpu.CompilerParams(vmem_limit_bytes=6 * 1024 * 1024),
    )(table, got)


def finish_table(cosine_table, sine_table):
    harmonic = np.arange(SHARES)[:, None] * ROWS + np.arange(SLOT_ROWS // OWN_MAX)
    filled = (np.arange(SLOT_ROWS // OWN_MAX) < ROWS) & (harmonic < ANGLES)

    def laid(table):
        return np.where(filled, table[:, harmonic % ANGLES], np.float32(0.0))[:, :, None]

    cosine, sine = laid(cosine_table), laid(sine_table)
    real = np.concatenate([cosine, -sine], axis=2).reshape(ANGLES, -1)
    imag = np.concatenate([sine, cosine], axis=2).reshape(ANGLES, -1)
    return np.concatenate([real, imag])


def fetch(blocks, group, roster, images, contrast_rows, table, small):
    halves = halve(blocks).reshape(BLOCK * 2, ANGLES, CYCLES)
    sliced = lax.all_to_all(halves, ("wide_1", "wide_2"), 0, 0, tiled=True)
    early = image_spectra(images, 0, contrast_rows, table)
    sliced, early, later = lax.optimization_barrier((sliced, early, contrast_rows))
    picked = pick(group, roster, sliced[:, None], 4)
    planes = lax.all_to_all(picked, HIGH, 0, 0, tiled=True)
    late = image_spectra(images, 1, later, table)
    planes, late, small = lax.optimization_barrier((planes, late, small))
    picked = pick(group, roster, planes, 8)
    mine = lax.all_to_all(picked, "wide_1", 0, 0, tiled=True).reshape(CLS_GRP, ANGLES, CYCLES)
    return mine, early, late, small


def exchanged_evidence(pair, bit):
    got = lax.ppermute(pair, "narrow", [(k, k ^ bit) for k in range(8)])
    top = jnp.maximum(pair[:1], got[:1])
    total = pair[1:] * jnp.exp(pair[:1] - top) + got[1:] * jnp.exp(got[:1] - top)
    return jnp.concatenate([top, total])


def per_device(images, defocus, class_index, rotation_index, owner_map, roster, ref_store):
    class_group = lax.axis_index("narrow")
    core = lax.axis_index("wide_2")
    cosine_table, sine_table = angle_tables(ANGLES)
    leading_class = class_group * CLS_GRP
    arrival = jnp.arange(CLS_GRP, dtype=jnp.int32)
    within = arrival % STEPS * BLOCK + arrival // STEPS
    class_ids = leading_class + within
    mine_group = jnp.arange(8, dtype=jnp.int32)[:, None] == class_group

    low_table = np.concatenate([cosine_table, sine_table]).astype(jnp.bfloat16)
    turn = np.concatenate([cosine_table, -sine_table], axis=-1)
    filled = ((0, CYCLES - ANGLES), (0, 0))
    back = np.concatenate([np.pad(cosine_table, filled), np.pad(sine_table, filled)])
    contrast_rows = contrast(defocus)
    square = contrast_rows * contrast_rows
    prior = rotation_prior(rotation_index).T
    member = (class_index[None, :] == class_ids[:, None]).astype(jnp.float32)
    owners = jnp.sum(jnp.where(mine_group, owner_map.reshape(8, CLS_GRP), 0), axis=0)
    owners = owners.reshape(STEPS, BLOCK).T.reshape(CLS_GRP)
    same = owners[:, None] == owners[None, :]
    ranking = jnp.sum(same & (within[None, :] < within[:, None]), axis=1)
    place = owners * OWN_MAX + ranking
    place = jnp.arange(ROWS, dtype=jnp.int32)[:, None] * 1024 + place[None, :]
    place = jnp.pad(
        place.reshape(1, ROWS * CLS_GRP),
        ((0, 0), (0, CYCLES - ROWS * CLS_GRP)),
        constant_values=2**20,
    )
    table = finish_table(cosine_table, sine_table)
    small = (square, prior, member, place)

    mine, early, late, small = fetch(
        ref_store[0, 0], class_group.reshape(1), roster, images, contrast_rows, low_table, small
    )
    square, prior, member, place = small
    other = swapped(mine)
    sums, evidence = score(
        core.reshape(1), mine, other, early, late, low_table, turn, back, square, prior, member
    )
    share = pack(lax.all_to_all(sums, "wide_2", 0, 0, tiled=True))
    share = share.reshape(SHARES, ROWS * CLS_GRP, CYCLES)
    share = lax.all_to_all(share, ("wide_low", "wide_1"), 0, 0, tiled=True)
    own_share = lax.axis_index(("wide_low", "wide_1"))
    sent = route(own_share.reshape(1), place, share).reshape(64, SLOT_ROWS, CYCLES)
    sent, evidence = lax.optimization_barrier((sent, evidence))
    got = lax.all_to_all(sent, WIDE, 0, 0, tiled=True)
    for bit in (2, 4, 1):
        evidence = exchanged_evidence(evidence, bit)
    log_evidence = evidence[0] + jnp.log(evidence[1])
    got = got.reshape(2, 2 * SHARES * SLOT_ROWS, CYCLES)
    new_references = finish(table, got).reshape(1, 1, OWN_MAX, ANGLES, 2 * CYCLES)
    return (new_references, log_evidence)


def solution(mesh):
    split = Mesh(
        mesh.devices.reshape(2, 2, 8, 2, mesh.shape["narrow"]),
        (*WIDE, "narrow"),
    )
    placed = (
        P(WIDE, None, None),
        P(WIDE),
        P(WIDE),
        P(WIDE),
        P(),
        P(),
        P(WIDE, "narrow", None, None, None),
    )
    return jax.shard_map(
        per_device,
        mesh=split,
        in_specs=placed,
        out_specs=(P(WIDE, "narrow", None, None, None), P(WIDE)),
        check_vma=False,
    )
```

```python
import math

import jax
import jax.numpy as jnp
import numpy as np
from jax import lax
from jax.experimental import pallas as pl
from jax.experimental.pallas import tpu as pltpu
from jax.sharding import Mesh
from jax.sharding import PartitionSpec as P

CYCLES = 128
ANGLES = 72
STEPS = 3
BLOCK = 8
OWN_MAX = 4
CLS_GRP = 24
SIGMA_ROT = 8
SHARES = 16
ROWS = 5
SLOT_ROWS = 24
DENOM_SHARE, DENOM_ROW = divmod(ANGLES, ROWS)
CHUNKS = 4
HIGH = ("wide_high", "wide_low")
WIDE = (*HIGH, "wide_1", "wide_2")


TAU = 1.0
CONTRAST = 0.1
TOP_PRECISION = lax.Precision.HIGHEST


def swapped(x):
    return lax.ppermute(x, "wide_2", [(0, 1), (1, 0)])


def angle_tables(length):
    counting = np.arange(length)
    products = counting[:, None] * counting[None, :] % length
    phase_angle = products.astype(np.float32) * np.float32(2.0 * math.pi / length)
    return (np.cos(phase_angle), np.sin(phase_angle))


def contrast(defocus_rows):
    cycle_freq = (jnp.arange(CYCLES, dtype=jnp.float32) + 1.0) / CYCLES
    phase_angle = 8.0 * math.pi * defocus_rows[:, None] * cycle_freq[None, :] ** 2
    return -jnp.sin(phase_angle) - CONTRAST * jnp.cos(phase_angle)


def spectrum_of(polar, table):
    both = jnp.dot(table, polar, preferred_element_type=jnp.float32)
    cos_part, sin_part = both[:ANGLES], both[ANGLES:]
    real_part = cos_part[:, :CYCLES] + sin_part[:, CYCLES:]
    imag_part = cos_part[:, CYCLES:] - sin_part[:, :CYCLES]
    return real_part, imag_part


def spectra_kernel(table_ref, contrast_ref, image_ref, out_ref, held_real, held_imag):
    table = table_ref[...]
    count = image_ref.shape[0]
    for row in range(count):
        factor = contrast_ref[row : row + 1, :]
        factor = jnp.concatenate([factor, factor], axis=-1)
        weighted = (image_ref[row].astype(jnp.float32) * factor).astype(jnp.bfloat16)
        rows = pl.ds(row, ANGLES, stride=count)
        held_real[rows, :], held_imag[rows, :] = spectrum_of(weighted, table)
    shape = (ANGLES, count, CYCLES)
    out_ref[:, :, :CYCLES] = held_real[...].reshape(shape).astype(jnp.bfloat16)
    out_ref[:, :, CYCLES:] = held_imag[...].reshape(shape).astype(jnp.bfloat16)


def image_spectra(images, half, contrast_rows, table):
    particles = contrast_rows.shape[0] // 2
    count = 16
    skipped = half * particles // count
    return pl.pallas_call(
        spectra_kernel,
        grid=(particles // count,),
        in_specs=[
            pl.BlockSpec((2 * ANGLES, ANGLES), lambda i: (0, 0)),
            pl.BlockSpec((count, CYCLES), lambda i: (i + skipped, 0)),
            pl.BlockSpec((count, ANGLES, 2 * CYCLES), lambda i: (i + skipped, 0, 0)),
        ],
        out_specs=pl.BlockSpec((ANGLES, count, 2 * CYCLES), lambda i: (0, i, 0)),
        out_shape=jax.ShapeDtypeStruct((ANGLES, particles, 2 * CYCLES), jnp.bfloat16),
        scratch_shapes=[pltpu.VMEM((ANGLES * count, CYCLES), jnp.float32)] * 2,
        compiler_params=pltpu.CompilerParams(vmem_limit_bytes=56 * 1024 * 1024),
        cost_estimate=pl.CostEstimate(
            flops=particles * 4 * ANGLES * ANGLES * 2 * CYCLES,
            bytes_accessed=4 * particles * ANGLES * 2 * CYCLES,
            transcendentals=0,
        ),
    )(table, contrast_rows, images)


def pick_kernel(group_ref, roster_ref, source_ref, out_ref):
    planes = source_ref.shape[1] == STEPS
    for step in range(STEPS):
        holder = roster_ref[group_ref[0], step]
        value = source_ref[holder >> 4, step] if planes else source_ref[holder & 15, 0]
        for copy in range(out_ref.shape[0]):
            out_ref[copy, step] = value


def pick(group, roster, source, copies):
    smem = pl.BlockSpec(memory_space=pltpu.SMEM)
    vmem = pl.BlockSpec(memory_space=pltpu.VMEM)
    return pl.pallas_call(
        pick_kernel,
        in_specs=[smem, smem, vmem],
        out_specs=vmem,
        out_shape=jax.ShapeDtypeStruct((copies, STEPS, ANGLES, CYCLES), jnp.bfloat16),
        compiler_params=pltpu.CompilerParams(vmem_limit_bytes=2 * 1024 * 1024),
    )(group, roster, source)


def score_kernel(
    core_ref,
    mine_ref,
    other_ref,
    early_ref,
    late_ref,
    low_ref,
    turn_ref,
    back_ref,
    square_ref,
    prior_ref,
    member_ref,
    sums_ref,
    evidence_ref,
    ref_real,
    ref_imag,
    corr,
    scores,
    power,
    spectra_ref,
    sem,
):
    particles = spectra_ref.shape[1]
    depth, half = ANGLES // CHUNKS, particles // 2
    arriving = [
        pltpu.make_async_copy(
            source.at[pl.ds(n * depth, depth)],
            spectra_ref.at[pl.ds(n * depth, depth), pl.ds(k * half, half)],
            sem.at[n, k],
        )
        for n in range(CHUNKS)
        for k, source in enumerate((early_ref, late_ref))
    ]
    for copy in arriving:
        copy.start()
    first = core_ref[0] == 0
    table = low_ref[...]
    for c in range(CLS_GRP):
        mine, other = mine_ref[c], other_ref[c]
        polar = jnp.concatenate(
            [jnp.where(first, mine, other), jnp.where(first, other, mine)], axis=-1
        )
        real, imag = (
            part.astype(jnp.bfloat16).astype(jnp.float32) for part in spectrum_of(polar, table)
        )
        rows = pl.ds(c, ANGLES, stride=CLS_GRP)
        ref_real[rows, :], ref_imag[rows, :] = real, imag
        power[c : c + 1, :] = jnp.sum(real * real + imag * imag, axis=0, keepdims=True)
    square = square_ref[...]
    across = (((1,), (1,)), ((), ()))
    energy = 0.5 * lax.dot_general(
        power[...], square, across, precision=TOP_PRECISION, preferred_element_type=jnp.float32
    )
    for m in range(ANGLES):
        if m % depth == 0:
            for copy in arriving[m // depth * 2 : m // depth * 2 + 2]:
                copy.wait()
        rows = slice(m * CLS_GRP, (m + 1) * CLS_GRP)
        real, imag = ref_real[rows, :], ref_imag[rows, :]
        both = jnp.concatenate(
            [jnp.concatenate([real, -imag], axis=0), jnp.concatenate([imag, real], axis=0)],
            axis=-1,
        ).astype(jnp.bfloat16)
        corr[m * 2 * CLS_GRP : (m + 1) * 2 * CLS_GRP, :] = lax.dot_general(
            both, spectra_ref[m], across, preferred_element_type=jnp.float32
        )
    turn, prior = turn_ref[...], prior_ref[...]
    best = jnp.full((ANGLES, particles), -jnp.inf, jnp.float32)
    own = jnp.zeros((ANGLES, particles), jnp.float32)
    for c in range(0, CLS_GRP, 2):
        pair = [
            jnp.concatenate(
                [
                    corr[pl.ds(k, ANGLES, stride=2 * CLS_GRP), :],
                    corr[pl.ds(CLS_GRP + k, ANGLES, stride=2 * CLS_GRP), :],
                ],
                axis=0,
            )
            for k in (c, c + 1)
        ]
        rotated = jnp.dot(
            turn,
            jnp.concatenate(pair, axis=-1),
            precision=TOP_PRECISION,
            preferred_element_type=jnp.float32,
        )
        for k in range(2):
            value = rotated[:, k * particles : (k + 1) * particles]
            value = (value - energy[c + k : c + k + 1, :]) * (1.0 / ANGLES) + prior
            scores[c + k] = value
            best = jnp.maximum(best, value)
            own = own + jnp.where(member_ref[c + k : c + k + 1, :] > 0, value, 0.0)
    top = jnp.max(best, axis=0, keepdims=True)
    total = jnp.zeros((ANGLES, particles), jnp.float32)
    for c in range(CLS_GRP):
        total = total + jnp.exp(scores[c] - top)
    evidence_ref[0:1, :] = top
    evidence_ref[1:2, :] = jnp.sum(total, axis=0, keepdims=True)
    weight = jnp.exp(own - jnp.max(own, axis=0, keepdims=True))
    weight = weight / jnp.sum(weight, axis=0, keepdims=True)
    turned_back = jnp.dot(
        back_ref[...], weight, precision=TOP_PRECISION, preferred_element_type=jnp.float32
    )
    h_real = turned_back[:particles].T
    h_imag = turned_back[particles:].T
    member = member_ref[...]
    chosen = member.astype(jnp.bfloat16)
    for m in range(ANGLES):
        x_real = spectra_ref[m, :, :CYCLES].astype(jnp.float32)
        x_imag = spectra_ref[m, :, CYCLES:].astype(jnp.float32)
        hr, hi = h_real[:, m : m + 1], h_imag[:, m : m + 1]
        aligned = jnp.concatenate(
            [x_real * hr - x_imag * hi, x_real * hi + x_imag * hr], axis=-1
        ).astype(jnp.bfloat16)
        sums = jnp.dot(chosen, aligned, preferred_element_type=jnp.float32)
        sums_ref[0, m] = sums[:, :CYCLES]
        sums_ref[1, m] = sums[:, CYCLES:]
    denom = jnp.dot(
        member, square, precision=TOP_PRECISION, preferred_element_type=jnp.float32
    )
    sums_ref[0, ANGLES] = denom
    sums_ref[1, ANGLES] = denom


def score(core, mine, other, early, late, low_table, turn, back, square, prior, member):
    particles = 2 * early.shape[1]
    sums = jax.ShapeDtypeStruct((2, ANGLES + 1, CLS_GRP, CYCLES), jnp.float32)
    evidence = jax.ShapeDtypeStruct((2, particles), jnp.float32)
    vmem = pl.BlockSpec(memory_space=pltpu.VMEM)
    return pl.pallas_call(
        score_kernel,
        in_specs=[pl.BlockSpec(memory_space=pltpu.SMEM), vmem, vmem]
        + [pl.BlockSpec(memory_space=pltpu.HBM)] * 2
        + [vmem] * 6,
        out_specs=(vmem, vmem),
        out_shape=(sums, evidence),
        scratch_shapes=[
            pltpu.VMEM((ANGLES * CLS_GRP, CYCLES), jnp.float32),
            pltpu.VMEM((ANGLES * CLS_GRP, CYCLES), jnp.float32),
            pltpu.VMEM((ANGLES * 2 * CLS_GRP, particles), jnp.float32),
            pltpu.VMEM((CLS_GRP, ANGLES, particles), jnp.float32),
            pltpu.VMEM((CLS_GRP, CYCLES), jnp.float32),
            pltpu.VMEM((ANGLES, particles, 2 * CYCLES), jnp.bfloat16),
            pltpu.SemaphoreType.DMA((CHUNKS, 2)),
        ],
        compiler_params=pltpu.CompilerParams(vmem_limit_bytes=50 * 1024 * 1024),
    )(core, mine, other, early, late, low_table, turn, back, square, prior, member)


def pack_kernel(got_ref, out_ref):
    denom = got_ref[0, ANGLES] + got_ref[1, ANGLES]
    high = denom.astype(jnp.bfloat16)
    low = (denom - high.astype(jnp.float32)).astype(jnp.bfloat16)
    for m in range(SHARES * ROWS):
        if m < ANGLES:
            value = (got_ref[0, m] + got_ref[1, m]).astype(jnp.bfloat16)
        elif m < ANGLES + 2:
            value = (high, low)[m - ANGLES]
        else:
            value = jnp.zeros_like(high)
        out_ref[m // ROWS, m % ROWS] = value


def pack(got):
    vmem = pl.BlockSpec(memory_space=pltpu.VMEM)
    return pl.pallas_call(
        pack_kernel,
        in_specs=[vmem],
        out_specs=vmem,
        out_shape=jax.ShapeDtypeStruct((SHARES, ROWS, CLS_GRP, CYCLES), jnp.bfloat16),
        compiler_params=pltpu.CompilerParams(vmem_limit_bytes=4 * 1024 * 1024),
    )(got)


def rotation_prior(rotation_rows):
    counting = jnp.arange(ANGLES, dtype=jnp.int32)
    distance = jnp.abs(counting[None, :] - rotation_rows[:, None])
    distance = jnp.minimum(distance, ANGLES - distance).astype(jnp.float32)
    return -0.5 * (distance / SIGMA_ROT) ** 2


def halve_kernel(blocks_ref, out_ref):
    for half in range(2):
        out_ref[:, half] = blocks_ref[:, :, half * CYCLES : (half + 1) * CYCLES]


def halve(blocks):
    count = 4
    return pl.pallas_call(
        halve_kernel,
        grid=(BLOCK // count,),
        in_specs=[pl.BlockSpec((count, ANGLES, 2 * CYCLES), lambda i: (i, 0, 0))],
        out_specs=pl.BlockSpec((count, 2, ANGLES, CYCLES), lambda i: (i, 0, 0, 0)),
        out_shape=jax.ShapeDtypeStruct((BLOCK, 2, ANGLES, CYCLES), jnp.bfloat16),
        compiler_params=pltpu.CompilerParams(vmem_limit_bytes=60 * 1024 * 1024),
    )(blocks)


def route_kernel(share_ref, place_ref, got_ref, out_ref):
    total = got_ref[0].astype(jnp.float32)
    for peer in range(1, SHARES):
        total = total + got_ref[peer].astype(jnp.float32)
    start = DENOM_ROW * CLS_GRP
    first, second = total[start : start + CLS_GRP], total[start + CLS_GRP : start + 2 * CLS_GRP]
    denom = first + second
    high = denom.astype(jnp.bfloat16).astype(jnp.float32)
    has_denom = share_ref[0] == DENOM_SHARE
    empty = jnp.zeros((CYCLES - ROWS * CLS_GRP, CYCLES), jnp.float32)
    share = jnp.concatenate(
        [
            total[:start],
            jnp.where(has_denom, high, first),
            jnp.where(has_denom, denom - high, second),
            total[start + 2 * CLS_GRP :],
            empty,
        ],
        axis=0,
    ).astype(jnp.bfloat16)
    place = place_ref[...]
    line = lax.broadcasted_iota(jnp.int32, (SLOT_ROWS, CYCLES), 0)
    line = (line // OWN_MAX) * 1024 + line % OWN_MAX - place
    for owner in range(0, 64, 8):
        chosen = jnp.concatenate(
            [jnp.where(line == -OWN_MAX * (owner + k), 1.0, 0.0) for k in range(8)], axis=0
        ).astype(jnp.bfloat16)
        out_ref[owner * SLOT_ROWS : (owner + 8) * SLOT_ROWS, :] = jnp.dot(
            chosen, share, preferred_element_type=jnp.float32
        ).astype(jnp.bfloat16)


def route(share, place, got):
    vmem = pl.BlockSpec(memory_space=pltpu.VMEM)
    return pl.pallas_call(
        route_kernel,
        in_specs=[pl.BlockSpec(memory_space=pltpu.SMEM), vmem, vmem],
        out_specs=vmem,
        out_shape=jax.ShapeDtypeStruct((64 * SLOT_ROWS, CYCLES), jnp.bfloat16),
        compiler_params=pltpu.CompilerParams(vmem_limit_bytes=6 * 1024 * 1024),
    )(share, place, got)


def finish_kernel(table_ref, got_ref, out_ref, held):
    total = got_ref[0].astype(jnp.float32) + got_ref[1].astype(jnp.float32)
    held[...] = total
    at = DENOM_SHARE * 2 * SLOT_ROWS + DENOM_ROW * OWN_MAX
    denom = total[at : at + OWN_MAX] + total[at + OWN_MAX : at + 2 * OWN_MAX]
    scale = (1.0 / ANGLES) / (denom + TAU)
    for slot in range(0, OWN_MAX, 2):
        pair = [
            held[pl.ds(k, held.shape[0] // OWN_MAX, stride=OWN_MAX), :] * scale[k : k + 1]
            for k in (slot, slot + 1)
        ]
        polar = jnp.dot(
            table_ref[...],
            jnp.concatenate(pair, axis=-1),
            precision=TOP_PRECISION,
            preferred_element_type=jnp.float32,
        ).astype(jnp.bfloat16)
        for k in range(2):
            columns = slice(k * CYCLES, (k + 1) * CYCLES)
            out_ref[slot + k, :, :CYCLES] = polar[:ANGLES, columns]
            out_ref[slot + k, :, CYCLES:] = polar[ANGLES:, columns]


def finish(table, got):
    vmem = pl.BlockSpec(memory_space=pltpu.VMEM)
    return pl.pallas_call(
        finish_kernel,
        in_specs=[vmem, vmem],
        out_specs=vmem,
        out_shape=jax.ShapeDtypeStruct((OWN_MAX, ANGLES, 2 * CYCLES), jnp.bfloat16),
        scratch_shapes=[pltpu.VMEM((2 * SHARES * SLOT_ROWS, CYCLES), jnp.float32)],
        compiler_params=pltpu.CompilerParams(vmem_limit_bytes=6 * 1024 * 1024),
    )(table, got)


def finish_table(cosine_table, sine_table):
    harmonic = np.arange(SHARES)[:, None] * ROWS + np.arange(SLOT_ROWS // OWN_MAX)
    filled = (np.arange(SLOT_ROWS // OWN_MAX) < ROWS) & (harmonic < ANGLES)

    def laid(table):
        return np.where(filled, table[:, harmonic % ANGLES], np.float32(0.0))[:, :, None]

    cosine, sine = laid(cosine_table), laid(sine_table)
    real = np.concatenate([cosine, -sine], axis=2).reshape(ANGLES, -1)
    imag = np.concatenate([sine, cosine], axis=2).reshape(ANGLES, -1)
    return np.concatenate([real, imag])


def fetch(blocks, group, roster, images, contrast_rows, table, small):
    halves = halve(blocks).reshape(BLOCK * 2, ANGLES, CYCLES)
    sliced = lax.all_to_all(halves, ("wide_1", "wide_2"), 0, 0, tiled=True)
    early = image_spectra(images, 0, contrast_rows, table)
    sliced, early, later = lax.optimization_barrier((sliced, early, contrast_rows))
    picked = pick(group, roster, sliced[:, None], 4)
    planes = lax.all_to_all(picked, HIGH, 0, 0, tiled=True)
    late = image_spectra(images, 1, later, table)
    planes, late, small = lax.optimization_barrier((planes, late, small))
    picked = pick(group, roster, planes, 8)
    mine = lax.all_to_all(picked, "wide_1", 0, 0, tiled=True).reshape(CLS_GRP, ANGLES, CYCLES)
    return mine, early, late, small


def exchanged_evidence(pair, bit):
    got = lax.ppermute(pair, "narrow", [(k, k ^ bit) for k in range(8)])
    top = jnp.maximum(pair[:1], got[:1])
    total = pair[1:] * jnp.exp(pair[:1] - top) + got[1:] * jnp.exp(got[:1] - top)
    return jnp.concatenate([top, total])


def per_device(images, defocus, class_index, rotation_index, owner_map, roster, ref_store):
    class_group = lax.axis_index("narrow")
    core = lax.axis_index("wide_2")
    cosine_table, sine_table = angle_tables(ANGLES)
    leading_class = class_group * CLS_GRP
    arrival = jnp.arange(CLS_GRP, dtype=jnp.int32)
    within = arrival % STEPS * BLOCK + arrival // STEPS
    class_ids = leading_class + within
    mine_group = jnp.arange(8, dtype=jnp.int32)[:, None] == class_group

    low_table = np.concatenate([cosine_table, sine_table]).astype(jnp.bfloat16)
    turn = np.concatenate([cosine_table, -sine_table], axis=-1)
    filled = ((0, CYCLES - ANGLES), (0, 0))
    back = np.concatenate([np.pad(cosine_table, filled), np.pad(sine_table, filled)])
    contrast_rows = contrast(defocus)
    square = contrast_rows * contrast_rows
    prior = rotation_prior(rotation_index).T
    member = (class_index[None, :] == class_ids[:, None]).astype(jnp.float32)
    owners = jnp.sum(jnp.where(mine_group, owner_map.reshape(8, CLS_GRP), 0), axis=0)
    owners = owners.reshape(STEPS, BLOCK).T.reshape(CLS_GRP)
    same = owners[:, None] == owners[None, :]
    ranking = jnp.sum(same & (within[None, :] < within[:, None]), axis=1)
    place = owners * OWN_MAX + ranking
    place = jnp.arange(ROWS, dtype=jnp.int32)[:, None] * 1024 + place[None, :]
    place = jnp.pad(
        place.reshape(1, ROWS * CLS_GRP),
        ((0, 0), (0, CYCLES - ROWS * CLS_GRP)),
        constant_values=2**20,
    )
    table = finish_table(cosine_table, sine_table)
    small = (square, prior, member, place)

    mine, early, late, small = fetch(
        ref_store[0, 0], class_group.reshape(1), roster, images, contrast_rows, low_table, small
    )
    square, prior, member, place = small
    other = swapped(mine)
    sums, evidence = score(
        core.reshape(1), mine, other, early, late, low_table, turn, back, square, prior, member
    )
    share = pack(lax.all_to_all(sums, "wide_2", 0, 0, tiled=True))
    share = share.reshape(SHARES, ROWS * CLS_GRP, CYCLES)
    share, evidence = lax.optimization_barrier((share, evidence))
    share = lax.all_to_all(share, ("wide_low", "wide_1"), 0, 0, tiled=True)
    for bit in (2, 4):
        evidence = exchanged_evidence(evidence, bit)
    share, evidence = lax.optimization_barrier((share, evidence))
    own_share = lax.axis_index(("wide_low", "wide_1"))
    sent = route(own_share.reshape(1), place, share).reshape(64, SLOT_ROWS, CYCLES)
    sent, evidence = lax.optimization_barrier((sent, evidence))
    got = lax.all_to_all(sent, WIDE, 0, 0, tiled=True)
    evidence = exchanged_evidence(evidence, 1)
    log_evidence = evidence[0] + jnp.log(evidence[1])
    got = got.reshape(2, 2 * SHARES * SLOT_ROWS, CYCLES)
    new_references = finish(table, got).reshape(1, 1, OWN_MAX, ANGLES, 2 * CYCLES)
    return (new_references, log_evidence)


def solution(mesh):
    split = Mesh(
        mesh.devices.reshape(2, 2, 8, 2, mesh.shape["narrow"]),
        (*WIDE, "narrow"),
    )
    placed = (
        P(WIDE, None, None),
        P(WIDE),
        P(WIDE),
        P(WIDE),
        P(),
        P(),
        P(WIDE, "narrow", None, None, None),
    )
    return jax.shard_map(
        per_device,
        mesh=split,
        in_specs=placed,
        out_specs=(P(WIDE, "narrow", None, None, None), P(WIDE)),
        check_vma=False,
    )
```

```python
import math

import jax
import jax.numpy as jnp
import numpy as np
from jax import lax
from jax.experimental import pallas as pl
from jax.experimental.pallas import tpu as pltpu
from jax.sharding import Mesh
from jax.sharding import PartitionSpec as P

CYCLES = 128
ANGLES = 72
STEPS = 3
BLOCK = 8
OWN_MAX = 4
CLS_GRP = 24
SIGMA_ROT = 8
SHARES = 16
ROWS = 5
SLOT_ROWS = 24
DENOM_SHARE, DENOM_ROW = divmod(ANGLES, ROWS)
CHUNKS = 4
HIGH = ("wide_high", "wide_low")
WIDE = (*HIGH, "wide_1", "wide_2")


TAU = 1.0
CONTRAST = 0.1
TOP_PRECISION = lax.Precision.HIGHEST


def swapped(x):
    return lax.ppermute(x, "wide_2", [(0, 1), (1, 0)])


def angle_tables(length):
    counting = np.arange(length)
    products = counting[:, None] * counting[None, :] % length
    phase_angle = products.astype(np.float32) * np.float32(2.0 * math.pi / length)
    return (np.cos(phase_angle), np.sin(phase_angle))


def contrast(defocus_rows):
    cycle_freq = (jnp.arange(CYCLES, dtype=jnp.float32) + 1.0) / CYCLES
    phase_angle = 8.0 * math.pi * defocus_rows[:, None] * cycle_freq[None, :] ** 2
    return -jnp.sin(phase_angle) - CONTRAST * jnp.cos(phase_angle)


def spectrum_of(polar, table):
    both = jnp.dot(table, polar, preferred_element_type=jnp.float32)
    cos_part, sin_part = both[:ANGLES], both[ANGLES:]
    real_part = cos_part[:, :CYCLES] + sin_part[:, CYCLES:]
    imag_part = cos_part[:, CYCLES:] - sin_part[:, :CYCLES]
    return real_part, imag_part


def spectra_kernel(table_ref, contrast_ref, image_ref, out_ref, held_real, held_imag):
    table = table_ref[...]
    count = image_ref.shape[0]
    for row in range(count):
        factor = contrast_ref[row : row + 1, :]
        factor = jnp.concatenate([factor, factor], axis=-1)
        weighted = (image_ref[row].astype(jnp.float32) * factor).astype(jnp.bfloat16)
        rows = pl.ds(row, ANGLES, stride=count)
        held_real[rows, :], held_imag[rows, :] = spectrum_of(weighted, table)
    shape = (ANGLES, count, CYCLES)
    out_ref[:, :, :CYCLES] = held_real[...].reshape(shape).astype(jnp.bfloat16)
    out_ref[:, :, CYCLES:] = held_imag[...].reshape(shape).astype(jnp.bfloat16)


def image_spectra(images, half, contrast_rows, table):
    particles = contrast_rows.shape[0] // 2
    count = 16
    skipped = half * particles // count
    return pl.pallas_call(
        spectra_kernel,
        grid=(particles // count,),
        in_specs=[
            pl.BlockSpec((2 * ANGLES, ANGLES), lambda i: (0, 0)),
            pl.BlockSpec((count, CYCLES), lambda i: (i + skipped, 0)),
            pl.BlockSpec((count, ANGLES, 2 * CYCLES), lambda i: (i + skipped, 0, 0)),
        ],
        out_specs=pl.BlockSpec((ANGLES, count, 2 * CYCLES), lambda i: (0, i, 0)),
        out_shape=jax.ShapeDtypeStruct((ANGLES, particles, 2 * CYCLES), jnp.bfloat16),
        scratch_shapes=[pltpu.VMEM((ANGLES * count, CYCLES), jnp.float32)] * 2,
        compiler_params=pltpu.CompilerParams(vmem_limit_bytes=56 * 1024 * 1024),
        cost_estimate=pl.CostEstimate(
            flops=particles * 4 * ANGLES * ANGLES * 2 * CYCLES,
            bytes_accessed=4 * particles * ANGLES * 2 * CYCLES,
            transcendentals=0,
        ),
    )(table, contrast_rows, images)


def pick_kernel(group_ref, roster_ref, source_ref, out_ref):
    planes = source_ref.shape[1] == STEPS
    for step in range(STEPS):
        holder = roster_ref[group_ref[0], step]
        value = source_ref[holder >> 4, step] if planes else source_ref[holder & 15, 0]
        for copy in range(out_ref.shape[0]):
            out_ref[copy, step] = value


def pick(group, roster, source, copies):
    smem = pl.BlockSpec(memory_space=pltpu.SMEM)
    vmem = pl.BlockSpec(memory_space=pltpu.VMEM)
    return pl.pallas_call(
        pick_kernel,
        in_specs=[smem, smem, vmem],
        out_specs=vmem,
        out_shape=jax.ShapeDtypeStruct((copies, STEPS, ANGLES, CYCLES), jnp.bfloat16),
        compiler_params=pltpu.CompilerParams(vmem_limit_bytes=2 * 1024 * 1024),
    )(group, roster, source)


def score_kernel(
    core_ref,
    mine_ref,
    other_ref,
    early_ref,
    late_ref,
    low_ref,
    turn_ref,
    back_ref,
    square_ref,
    prior_ref,
    member_ref,
    keep_ref,
    send_ref,
    evidence_ref,
    ref_real,
    ref_imag,
    corr,
    scores,
    power,
    spectra_ref,
    sem,
):
    particles = spectra_ref.shape[1]
    depth, half = ANGLES // CHUNKS, particles // 2
    arriving = [
        pltpu.make_async_copy(
            source.at[pl.ds(n * depth, depth)],
            spectra_ref.at[pl.ds(n * depth, depth), pl.ds(k * half, half)],
            sem.at[n, k],
        )
        for n in range(CHUNKS)
        for k, source in enumerate((early_ref, late_ref))
    ]
    for copy in arriving:
        copy.start()
    first = core_ref[0] == 0
    table = low_ref[...]
    for c in range(CLS_GRP):
        mine, other = mine_ref[c], other_ref[c]
        polar = jnp.concatenate(
            [jnp.where(first, mine, other), jnp.where(first, other, mine)], axis=-1
        )
        real, imag = (
            part.astype(jnp.bfloat16).astype(jnp.float32) for part in spectrum_of(polar, table)
        )
        rows = pl.ds(c, ANGLES, stride=CLS_GRP)
        ref_real[rows, :], ref_imag[rows, :] = real, imag
        power[c : c + 1, :] = jnp.sum(real * real + imag * imag, axis=0, keepdims=True)
    square = square_ref[...]
    across = (((1,), (1,)), ((), ()))
    energy = 0.5 * lax.dot_general(
        power[...], square, across, precision=TOP_PRECISION, preferred_element_type=jnp.float32
    )
    for m in range(ANGLES):
        if m % depth == 0:
            for copy in arriving[m // depth * 2 : m // depth * 2 + 2]:
                copy.wait()
        rows = slice(m * CLS_GRP, (m + 1) * CLS_GRP)
        real, imag = ref_real[rows, :], ref_imag[rows, :]
        both = jnp.concatenate(
            [jnp.concatenate([real, -imag], axis=0), jnp.concatenate([imag, real], axis=0)],
            axis=-1,
        ).astype(jnp.bfloat16)
        corr[m * 2 * CLS_GRP : (m + 1) * 2 * CLS_GRP, :] = lax.dot_general(
            both, spectra_ref[m], across, preferred_element_type=jnp.float32
        )
    turn, prior = turn_ref[...], prior_ref[...]
    best = jnp.full((ANGLES, particles), -jnp.inf, jnp.float32)
    own = jnp.zeros((ANGLES, particles), jnp.float32)
    for c in range(0, CLS_GRP, 2):
        pair = [
            jnp.concatenate(
                [
                    corr[pl.ds(k, ANGLES, stride=2 * CLS_GRP), :],
                    corr[pl.ds(CLS_GRP + k, ANGLES, stride=2 * CLS_GRP), :],
                ],
                axis=0,
            )
            for k in (c, c + 1)
        ]
        rotated = jnp.dot(
            turn,
            jnp.concatenate(pair, axis=-1),
            precision=TOP_PRECISION,
            preferred_element_type=jnp.float32,
        )
        for k in range(2):
            value = rotated[:, k * particles : (k + 1) * particles]
            value = (value - energy[c + k : c + k + 1, :]) * (1.0 / ANGLES) + prior
            scores[c + k] = value
            best = jnp.maximum(best, value)
            own = own + jnp.where(member_ref[c + k : c + k + 1, :] > 0, value, 0.0)
    top = jnp.max(best, axis=0, keepdims=True)
    total = jnp.zeros((ANGLES, particles), jnp.float32)
    for c in range(CLS_GRP):
        total = total + jnp.exp(scores[c] - top)
    evidence_ref[0:1, :] = top
    evidence_ref[1:2, :] = jnp.sum(total, axis=0, keepdims=True)
    weight = jnp.exp(own - jnp.max(own, axis=0, keepdims=True))
    weight = weight / jnp.sum(weight, axis=0, keepdims=True)
    turned_back = jnp.dot(
        back_ref[...], weight, precision=TOP_PRECISION, preferred_element_type=jnp.float32
    )
    h_real = turned_back[:particles].T
    h_imag = turned_back[particles:].T
    member = member_ref[...]
    chosen = member.astype(jnp.bfloat16)
    for m in range(ANGLES):
        x_real = spectra_ref[m, :, :CYCLES].astype(jnp.float32)
        x_imag = spectra_ref[m, :, CYCLES:].astype(jnp.float32)
        hr, hi = h_real[:, m : m + 1], h_imag[:, m : m + 1]
        aligned = jnp.concatenate(
            [x_real * hr - x_imag * hi, x_real * hi + x_imag * hr], axis=-1
        ).astype(jnp.bfloat16)
        sums = jnp.dot(chosen, aligned, preferred_element_type=jnp.float32)
        real_sum, imag_sum = sums[:, :CYCLES], sums[:, CYCLES:]
        keep_ref[m] = jnp.where(first, real_sum, imag_sum)
        send_ref[m] = jnp.where(first, imag_sum, real_sum)
    denom = jnp.dot(
        member, square, precision=TOP_PRECISION, preferred_element_type=jnp.float32
    )
    keep_ref[ANGLES] = denom
    send_ref[ANGLES] = denom


def score(core, mine, other, early, late, low_table, turn, back, square, prior, member):
    particles = 2 * early.shape[1]
    sums = jax.ShapeDtypeStruct((ANGLES + 1, CLS_GRP, CYCLES), jnp.float32)
    evidence = jax.ShapeDtypeStruct((2, particles), jnp.float32)
    vmem = pl.BlockSpec(memory_space=pltpu.VMEM)
    return pl.pallas_call(
        score_kernel,
        in_specs=[pl.BlockSpec(memory_space=pltpu.SMEM), vmem, vmem]
        + [pl.BlockSpec(memory_space=pltpu.HBM)] * 2
        + [vmem] * 6,
        out_specs=(vmem, vmem, vmem),
        out_shape=(sums, sums, evidence),
        scratch_shapes=[
            pltpu.VMEM((ANGLES * CLS_GRP, CYCLES), jnp.float32),
            pltpu.VMEM((ANGLES * CLS_GRP, CYCLES), jnp.float32),
            pltpu.VMEM((ANGLES * 2 * CLS_GRP, particles), jnp.float32),
            pltpu.VMEM((CLS_GRP, ANGLES, particles), jnp.float32),
            pltpu.VMEM((CLS_GRP, CYCLES), jnp.float32),
            pltpu.VMEM((ANGLES, particles, 2 * CYCLES), jnp.bfloat16),
            pltpu.SemaphoreType.DMA((CHUNKS, 2)),
        ],
        compiler_params=pltpu.CompilerParams(vmem_limit_bytes=50 * 1024 * 1024),
    )(core, mine, other, early, late, low_table, turn, back, square, prior, member)


def pack_kernel(keep_ref, got_ref, out_ref):
    denom = keep_ref[ANGLES] + got_ref[ANGLES]
    high = denom.astype(jnp.bfloat16)
    low = (denom - high.astype(jnp.float32)).astype(jnp.bfloat16)
    for m in range(SHARES * ROWS):
        if m < ANGLES:
            value = (keep_ref[m] + got_ref[m]).astype(jnp.bfloat16)
        elif m < ANGLES + 2:
            value = (high, low)[m - ANGLES]
        else:
            value = jnp.zeros_like(high)
        out_ref[m // ROWS, m % ROWS] = value


def pack(keep, got):
    vmem = pl.BlockSpec(memory_space=pltpu.VMEM)
    return pl.pallas_call(
        pack_kernel,
        in_specs=[vmem, vmem],
        out_specs=vmem,
        out_shape=jax.ShapeDtypeStruct((SHARES, ROWS, CLS_GRP, CYCLES), jnp.bfloat16),
        compiler_params=pltpu.CompilerParams(vmem_limit_bytes=4 * 1024 * 1024),
    )(keep, got)


def rotation_prior(rotation_rows):
    counting = jnp.arange(ANGLES, dtype=jnp.int32)
    distance = jnp.abs(counting[None, :] - rotation_rows[:, None])
    distance = jnp.minimum(distance, ANGLES - distance).astype(jnp.float32)
    return -0.5 * (distance / SIGMA_ROT) ** 2


def halve_kernel(blocks_ref, out_ref):
    for half in range(2):
        out_ref[:, half] = blocks_ref[:, :, half * CYCLES : (half + 1) * CYCLES]


def halve(blocks):
    count = 4
    return pl.pallas_call(
        halve_kernel,
        grid=(BLOCK // count,),
        in_specs=[pl.BlockSpec((count, ANGLES, 2 * CYCLES), lambda i: (i, 0, 0))],
        out_specs=pl.BlockSpec((count, 2, ANGLES, CYCLES), lambda i: (i, 0, 0, 0)),
        out_shape=jax.ShapeDtypeStruct((BLOCK, 2, ANGLES, CYCLES), jnp.bfloat16),
        compiler_params=pltpu.CompilerParams(vmem_limit_bytes=60 * 1024 * 1024),
    )(blocks)


def route_kernel(share_ref, place_ref, got_ref, out_ref):
    total = got_ref[0].astype(jnp.float32)
    for peer in range(1, SHARES):
        total = total + got_ref[peer].astype(jnp.float32)
    start = DENOM_ROW * CLS_GRP
    first, second = total[start : start + CLS_GRP], total[start + CLS_GRP : start + 2 * CLS_GRP]
    denom = first + second
    high = denom.astype(jnp.bfloat16).astype(jnp.float32)
    has_denom = share_ref[0] == DENOM_SHARE
    empty = jnp.zeros((CYCLES - ROWS * CLS_GRP, CYCLES), jnp.float32)
    share = jnp.concatenate(
        [
            total[:start],
            jnp.where(has_denom, high, first),
            jnp.where(has_denom, denom - high, second),
            total[start + 2 * CLS_GRP :],
            empty,
        ],
        axis=0,
    ).astype(jnp.bfloat16)
    place = place_ref[...]
    line = lax.broadcasted_iota(jnp.int32, (SLOT_ROWS, CYCLES), 0)
    line = (line // OWN_MAX) * 1024 + line % OWN_MAX - place
    for owner in range(0, 64, 8):
        chosen = jnp.concatenate(
            [jnp.where(line == -OWN_MAX * (owner + k), 1.0, 0.0) for k in range(8)], axis=0
        ).astype(jnp.bfloat16)
        out_ref[owner * SLOT_ROWS : (owner + 8) * SLOT_ROWS, :] = jnp.dot(
            chosen, share, preferred_element_type=jnp.float32
        ).astype(jnp.bfloat16)


def route(share, place, got):
    vmem = pl.BlockSpec(memory_space=pltpu.VMEM)
    return pl.pallas_call(
        route_kernel,
        in_specs=[pl.BlockSpec(memory_space=pltpu.SMEM), vmem, vmem],
        out_specs=vmem,
        out_shape=jax.ShapeDtypeStruct((64 * SLOT_ROWS, CYCLES), jnp.bfloat16),
        compiler_params=pltpu.CompilerParams(vmem_limit_bytes=6 * 1024 * 1024),
    )(share, place, got)


def finish_kernel(table_ref, got_ref, out_ref, held):
    total = got_ref[0].astype(jnp.float32) + got_ref[1].astype(jnp.float32)
    held[...] = total
    at = DENOM_SHARE * 2 * SLOT_ROWS + DENOM_ROW * OWN_MAX
    denom = total[at : at + OWN_MAX] + total[at + OWN_MAX : at + 2 * OWN_MAX]
    scale = (1.0 / ANGLES) / (denom + TAU)
    for slot in range(0, OWN_MAX, 2):
        pair = [
            held[pl.ds(k, held.shape[0] // OWN_MAX, stride=OWN_MAX), :] * scale[k : k + 1]
            for k in (slot, slot + 1)
        ]
        polar = jnp.dot(
            table_ref[...],
            jnp.concatenate(pair, axis=-1),
            precision=TOP_PRECISION,
            preferred_element_type=jnp.float32,
        ).astype(jnp.bfloat16)
        for k in range(2):
            columns = slice(k * CYCLES, (k + 1) * CYCLES)
            out_ref[slot + k, :, :CYCLES] = polar[:ANGLES, columns]
            out_ref[slot + k, :, CYCLES:] = polar[ANGLES:, columns]


def finish(table, got):
    vmem = pl.BlockSpec(memory_space=pltpu.VMEM)
    return pl.pallas_call(
        finish_kernel,
        in_specs=[vmem, vmem],
        out_specs=vmem,
        out_shape=jax.ShapeDtypeStruct((OWN_MAX, ANGLES, 2 * CYCLES), jnp.bfloat16),
        scratch_shapes=[pltpu.VMEM((2 * SHARES * SLOT_ROWS, CYCLES), jnp.float32)],
        compiler_params=pltpu.CompilerParams(vmem_limit_bytes=6 * 1024 * 1024),
    )(table, got)


def finish_table(cosine_table, sine_table):
    harmonic = np.arange(SHARES)[:, None] * ROWS + np.arange(SLOT_ROWS // OWN_MAX)
    filled = (np.arange(SLOT_ROWS // OWN_MAX) < ROWS) & (harmonic < ANGLES)

    def laid(table):
        return np.where(filled, table[:, harmonic % ANGLES], np.float32(0.0))[:, :, None]

    cosine, sine = laid(cosine_table), laid(sine_table)
    real = np.concatenate([cosine, -sine], axis=2).reshape(ANGLES, -1)
    imag = np.concatenate([sine, cosine], axis=2).reshape(ANGLES, -1)
    return np.concatenate([real, imag])


def fetch(blocks, group, roster, images, contrast_rows, table, small):
    halves = halve(blocks).reshape(BLOCK * 2, ANGLES, CYCLES)
    sliced = lax.all_to_all(halves, ("wide_1", "wide_2"), 0, 0, tiled=True)
    early = image_spectra(images, 0, contrast_rows, table)
    sliced, early, later = lax.optimization_barrier((sliced, early, contrast_rows))
    picked = pick(group, roster, sliced[:, None], 4)
    planes = lax.all_to_all(picked, HIGH, 0, 0, tiled=True)
    late = image_spectra(images, 1, later, table)
    planes, late, small = lax.optimization_barrier((planes, late, small))
    picked = pick(group, roster, planes, 8)
    mine = lax.all_to_all(picked, "wide_1", 0, 0, tiled=True).reshape(CLS_GRP, ANGLES, CYCLES)
    return mine, early, late, small


def exchanged_evidence(pair, bit):
    got = lax.ppermute(pair, "narrow", [(k, k ^ bit) for k in range(8)])
    top = jnp.maximum(pair[:1], got[:1])
    total = pair[1:] * jnp.exp(pair[:1] - top) + got[1:] * jnp.exp(got[:1] - top)
    return jnp.concatenate([top, total])


def per_device(images, defocus, class_index, rotation_index, owner_map, roster, ref_store):
    class_group = lax.axis_index("narrow")
    core = lax.axis_index("wide_2")
    cosine_table, sine_table = angle_tables(ANGLES)
    leading_class = class_group * CLS_GRP
    arrival = jnp.arange(CLS_GRP, dtype=jnp.int32)
    within = arrival % STEPS * BLOCK + arrival // STEPS
    class_ids = leading_class + within
    mine_group = jnp.arange(8, dtype=jnp.int32)[:, None] == class_group

    low_table = np.concatenate([cosine_table, sine_table]).astype(jnp.bfloat16)
    turn = np.concatenate([cosine_table, -sine_table], axis=-1)
    filled = ((0, CYCLES - ANGLES), (0, 0))
    back = np.concatenate([np.pad(cosine_table, filled), np.pad(sine_table, filled)])
    contrast_rows = contrast(defocus)
    square = contrast_rows * contrast_rows
    prior = rotation_prior(rotation_index).T
    member = (class_index[None, :] == class_ids[:, None]).astype(jnp.float32)
    def places(owner_map):
        owners = jnp.sum(jnp.where(mine_group, owner_map.reshape(8, CLS_GRP), 0), axis=0)
        owners = owners.reshape(STEPS, BLOCK).T.reshape(CLS_GRP)
        same = owners[:, None] == owners[None, :]
        ranking = jnp.sum(same & (within[None, :] < within[:, None]), axis=1)
        place = owners * OWN_MAX + ranking
        place = jnp.arange(ROWS, dtype=jnp.int32)[:, None] * 1024 + place[None, :]
        return jnp.pad(
            place.reshape(1, ROWS * CLS_GRP),
            ((0, 0), (0, CYCLES - ROWS * CLS_GRP)),
            constant_values=2**20,
        )

    table = finish_table(cosine_table, sine_table)
    small = (square, prior, member)

    mine, early, late, small = fetch(
        ref_store[0, 0], class_group.reshape(1), roster, images, contrast_rows, low_table, small
    )
    square, prior, member = small
    other = swapped(mine)
    keep, send, evidence = score(
        core.reshape(1), mine, other, early, late, low_table, turn, back, square, prior, member
    )
    send, owner_map = lax.optimization_barrier((send, owner_map))
    got, place = lax.optimization_barrier((swapped(send), places(owner_map)))
    share = pack(keep, got)
    share = share.reshape(SHARES, ROWS * CLS_GRP, CYCLES)
    share, evidence = lax.optimization_barrier((share, evidence))
    share = lax.all_to_all(share, ("wide_low", "wide_1"), 0, 0, tiled=True)
    for bit in (2, 4):
        evidence = exchanged_evidence(evidence, bit)
    share, evidence = lax.optimization_barrier((share, evidence))
    own_share = lax.axis_index(("wide_low", "wide_1"))
    sent = route(own_share.reshape(1), place, share).reshape(64, SLOT_ROWS, CYCLES)
    sent, evidence = lax.optimization_barrier((sent, evidence))
    got = lax.all_to_all(sent, WIDE, 0, 0, tiled=True)
    evidence = exchanged_evidence(evidence, 1)
    log_evidence = evidence[0] + jnp.log(evidence[1])
    got = got.reshape(2, 2 * SHARES * SLOT_ROWS, CYCLES)
    new_references = finish(table, got).reshape(1, 1, OWN_MAX, ANGLES, 2 * CYCLES)
    return (new_references, log_evidence)


def solution(mesh):
    split = Mesh(
        mesh.devices.reshape(2, 2, 8, 2, mesh.shape["narrow"]),
        (*WIDE, "narrow"),
    )
    placed = (
        P(WIDE, None, None),
        P(WIDE),
        P(WIDE),
        P(WIDE),
        P(),
        P(),
        P(WIDE, "narrow", None, None, None),
    )
    return jax.shard_map(
        per_device,
        mesh=split,
        in_specs=placed,
        out_specs=(P(WIDE, "narrow", None, None, None), P(WIDE)),
        check_vma=False,
    )
```

```python
import math

import jax
import jax.numpy as jnp
import numpy as np
from jax import lax
from jax.experimental import pallas as pl
from jax.experimental.pallas import tpu as pltpu
from jax.sharding import Mesh
from jax.sharding import PartitionSpec as P

CYCLES = 128
ANGLES = 72
STEPS = 3
BLOCK = 8
OWN_MAX = 4
CLS_GRP = 24
SIGMA_ROT = 8
SHARES = 16
ROWS = 5
SLOT_ROWS = 24
DENOM_SHARE, DENOM_ROW = divmod(ANGLES, ROWS)
CHUNKS = 4
HIGH = ("wide_high", "wide_low")
WIDE = (*HIGH, "wide_1", "wide_2")


TAU = 1.0
CONTRAST = 0.1
TOP_PRECISION = lax.Precision.HIGHEST


def swapped(x):
    return lax.ppermute(x, "wide_2", [(0, 1), (1, 0)])


def angle_tables(length):
    counting = np.arange(length)
    products = counting[:, None] * counting[None, :] % length
    phase_angle = products.astype(np.float32) * np.float32(2.0 * math.pi / length)
    return (np.cos(phase_angle), np.sin(phase_angle))


def contrast(defocus_rows):
    cycle_freq = (jnp.arange(CYCLES, dtype=jnp.float32) + 1.0) / CYCLES
    phase_angle = 8.0 * math.pi * defocus_rows[:, None] * cycle_freq[None, :] ** 2
    return -jnp.sin(phase_angle) - CONTRAST * jnp.cos(phase_angle)


def spectrum_of(polar, table):
    both = jnp.dot(table, polar, preferred_element_type=jnp.float32)
    cos_part, sin_part = both[:ANGLES], both[ANGLES:]
    real_part = cos_part[:, :CYCLES] + sin_part[:, CYCLES:]
    imag_part = cos_part[:, CYCLES:] - sin_part[:, :CYCLES]
    return real_part, imag_part


def spectra_kernel(table_ref, contrast_ref, image_ref, out_ref, held_real, held_imag):
    table = table_ref[...]
    count = image_ref.shape[0]
    for row in range(count):
        factor = contrast_ref[row : row + 1, :]
        factor = jnp.concatenate([factor, factor], axis=-1)
        weighted = (image_ref[row].astype(jnp.float32) * factor).astype(jnp.bfloat16)
        rows = pl.ds(row, ANGLES, stride=count)
        held_real[rows, :], held_imag[rows, :] = spectrum_of(weighted, table)
    shape = (ANGLES, count, CYCLES)
    out_ref[:, :, :CYCLES] = held_real[...].reshape(shape).astype(jnp.bfloat16)
    out_ref[:, :, CYCLES:] = held_imag[...].reshape(shape).astype(jnp.bfloat16)


def image_spectra(images, half, contrast_rows, table):
    particles = contrast_rows.shape[0] // 2
    count = 16
    skipped = half * particles // count
    return pl.pallas_call(
        spectra_kernel,
        grid=(particles // count,),
        in_specs=[
            pl.BlockSpec((2 * ANGLES, ANGLES), lambda i: (0, 0)),
            pl.BlockSpec((count, CYCLES), lambda i: (i + skipped, 0)),
            pl.BlockSpec((count, ANGLES, 2 * CYCLES), lambda i: (i + skipped, 0, 0)),
        ],
        out_specs=pl.BlockSpec((ANGLES, count, 2 * CYCLES), lambda i: (0, i, 0)),
        out_shape=jax.ShapeDtypeStruct((ANGLES, particles, 2 * CYCLES), jnp.bfloat16),
        scratch_shapes=[pltpu.VMEM((ANGLES * count, CYCLES), jnp.float32)] * 2,
        compiler_params=pltpu.CompilerParams(vmem_limit_bytes=56 * 1024 * 1024),
        cost_estimate=pl.CostEstimate(
            flops=particles * 4 * ANGLES * ANGLES * 2 * CYCLES,
            bytes_accessed=4 * particles * ANGLES * 2 * CYCLES,
            transcendentals=0,
        ),
    )(table, contrast_rows, images)


def pick_kernel(group_ref, roster_ref, source_ref, out_ref):
    for step in range(STEPS):
        holder = roster_ref[group_ref[0], step]
        value = source_ref[holder >> 4, step]
        for copy in range(out_ref.shape[0]):
            out_ref[copy, step] = value


def pick_far_kernel(group_ref, roster_ref, source_ref, out_ref, sems):
    copies = [
        pltpu.make_async_copy(
            source_ref.at[roster_ref[group_ref[0], step] & 15], out_ref.at[copy, step], sems.at[copy, step]
        )
        for step in range(STEPS)
        for copy in range(out_ref.shape[0])
    ]
    for copy in copies:
        copy.start()
    for copy in copies:
        copy.wait()


def pick_far(group, roster, source, copies):
    smem = pl.BlockSpec(memory_space=pltpu.SMEM)
    return pl.pallas_call(
        pick_far_kernel,
        in_specs=[smem, smem, pl.BlockSpec(memory_space=pltpu.VMEM)],
        out_specs=pl.BlockSpec(memory_space=pl.ANY),
        out_shape=jax.ShapeDtypeStruct((copies, STEPS, ANGLES, CYCLES), jnp.bfloat16),
        scratch_shapes=[pltpu.SemaphoreType.DMA((copies, STEPS))],
        compiler_params=pltpu.CompilerParams(vmem_limit_bytes=2 * 1024 * 1024),
    )(group, roster, source)


def pick(group, roster, source, copies):
    smem = pl.BlockSpec(memory_space=pltpu.SMEM)
    vmem = pl.BlockSpec(memory_space=pltpu.VMEM)
    return pl.pallas_call(
        pick_kernel,
        in_specs=[smem, smem, vmem],
        out_specs=vmem,
        out_shape=jax.ShapeDtypeStruct((copies, STEPS, ANGLES, CYCLES), jnp.bfloat16),
        compiler_params=pltpu.CompilerParams(vmem_limit_bytes=2 * 1024 * 1024),
    )(group, roster, source)


def score_kernel(
    core_ref,
    mine_ref,
    other_ref,
    early_ref,
    late_ref,
    low_ref,
    turn_ref,
    back_ref,
    square_ref,
    prior_ref,
    member_ref,
    keep_ref,
    send_ref,
    evidence_ref,
    ref_real,
    ref_imag,
    corr,
    scores,
    power,
    spectra_ref,
    sem,
):
    particles = spectra_ref.shape[1]
    depth, half = ANGLES // CHUNKS, particles // 2
    arriving = [
        pltpu.make_async_copy(
            source.at[pl.ds(n * depth, depth)],
            spectra_ref.at[pl.ds(n * depth, depth), pl.ds(k * half, half)],
            sem.at[n, k],
        )
        for n in range(CHUNKS)
        for k, source in enumerate((early_ref, late_ref))
    ]
    for copy in arriving:
        copy.start()
    first = core_ref[0] == 0
    table = low_ref[...]
    for c in range(CLS_GRP):
        mine, other = mine_ref[c], other_ref[c]
        polar = jnp.concatenate(
            [jnp.where(first, mine, other), jnp.where(first, other, mine)], axis=-1
        )
        real, imag = (
            part.astype(jnp.bfloat16).astype(jnp.float32) for part in spectrum_of(polar, table)
        )
        rows = pl.ds(c, ANGLES, stride=CLS_GRP)
        ref_real[rows, :], ref_imag[rows, :] = real, imag
        power[c : c + 1, :] = jnp.sum(real * real + imag * imag, axis=0, keepdims=True)
    square = square_ref[...]
    across = (((1,), (1,)), ((), ()))
    energy = 0.5 * lax.dot_general(
        power[...], square, across, precision=TOP_PRECISION, preferred_element_type=jnp.float32
    )
    member = member_ref[...]
    denom = jnp.dot(
        member, square, precision=TOP_PRECISION, preferred_element_type=jnp.float32
    )
    keep_ref[ANGLES] = denom
    send_ref[ANGLES] = denom
    for m in range(ANGLES):
        if m % depth == 0:
            for copy in arriving[m // depth * 2 : m // depth * 2 + 2]:
                copy.wait()
        rows = slice(m * CLS_GRP, (m + 1) * CLS_GRP)
        real, imag = ref_real[rows, :], ref_imag[rows, :]
        both = jnp.concatenate(
            [jnp.concatenate([real, -imag], axis=0), jnp.concatenate([imag, real], axis=0)],
            axis=-1,
        ).astype(jnp.bfloat16)
        corr[m * 2 * CLS_GRP : (m + 1) * 2 * CLS_GRP, :] = lax.dot_general(
            both, spectra_ref[m], across, preferred_element_type=jnp.float32
        )
    turn, prior = turn_ref[...], prior_ref[...]
    best = jnp.full((ANGLES, particles), -jnp.inf, jnp.float32)
    own = jnp.zeros((ANGLES, particles), jnp.float32)
    for c in range(0, CLS_GRP, 2):
        pair = [
            jnp.concatenate(
                [
                    corr[pl.ds(k, ANGLES, stride=2 * CLS_GRP), :],
                    corr[pl.ds(CLS_GRP + k, ANGLES, stride=2 * CLS_GRP), :],
                ],
                axis=0,
            )
            for k in (c, c + 1)
        ]
        rotated = jnp.dot(
            turn,
            jnp.concatenate(pair, axis=-1),
            precision=TOP_PRECISION,
            preferred_element_type=jnp.float32,
        )
        for k in range(2):
            value = rotated[:, k * particles : (k + 1) * particles]
            value = (value - energy[c + k : c + k + 1, :]) * (1.0 / ANGLES) + prior
            scores[c + k] = value
            best = jnp.maximum(best, value)
            own = own + jnp.where(member_ref[c + k : c + k + 1, :] > 0, value, 0.0)
    weight = jnp.exp(own - jnp.max(own, axis=0, keepdims=True))
    weight = weight / jnp.sum(weight, axis=0, keepdims=True)
    turned_back = jnp.dot(
        back_ref[...], weight, precision=TOP_PRECISION, preferred_element_type=jnp.float32
    )
    h_real = turned_back[:particles].T
    h_imag = turned_back[particles:].T
    top = jnp.max(best, axis=0, keepdims=True)
    total = jnp.zeros((ANGLES, particles), jnp.float32)
    for c in range(CLS_GRP):
        total = total + jnp.exp(scores[c] - top)
    evidence_ref[0:1, :] = top
    evidence_ref[1:2, :] = jnp.sum(total, axis=0, keepdims=True)
    chosen = member.astype(jnp.bfloat16)
    for m in range(ANGLES):
        x_real = spectra_ref[m, :, :CYCLES].astype(jnp.float32)
        x_imag = spectra_ref[m, :, CYCLES:].astype(jnp.float32)
        hr, hi = h_real[:, m : m + 1], h_imag[:, m : m + 1]
        aligned = jnp.concatenate(
            [x_real * hr - x_imag * hi, x_real * hi + x_imag * hr], axis=-1
        ).astype(jnp.bfloat16)
        sums = jnp.dot(chosen, aligned, preferred_element_type=jnp.float32)
        real_sum, imag_sum = sums[:, :CYCLES], sums[:, CYCLES:]
        keep_ref[m] = jnp.where(first, real_sum, imag_sum)
        send_ref[m] = jnp.where(first, imag_sum, real_sum)


def score(core, mine, other, early, late, low_table, turn, back, square, prior, member):
    particles = 2 * early.shape[1]
    sums = jax.ShapeDtypeStruct((ANGLES + 1, CLS_GRP, CYCLES), jnp.float32)
    evidence = jax.ShapeDtypeStruct((2, particles), jnp.float32)
    vmem = pl.BlockSpec(memory_space=pltpu.VMEM)
    return pl.pallas_call(
        score_kernel,
        in_specs=[pl.BlockSpec(memory_space=pltpu.SMEM), vmem, vmem]
        + [pl.BlockSpec(memory_space=pltpu.HBM)] * 2
        + [vmem] * 6,
        out_specs=(vmem, vmem, vmem),
        out_shape=(sums, sums, evidence),
        scratch_shapes=[
            pltpu.VMEM((ANGLES * CLS_GRP, CYCLES), jnp.float32),
            pltpu.VMEM((ANGLES * CLS_GRP, CYCLES), jnp.float32),
            pltpu.VMEM((ANGLES * 2 * CLS_GRP, particles), jnp.float32),
            pltpu.VMEM((CLS_GRP, ANGLES, particles), jnp.float32),
            pltpu.VMEM((CLS_GRP, CYCLES), jnp.float32),
            pltpu.VMEM((ANGLES, particles, 2 * CYCLES), jnp.bfloat16),
            pltpu.SemaphoreType.DMA((CHUNKS, 2)),
        ],
        compiler_params=pltpu.CompilerParams(vmem_limit_bytes=50 * 1024 * 1024),
    )(core, mine, other, early, late, low_table, turn, back, square, prior, member)


def pack_kernel(keep_ref, got_ref, out_ref):
    denom = keep_ref[ANGLES] + got_ref[ANGLES]
    high = denom.astype(jnp.bfloat16)
    low = (denom - high.astype(jnp.float32)).astype(jnp.bfloat16)
    for m in range(SHARES * ROWS):
        if m < ANGLES:
            value = (keep_ref[m] + got_ref[m]).astype(jnp.bfloat16)
        elif m < ANGLES + 2:
            value = (high, low)[m - ANGLES]
        else:
            value = jnp.zeros_like(high)
        out_ref[m // ROWS, m % ROWS] = value


def pack(keep, got):
    vmem = pl.BlockSpec(memory_space=pltpu.VMEM)
    return pl.pallas_call(
        pack_kernel,
        in_specs=[vmem, vmem],
        out_specs=vmem,
        out_shape=jax.ShapeDtypeStruct((SHARES, ROWS, CLS_GRP, CYCLES), jnp.bfloat16),
        compiler_params=pltpu.CompilerParams(vmem_limit_bytes=4 * 1024 * 1024),
    )(keep, got)


def rotation_prior(rotation_rows):
    counting = jnp.arange(ANGLES, dtype=jnp.int32)
    distance = jnp.abs(counting[None, :] - rotation_rows[:, None])
    distance = jnp.minimum(distance, ANGLES - distance).astype(jnp.float32)
    return -0.5 * (distance / SIGMA_ROT) ** 2


def halve_kernel(blocks_ref, out_ref):
    for half in range(2):
        out_ref[:, half] = blocks_ref[:, :, half * CYCLES : (half + 1) * CYCLES]


def halve(blocks):
    count = 4
    return pl.pallas_call(
        halve_kernel,
        grid=(BLOCK // count,),
        in_specs=[pl.BlockSpec((count, ANGLES, 2 * CYCLES), lambda i: (i, 0, 0))],
        out_specs=pl.BlockSpec((count, 2, ANGLES, CYCLES), lambda i: (i, 0, 0, 0)),
        out_shape=jax.ShapeDtypeStruct((BLOCK, 2, ANGLES, CYCLES), jnp.bfloat16),
        compiler_params=pltpu.CompilerParams(vmem_limit_bytes=60 * 1024 * 1024),
    )(blocks)


def route_kernel(share_ref, place_ref, got_ref, out_ref):
    total = got_ref[0].astype(jnp.float32)
    for peer in range(1, SHARES):
        total = total + got_ref[peer].astype(jnp.float32)
    start = DENOM_ROW * CLS_GRP
    first, second = total[start : start + CLS_GRP], total[start + CLS_GRP : start + 2 * CLS_GRP]
    denom = first + second
    high = denom.astype(jnp.bfloat16).astype(jnp.float32)
    has_denom = share_ref[0] == DENOM_SHARE
    empty = jnp.zeros((CYCLES - ROWS * CLS_GRP, CYCLES), jnp.float32)
    share = jnp.concatenate(
        [
            total[:start],
            jnp.where(has_denom, high, first),
            jnp.where(has_denom, denom - high, second),
            total[start + 2 * CLS_GRP :],
            empty,
        ],
        axis=0,
    ).astype(jnp.bfloat16)
    place = place_ref[...]
    line = lax.broadcasted_iota(jnp.int32, (SLOT_ROWS, CYCLES), 0)
    line = (line // OWN_MAX) * 1024 + line % OWN_MAX - place
    for owner in range(0, 64, 8):
        chosen = jnp.concatenate(
            [jnp.where(line == -OWN_MAX * (owner + k), 1.0, 0.0) for k in range(8)], axis=0
        ).astype(jnp.bfloat16)
        out_ref[owner * SLOT_ROWS : (owner + 8) * SLOT_ROWS, :] = jnp.dot(
            chosen, share, preferred_element_type=jnp.float32
        ).astype(jnp.bfloat16)


def route(share, place, got):
    vmem = pl.BlockSpec(memory_space=pltpu.VMEM)
    return pl.pallas_call(
        route_kernel,
        in_specs=[pl.BlockSpec(memory_space=pltpu.SMEM), vmem, vmem],
        out_specs=vmem,
        out_shape=jax.ShapeDtypeStruct((64 * SLOT_ROWS, CYCLES), jnp.bfloat16),
        compiler_params=pltpu.CompilerParams(vmem_limit_bytes=6 * 1024 * 1024),
    )(share, place, got)


def finish_kernel(table_ref, got_ref, out_ref, held):
    total = got_ref[0].astype(jnp.float32) + got_ref[1].astype(jnp.float32)
    held[...] = total
    at = DENOM_SHARE * 2 * SLOT_ROWS + DENOM_ROW * OWN_MAX
    denom = total[at : at + OWN_MAX] + total[at + OWN_MAX : at + 2 * OWN_MAX]
    scale = (1.0 / ANGLES) / (denom + TAU)
    for slot in range(0, OWN_MAX, 2):
        pair = [
            held[pl.ds(k, held.shape[0] // OWN_MAX, stride=OWN_MAX), :] * scale[k : k + 1]
            for k in (slot, slot + 1)
        ]
        polar = jnp.dot(
            table_ref[...],
            jnp.concatenate(pair, axis=-1),
            precision=TOP_PRECISION,
            preferred_element_type=jnp.float32,
        ).astype(jnp.bfloat16)
        for k in range(2):
            columns = slice(k * CYCLES, (k + 1) * CYCLES)
            out_ref[slot + k, :, :CYCLES] = polar[:ANGLES, columns]
            out_ref[slot + k, :, CYCLES:] = polar[ANGLES:, columns]


def finish(table, got):
    vmem = pl.BlockSpec(memory_space=pltpu.VMEM)
    return pl.pallas_call(
        finish_kernel,
        in_specs=[vmem, vmem],
        out_specs=vmem,
        out_shape=jax.ShapeDtypeStruct((OWN_MAX, ANGLES, 2 * CYCLES), jnp.bfloat16),
        scratch_shapes=[pltpu.VMEM((2 * SHARES * SLOT_ROWS, CYCLES), jnp.float32)],
        compiler_params=pltpu.CompilerParams(vmem_limit_bytes=6 * 1024 * 1024),
    )(table, got)


def finish_table(cosine_table, sine_table):
    harmonic = np.arange(SHARES)[:, None] * ROWS + np.arange(SLOT_ROWS // OWN_MAX)
    filled = (np.arange(SLOT_ROWS // OWN_MAX) < ROWS) & (harmonic < ANGLES)

    def laid(table):
        return np.where(filled, table[:, harmonic % ANGLES], np.float32(0.0))[:, :, None]

    cosine, sine = laid(cosine_table), laid(sine_table)
    real = np.concatenate([cosine, -sine], axis=2).reshape(ANGLES, -1)
    imag = np.concatenate([sine, cosine], axis=2).reshape(ANGLES, -1)
    return np.concatenate([real, imag])


def fetch(blocks, group, roster, images, contrast_rows, table, small):
    halves = halve(blocks).reshape(BLOCK * 2, ANGLES, CYCLES)
    sliced = lax.all_to_all(halves, ("wide_1", "wide_2"), 0, 0, tiled=True)
    early = image_spectra(images, 0, contrast_rows, table)
    sliced, early, later = lax.optimization_barrier((sliced, early, contrast_rows))
    picked = pick_far(group, roster, sliced, 4)
    planes = lax.all_to_all(picked, HIGH, 0, 0, tiled=True)
    late = image_spectra(images, 1, later, table)
    planes, late, small = lax.optimization_barrier((planes, late, small))
    picked = pick(group, roster, planes, 8)
    mine = lax.all_to_all(picked, "wide_1", 0, 0, tiled=True).reshape(CLS_GRP, ANGLES, CYCLES)
    return mine, early, late, small


def exchanged_evidence(pair, bit):
    got = lax.ppermute(pair, "narrow", [(k, k ^ bit) for k in range(8)])
    top = jnp.maximum(pair[:1], got[:1])
    total = pair[1:] * jnp.exp(pair[:1] - top) + got[1:] * jnp.exp(got[:1] - top)
    return jnp.concatenate([top, total])


def per_device(images, defocus, class_index, rotation_index, owner_map, roster, ref_store):
    class_group = lax.axis_index("narrow")
    core = lax.axis_index("wide_2")
    cosine_table, sine_table = angle_tables(ANGLES)
    leading_class = class_group * CLS_GRP
    arrival = jnp.arange(CLS_GRP, dtype=jnp.int32)
    within = arrival % STEPS * BLOCK + arrival // STEPS
    class_ids = leading_class + within
    mine_group = jnp.arange(8, dtype=jnp.int32)[:, None] == class_group

    low_table = np.concatenate([cosine_table, sine_table]).astype(jnp.bfloat16)
    turn = np.concatenate([cosine_table, -sine_table], axis=-1)
    filled = ((0, CYCLES - ANGLES), (0, 0))
    back = np.concatenate([np.pad(cosine_table, filled), np.pad(sine_table, filled)])
    contrast_rows = contrast(defocus)
    square = contrast_rows * contrast_rows
    prior = rotation_prior(rotation_index).T
    member = (class_index[None, :] == class_ids[:, None]).astype(jnp.float32)
    def places(owner_map):
        owners = jnp.sum(jnp.where(mine_group, owner_map.reshape(8, CLS_GRP), 0), axis=0)
        owners = owners.reshape(STEPS, BLOCK).T.reshape(CLS_GRP)
        same = owners[:, None] == owners[None, :]
        ranking = jnp.sum(same & (within[None, :] < within[:, None]), axis=1)
        place = owners * OWN_MAX + ranking
        place = jnp.arange(ROWS, dtype=jnp.int32)[:, None] * 1024 + place[None, :]
        return jnp.pad(
            place.reshape(1, ROWS * CLS_GRP),
            ((0, 0), (0, CYCLES - ROWS * CLS_GRP)),
            constant_values=2**20,
        )

    table = finish_table(cosine_table, sine_table)
    small = (square, prior, member)

    mine, early, late, small = fetch(
        ref_store[0, 0], class_group.reshape(1), roster, images, contrast_rows, low_table, small
    )
    square, prior, member = small
    other = swapped(mine)
    keep, send, evidence = score(
        core.reshape(1), mine, other, early, late, low_table, turn, back, square, prior, member
    )
    send, owner_map = lax.optimization_barrier((send, owner_map))
    got, place = lax.optimization_barrier((swapped(send), places(owner_map)))
    share = pack(keep, got)
    share = share.reshape(SHARES, ROWS * CLS_GRP, CYCLES)
    share, evidence = lax.optimization_barrier((share, evidence))
    share = lax.all_to_all(share, ("wide_low", "wide_1"), 0, 0, tiled=True)
    for bit in (2, 4):
        evidence = exchanged_evidence(evidence, bit)
    share, evidence = lax.optimization_barrier((share, evidence))
    own_share = lax.axis_index(("wide_low", "wide_1"))
    sent = route(own_share.reshape(1), place, share).reshape(64, SLOT_ROWS, CYCLES)
    sent, evidence = lax.optimization_barrier((sent, evidence))
    got = lax.all_to_all(sent, WIDE, 0, 0, tiled=True)
    evidence = exchanged_evidence(evidence, 1)
    log_evidence = evidence[0] + jnp.log(evidence[1])
    got = got.reshape(2, 2 * SHARES * SLOT_ROWS, CYCLES)
    new_references = finish(table, got).reshape(1, 1, OWN_MAX, ANGLES, 2 * CYCLES)
    return (new_references, log_evidence)


def solution(mesh):
    split = Mesh(
        mesh.devices.reshape(2, 2, 8, 2, mesh.shape["narrow"]),
        (*WIDE, "narrow"),
    )
    placed = (
        P(WIDE, None, None),
        P(WIDE),
        P(WIDE),
        P(WIDE),
        P(),
        P(),
        P(WIDE, "narrow", None, None, None),
    )
    return jax.shard_map(
        per_device,
        mesh=split,
        in_specs=placed,
        out_specs=(P(WIDE, "narrow", None, None, None), P(WIDE)),
        check_vma=False,
    )
```

```python
import math

import jax
import jax.numpy as jnp
import numpy as np
from jax import lax
from jax.experimental import pallas as pl
from jax.experimental.pallas import tpu as pltpu
from jax.sharding import Mesh
from jax.sharding import PartitionSpec as P

CYCLES = 128
ANGLES = 72
STEPS = 3
BLOCK = 8
OWN_MAX = 4
CLS_GRP = 24
SIGMA_ROT = 8
SHARES = 16
ROWS = 5
SLOT_ROWS = 24
DENOM_SHARE, DENOM_ROW = divmod(ANGLES, ROWS)
CHUNKS = 4
HIGH = ("wide_high", "wide_low")
WIDE = (*HIGH, "wide_1", "wide_2")


TAU = 1.0
CONTRAST = 0.1
TOP_PRECISION = lax.Precision.HIGHEST


def swapped(x):
    return lax.ppermute(x, "wide_2", [(0, 1), (1, 0)])


def angle_tables(length):
    counting = np.arange(length)
    products = counting[:, None] * counting[None, :] % length
    phase_angle = products.astype(np.float32) * np.float32(2.0 * math.pi / length)
    return (np.cos(phase_angle), np.sin(phase_angle))


def contrast(defocus_rows):
    cycle_freq = (jnp.arange(CYCLES, dtype=jnp.float32) + 1.0) / CYCLES
    phase_angle = 8.0 * math.pi * defocus_rows[:, None] * cycle_freq[None, :] ** 2
    return -jnp.sin(phase_angle) - CONTRAST * jnp.cos(phase_angle)


def spectrum_of(polar, table):
    both = jnp.dot(table, polar, preferred_element_type=jnp.float32)
    cos_part, sin_part = both[:ANGLES], both[ANGLES:]
    real_part = cos_part[:, :CYCLES] + sin_part[:, CYCLES:]
    imag_part = cos_part[:, CYCLES:] - sin_part[:, :CYCLES]
    return real_part, imag_part


def spectra_kernel(table_ref, contrast_ref, image_ref, out_ref, held_real, held_imag):
    table = table_ref[...]
    count = image_ref.shape[0]
    for row in range(count):
        factor = contrast_ref[row : row + 1, :]
        factor = jnp.concatenate([factor, factor], axis=-1)
        weighted = (image_ref[row].astype(jnp.float32) * factor).astype(jnp.bfloat16)
        rows = pl.ds(row, ANGLES, stride=count)
        held_real[rows, :], held_imag[rows, :] = spectrum_of(weighted, table)
    shape = (ANGLES, count, CYCLES)
    out_ref[:, :, :CYCLES] = held_real[...].reshape(shape).astype(jnp.bfloat16)
    out_ref[:, :, CYCLES:] = held_imag[...].reshape(shape).astype(jnp.bfloat16)


def image_spectra(images, half, contrast_rows, table):
    particles = contrast_rows.shape[0] // 2
    count = 16
    skipped = half * particles // count
    return pl.pallas_call(
        spectra_kernel,
        grid=(particles // count,),
        in_specs=[
            pl.BlockSpec((2 * ANGLES, ANGLES), lambda i: (0, 0)),
            pl.BlockSpec((count, CYCLES), lambda i: (i + skipped, 0)),
            pl.BlockSpec((count, ANGLES, 2 * CYCLES), lambda i: (i + skipped, 0, 0)),
        ],
        out_specs=pl.BlockSpec((ANGLES, count, 2 * CYCLES), lambda i: (0, i, 0)),
        out_shape=jax.ShapeDtypeStruct((ANGLES, particles, 2 * CYCLES), jnp.bfloat16),
        scratch_shapes=[pltpu.VMEM((ANGLES * count, CYCLES), jnp.float32)] * 2,
        compiler_params=pltpu.CompilerParams(vmem_limit_bytes=56 * 1024 * 1024),
        cost_estimate=pl.CostEstimate(
            flops=particles * 4 * ANGLES * ANGLES * 2 * CYCLES,
            bytes_accessed=4 * particles * ANGLES * 2 * CYCLES,
            transcendentals=0,
        ),
    )(table, contrast_rows, images)


def pick_kernel(group_ref, roster_ref, source_ref, out_ref):
    planes = source_ref.shape[1] == STEPS
    for step in range(STEPS):
        holder = roster_ref[group_ref[0], step]
        value = source_ref[holder >> 4, step] if planes else source_ref[holder & 15, 0]
        for copy in range(out_ref.shape[0]):
            out_ref[copy, step] = value


def pick(group, roster, source, copies):
    smem = pl.BlockSpec(memory_space=pltpu.SMEM)
    vmem = pl.BlockSpec(memory_space=pltpu.VMEM)
    return pl.pallas_call(
        pick_kernel,
        in_specs=[smem, smem, vmem],
        out_specs=vmem,
        out_shape=jax.ShapeDtypeStruct((copies, STEPS, ANGLES, CYCLES), jnp.bfloat16),
        compiler_params=pltpu.CompilerParams(vmem_limit_bytes=2 * 1024 * 1024),
    )(group, roster, source)


def score_kernel(
    core_ref,
    mine_ref,
    other_ref,
    early_ref,
    late_ref,
    low_ref,
    turn_ref,
    back_ref,
    square_ref,
    prior_ref,
    member_ref,
    keep_ref,
    send_ref,
    evidence_ref,
    ref_real,
    ref_imag,
    corr,
    scores,
    power,
    spectra_ref,
    sem,
):
    particles = spectra_ref.shape[1]
    depth, half = ANGLES // CHUNKS, particles // 2
    arriving = [
        pltpu.make_async_copy(
            source.at[pl.ds(n * depth, depth)],
            spectra_ref.at[pl.ds(n * depth, depth), pl.ds(k * half, half)],
            sem.at[n, k],
        )
        for n in range(CHUNKS)
        for k, source in enumerate((early_ref, late_ref))
    ]
    for copy in arriving:
        copy.start()
    first = core_ref[0] == 0
    table = low_ref[...]
    for c in range(CLS_GRP):
        mine, other = mine_ref[c], other_ref[c]
        polar = jnp.concatenate(
            [jnp.where(first, mine, other), jnp.where(first, other, mine)], axis=-1
        )
        real, imag = (
            part.astype(jnp.bfloat16).astype(jnp.float32) for part in spectrum_of(polar, table)
        )
        rows = pl.ds(c, ANGLES, stride=CLS_GRP)
        ref_real[rows, :], ref_imag[rows, :] = real, imag
        power[c : c + 1, :] = jnp.sum(real * real + imag * imag, axis=0, keepdims=True)
    square = square_ref[...]
    across = (((1,), (1,)), ((), ()))
    energy = 0.5 * lax.dot_general(
        power[...], square, across, precision=TOP_PRECISION, preferred_element_type=jnp.float32
    )
    for m in range(ANGLES):
        if m % depth == 0:
            for copy in arriving[m // depth * 2 : m // depth * 2 + 2]:
                copy.wait()
        rows = slice(m * CLS_GRP, (m + 1) * CLS_GRP)
        real, imag = ref_real[rows, :], ref_imag[rows, :]
        both = jnp.concatenate(
            [jnp.concatenate([real, -imag], axis=0), jnp.concatenate([imag, real], axis=0)],
            axis=-1,
        ).astype(jnp.bfloat16)
        corr[m * 2 * CLS_GRP : (m + 1) * 2 * CLS_GRP, :] = lax.dot_general(
            both, spectra_ref[m], across, preferred_element_type=jnp.float32
        )
    turn, prior = turn_ref[...], prior_ref[...]
    best = jnp.full((ANGLES, particles), -jnp.inf, jnp.float32)
    own = jnp.zeros((ANGLES, particles), jnp.float32)
    for c in range(0, CLS_GRP, 2):
        pair = [
            jnp.concatenate(
                [
                    corr[pl.ds(k, ANGLES, stride=2 * CLS_GRP), :],
                    corr[pl.ds(CLS_GRP + k, ANGLES, stride=2 * CLS_GRP), :],
                ],
                axis=0,
            )
            for k in (c, c + 1)
        ]
        rotated = jnp.dot(
            turn,
            jnp.concatenate(pair, axis=-1),
            precision=TOP_PRECISION,
            preferred_element_type=jnp.float32,
        )
        for k in range(2):
            value = rotated[:, k * particles : (k + 1) * particles]
            value = (value - energy[c + k : c + k + 1, :]) * (1.0 / ANGLES) + prior
            scores[c + k] = value
            best = jnp.maximum(best, value)
            own = own + jnp.where(member_ref[c + k : c + k + 1, :] > 0, value, 0.0)
    top = jnp.max(best, axis=0, keepdims=True)
    total = jnp.zeros((ANGLES, particles), jnp.float32)
    for c in range(CLS_GRP):
        total = total + jnp.exp(scores[c] - top)
    evidence_ref[0:1, :] = top
    evidence_ref[1:2, :] = jnp.sum(total, axis=0, keepdims=True)
    weight = jnp.exp(own - jnp.max(own, axis=0, keepdims=True))
    weight = weight / jnp.sum(weight, axis=0, keepdims=True)
    turned_back = jnp.dot(
        back_ref[...], weight, precision=TOP_PRECISION, preferred_element_type=jnp.float32
    )
    h_real = turned_back[:particles].T
    h_imag = turned_back[particles:].T
    member = member_ref[...]
    chosen = member.astype(jnp.bfloat16)
    for m in range(ANGLES):
        x_real = spectra_ref[m, :, :CYCLES].astype(jnp.float32)
        x_imag = spectra_ref[m, :, CYCLES:].astype(jnp.float32)
        hr, hi = h_real[:, m : m + 1], h_imag[:, m : m + 1]
        aligned = jnp.concatenate(
            [x_real * hr - x_imag * hi, x_real * hi + x_imag * hr], axis=-1
        ).astype(jnp.bfloat16)
        sums = jnp.dot(chosen, aligned, preferred_element_type=jnp.float32)
        real_sum, imag_sum = sums[:, :CYCLES], sums[:, CYCLES:]
        keep_ref[m] = jnp.where(first, real_sum, imag_sum)
        send_ref[m] = jnp.where(first, imag_sum, real_sum)
    denom = jnp.dot(
        member, square, precision=TOP_PRECISION, preferred_element_type=jnp.float32
    )
    keep_ref[ANGLES] = denom
    send_ref[ANGLES] = denom


def score(core, mine, other, early, late, low_table, turn, back, square, prior, member):
    particles = 2 * early.shape[1]
    sums = jax.ShapeDtypeStruct((ANGLES + 1, CLS_GRP, CYCLES), jnp.float32)
    evidence = jax.ShapeDtypeStruct((2, particles), jnp.float32)
    vmem = pl.BlockSpec(memory_space=pltpu.VMEM)
    return pl.pallas_call(
        score_kernel,
        in_specs=[pl.BlockSpec(memory_space=pltpu.SMEM), vmem, vmem]
        + [pl.BlockSpec(memory_space=pltpu.HBM)] * 2
        + [vmem] * 6,
        out_specs=(vmem, vmem, vmem),
        out_shape=(sums, sums, evidence),
        scratch_shapes=[
            pltpu.VMEM((ANGLES * CLS_GRP, CYCLES), jnp.float32),
            pltpu.VMEM((ANGLES * CLS_GRP, CYCLES), jnp.float32),
            pltpu.VMEM((ANGLES * 2 * CLS_GRP, particles), jnp.float32),
            pltpu.VMEM((CLS_GRP, ANGLES, particles), jnp.float32),
            pltpu.VMEM((CLS_GRP, CYCLES), jnp.float32),
            pltpu.VMEM((ANGLES, particles, 2 * CYCLES), jnp.bfloat16),
            pltpu.SemaphoreType.DMA((CHUNKS, 2)),
        ],
        compiler_params=pltpu.CompilerParams(vmem_limit_bytes=50 * 1024 * 1024),
    )(core, mine, other, early, late, low_table, turn, back, square, prior, member)


def pack_kernel(keep_ref, got_ref, out_ref):
    denom = keep_ref[ANGLES] + got_ref[ANGLES]
    high = denom.astype(jnp.bfloat16)
    low = (denom - high.astype(jnp.float32)).astype(jnp.bfloat16)
    for m in range(SHARES * ROWS):
        if m < ANGLES:
            value = (keep_ref[m] + got_ref[m]).astype(jnp.bfloat16)
        elif m < ANGLES + 2:
            value = (high, low)[m - ANGLES]
        else:
            value = jnp.zeros_like(high)
        out_ref[m // ROWS, m % ROWS] = value


def pack(keep, got):
    vmem = pl.BlockSpec(memory_space=pltpu.VMEM)
    return pl.pallas_call(
        pack_kernel,
        in_specs=[vmem, vmem],
        out_specs=vmem,
        out_shape=jax.ShapeDtypeStruct((SHARES, ROWS, CLS_GRP, CYCLES), jnp.bfloat16),
        compiler_params=pltpu.CompilerParams(vmem_limit_bytes=4 * 1024 * 1024),
    )(keep, got)


def rotation_prior(rotation_rows):
    counting = jnp.arange(ANGLES, dtype=jnp.int32)
    distance = jnp.abs(counting[None, :] - rotation_rows[:, None])
    distance = jnp.minimum(distance, ANGLES - distance).astype(jnp.float32)
    return -0.5 * (distance / SIGMA_ROT) ** 2


def halve_kernel(blocks_ref, out_ref):
    for half in range(2):
        out_ref[:, half] = blocks_ref[:, :, half * CYCLES : (half + 1) * CYCLES]


def halve(blocks):
    count = 4
    return pl.pallas_call(
        halve_kernel,
        grid=(BLOCK // count,),
        in_specs=[pl.BlockSpec((count, ANGLES, 2 * CYCLES), lambda i: (i, 0, 0))],
        out_specs=pl.BlockSpec((count, 2, ANGLES, CYCLES), lambda i: (i, 0, 0, 0)),
        out_shape=jax.ShapeDtypeStruct((BLOCK, 2, ANGLES, CYCLES), jnp.bfloat16),
        compiler_params=pltpu.CompilerParams(vmem_limit_bytes=60 * 1024 * 1024),
    )(blocks)


def route_kernel(share_ref, place_ref, got_ref, out_ref):
    total = got_ref[0].astype(jnp.float32)
    for peer in range(1, SHARES):
        total = total + got_ref[peer].astype(jnp.float32)
    start = DENOM_ROW * CLS_GRP
    first, second = total[start : start + CLS_GRP], total[start + CLS_GRP : start + 2 * CLS_GRP]
    denom = first + second
    high = denom.astype(jnp.bfloat16).astype(jnp.float32)
    has_denom = share_ref[0] == DENOM_SHARE
    empty = jnp.zeros((CYCLES - ROWS * CLS_GRP, CYCLES), jnp.float32)
    share = jnp.concatenate(
        [
            total[:start],
            jnp.where(has_denom, high, first),
            jnp.where(has_denom, denom - high, second),
            total[start + 2 * CLS_GRP :],
            empty,
        ],
        axis=0,
    ).astype(jnp.bfloat16)
    place = place_ref[...]
    line = lax.broadcasted_iota(jnp.int32, (SLOT_ROWS, CYCLES), 0)
    line = (line // OWN_MAX) * 1024 + line % OWN_MAX - place
    for owner in range(0, 64, 8):
        chosen = jnp.concatenate(
            [jnp.where(line == -OWN_MAX * (owner + k), 1.0, 0.0) for k in range(8)], axis=0
        ).astype(jnp.bfloat16)
        out_ref[owner * SLOT_ROWS : (owner + 8) * SLOT_ROWS, :] = jnp.dot(
            chosen, share, preferred_element_type=jnp.float32
        ).astype(jnp.bfloat16)


def route(share, place, got):
    vmem = pl.BlockSpec(memory_space=pltpu.VMEM)
    return pl.pallas_call(
        route_kernel,
        in_specs=[pl.BlockSpec(memory_space=pltpu.SMEM), vmem, vmem],
        out_specs=vmem,
        out_shape=jax.ShapeDtypeStruct((64 * SLOT_ROWS, CYCLES), jnp.bfloat16),
        compiler_params=pltpu.CompilerParams(vmem_limit_bytes=6 * 1024 * 1024),
    )(share, place, got)


def finish_kernel(table_ref, got_ref, out_ref, held):
    total = got_ref[0].astype(jnp.float32) + got_ref[1].astype(jnp.float32)
    held[...] = total
    at = DENOM_SHARE * 2 * SLOT_ROWS + DENOM_ROW * OWN_MAX
    denom = total[at : at + OWN_MAX] + total[at + OWN_MAX : at + 2 * OWN_MAX]
    scale = (1.0 / ANGLES) / (denom + TAU)
    for slot in range(0, OWN_MAX, 2):
        pair = [
            held[pl.ds(k, held.shape[0] // OWN_MAX, stride=OWN_MAX), :] * scale[k : k + 1]
            for k in (slot, slot + 1)
        ]
        polar = jnp.dot(
            table_ref[...],
            jnp.concatenate(pair, axis=-1),
            precision=TOP_PRECISION,
            preferred_element_type=jnp.float32,
        ).astype(jnp.bfloat16)
        for k in range(2):
            columns = slice(k * CYCLES, (k + 1) * CYCLES)
            out_ref[slot + k, :, :CYCLES] = polar[:ANGLES, columns]
            out_ref[slot + k, :, CYCLES:] = polar[ANGLES:, columns]


def finish(table, got):
    vmem = pl.BlockSpec(memory_space=pltpu.VMEM)
    return pl.pallas_call(
        finish_kernel,
        in_specs=[vmem, vmem],
        out_specs=vmem,
        out_shape=jax.ShapeDtypeStruct((OWN_MAX, ANGLES, 2 * CYCLES), jnp.bfloat16),
        scratch_shapes=[pltpu.VMEM((2 * SHARES * SLOT_ROWS, CYCLES), jnp.float32)],
        compiler_params=pltpu.CompilerParams(vmem_limit_bytes=6 * 1024 * 1024),
    )(table, got)


def finish_table(cosine_table, sine_table):
    harmonic = np.arange(SHARES)[:, None] * ROWS + np.arange(SLOT_ROWS // OWN_MAX)
    filled = (np.arange(SLOT_ROWS // OWN_MAX) < ROWS) & (harmonic < ANGLES)

    def laid(table):
        return np.where(filled, table[:, harmonic % ANGLES], np.float32(0.0))[:, :, None]

    cosine, sine = laid(cosine_table), laid(sine_table)
    real = np.concatenate([cosine, -sine], axis=2).reshape(ANGLES, -1)
    imag = np.concatenate([sine, cosine], axis=2).reshape(ANGLES, -1)
    return np.concatenate([real, imag])


def fetch(blocks, group, roster, images, contrast_rows, table, small):
    halves = halve(blocks).reshape(BLOCK * 2, ANGLES, CYCLES)
    sliced = lax.all_to_all(halves, ("wide_1", "wide_2"), 0, 0, tiled=True)
    early = image_spectra(images, 0, contrast_rows, table)
    sliced, early, later = lax.optimization_barrier((sliced, early, contrast_rows))
    picked = pick(group, roster, sliced[:, None], 4)
    planes = lax.all_to_all(picked, HIGH, 0, 0, tiled=True)
    late = image_spectra(images, 1, later, table)
    planes, late, small = lax.optimization_barrier((planes, late, small))
    picked = pick(group, roster, planes, 8)
    mine = lax.all_to_all(picked, "wide_1", 0, 0, tiled=True).reshape(CLS_GRP, ANGLES, CYCLES)
    return mine, early, late, small


def exchanged_evidence(pair, bit):
    got = lax.ppermute(pair, "narrow", [(k, k ^ bit) for k in range(8)])
    top = jnp.maximum(pair[:1], got[:1])
    total = pair[1:] * jnp.exp(pair[:1] - top) + got[1:] * jnp.exp(got[:1] - top)
    return jnp.concatenate([top, total])


def per_device(images, defocus, class_index, rotation_index, owner_map, roster, ref_store):
    class_group = lax.axis_index("narrow")
    core = lax.axis_index("wide_2")
    cosine_table, sine_table = angle_tables(ANGLES)
    leading_class = class_group * CLS_GRP
    arrival = jnp.arange(CLS_GRP, dtype=jnp.int32)
    within = arrival % STEPS * BLOCK + arrival // STEPS
    class_ids = leading_class + within
    mine_group = jnp.arange(8, dtype=jnp.int32)[:, None] == class_group

    low_table = np.concatenate([cosine_table, sine_table]).astype(jnp.bfloat16)
    turn = np.concatenate([cosine_table, -sine_table], axis=-1)
    filled = ((0, CYCLES - ANGLES), (0, 0))
    back = np.concatenate([np.pad(cosine_table, filled), np.pad(sine_table, filled)])
    contrast_rows = contrast(defocus)
    square = contrast_rows * contrast_rows
    prior = rotation_prior(rotation_index).T
    member = (class_index[None, :] == class_ids[:, None]).astype(jnp.float32)
    def places(owner_map):
        owners = jnp.sum(jnp.where(mine_group, owner_map.reshape(8, CLS_GRP), 0), axis=0)
        owners = owners.reshape(STEPS, BLOCK).T.reshape(CLS_GRP)
        same = owners[:, None] == owners[None, :]
        ranking = jnp.sum(same & (within[None, :] < within[:, None]), axis=1)
        place = owners * OWN_MAX + ranking
        place = jnp.arange(ROWS, dtype=jnp.int32)[:, None] * 1024 + place[None, :]
        return jnp.pad(
            place.reshape(1, ROWS * CLS_GRP),
            ((0, 0), (0, CYCLES - ROWS * CLS_GRP)),
            constant_values=2**20,
        )

    table = finish_table(cosine_table, sine_table)
    small = (square, prior, member)

    mine, early, late, small = fetch(
        ref_store[0, 0], class_group.reshape(1), roster, images, contrast_rows, low_table, small
    )
    square, prior, member = small
    other = swapped(mine)
    keep, send, evidence = score(
        core.reshape(1), mine, other, early, late, low_table, turn, back, square, prior, member
    )
    send, owner_map = lax.optimization_barrier((send, owner_map))
    got, place = lax.optimization_barrier((swapped(send), places(owner_map)))
    share = pack(keep, got)
    share = share.reshape(SHARES, ROWS * CLS_GRP, CYCLES)
    share, evidence = lax.optimization_barrier((share, evidence))
    share = lax.all_to_all(share, ("wide_low", "wide_1"), 0, 0, tiled=True)
    for bit in (2,):
        evidence = exchanged_evidence(evidence, bit)
    share, evidence = lax.optimization_barrier((share, evidence))
    own_share = lax.axis_index(("wide_low", "wide_1"))
    sent = route(own_share.reshape(1), place, share).reshape(64, SLOT_ROWS, CYCLES)
    sent, evidence = lax.optimization_barrier((sent, evidence))
    got = lax.all_to_all(sent, WIDE, 0, 0, tiled=True)
    evidence = exchanged_evidence(exchanged_evidence(evidence, 4), 1)
    log_evidence = evidence[0] + jnp.log(evidence[1])
    got = got.reshape(2, 2 * SHARES * SLOT_ROWS, CYCLES)
    new_references = finish(table, got).reshape(1, 1, OWN_MAX, ANGLES, 2 * CYCLES)
    return (new_references, log_evidence)


def solution(mesh):
    split = Mesh(
        mesh.devices.reshape(2, 2, 8, 2, mesh.shape["narrow"]),
        (*WIDE, "narrow"),
    )
    placed = (
        P(WIDE, None, None),
        P(WIDE),
        P(WIDE),
        P(WIDE),
        P(),
        P(),
        P(WIDE, "narrow", None, None, None),
    )
    return jax.shard_map(
        per_device,
        mesh=split,
        in_specs=placed,
        out_specs=(P(WIDE, "narrow", None, None, None), P(WIDE)),
        check_vma=False,
    )
```

```python
import math

import jax
import jax.numpy as jnp
import numpy as np
from jax import lax
from jax.experimental import pallas as pl
from jax.experimental.pallas import tpu as pltpu
from jax.sharding import Mesh
from jax.sharding import PartitionSpec as P

CYCLES = 128
ANGLES = 72
STEPS = 3
BLOCK = 8
OWN_MAX = 4
CLS_GRP = 24
SIGMA_ROT = 8
SHARES = 16
ROWS = 5
SLOT_ROWS = 24
DENOM_SHARE, DENOM_ROW = divmod(ANGLES, ROWS)
CHUNKS = 4
HIGH = ("wide_high", "wide_low")
WIDE = (*HIGH, "wide_1", "wide_2")


TAU = 1.0
CONTRAST = 0.1
TOP_PRECISION = lax.Precision.HIGHEST


def swapped(x):
    return lax.ppermute(x, "wide_2", [(0, 1), (1, 0)])


def angle_tables(length):
    counting = np.arange(length)
    products = counting[:, None] * counting[None, :] % length
    phase_angle = products.astype(np.float32) * np.float32(2.0 * math.pi / length)
    return (np.cos(phase_angle), np.sin(phase_angle))


def contrast(defocus_rows):
    cycle_freq = (jnp.arange(CYCLES, dtype=jnp.float32) + 1.0) / CYCLES
    phase_angle = 8.0 * math.pi * defocus_rows[:, None] * cycle_freq[None, :] ** 2
    return -jnp.sin(phase_angle) - CONTRAST * jnp.cos(phase_angle)


def spectrum_of(polar, table):
    both = jnp.dot(table, polar, preferred_element_type=jnp.float32)
    cos_part, sin_part = both[:ANGLES], both[ANGLES:]
    real_part = cos_part[:, :CYCLES] + sin_part[:, CYCLES:]
    imag_part = cos_part[:, CYCLES:] - sin_part[:, :CYCLES]
    return real_part, imag_part


def spectra_kernel(table_ref, contrast_ref, image_ref, out_ref, held_real, held_imag):
    table = table_ref[...]
    count = image_ref.shape[0]
    for row in range(count):
        factor = contrast_ref[row : row + 1, :]
        factor = jnp.concatenate([factor, factor], axis=-1)
        weighted = (image_ref[row].astype(jnp.float32) * factor).astype(jnp.bfloat16)
        rows = pl.ds(row, ANGLES, stride=count)
        held_real[rows, :], held_imag[rows, :] = spectrum_of(weighted, table)
    shape = (ANGLES, count, CYCLES)
    out_ref[:, :, :CYCLES] = held_real[...].reshape(shape).astype(jnp.bfloat16)
    out_ref[:, :, CYCLES:] = held_imag[...].reshape(shape).astype(jnp.bfloat16)


def image_spectra(images, half, contrast_rows, table):
    particles = contrast_rows.shape[0] // 2
    count = 16
    skipped = half * particles // count
    return pl.pallas_call(
        spectra_kernel,
        grid=(particles // count,),
        in_specs=[
            pl.BlockSpec((2 * ANGLES, ANGLES), lambda i: (0, 0)),
            pl.BlockSpec((count, CYCLES), lambda i: (i + skipped, 0)),
            pl.BlockSpec((count, ANGLES, 2 * CYCLES), lambda i: (i + skipped, 0, 0)),
        ],
        out_specs=pl.BlockSpec((ANGLES, count, 2 * CYCLES), lambda i: (0, i, 0)),
        out_shape=jax.ShapeDtypeStruct((ANGLES, particles, 2 * CYCLES), jnp.bfloat16),
        scratch_shapes=[pltpu.VMEM((ANGLES * count, CYCLES), jnp.float32)] * 2,
        compiler_params=pltpu.CompilerParams(vmem_limit_bytes=56 * 1024 * 1024),
        cost_estimate=pl.CostEstimate(
            flops=particles * 4 * ANGLES * ANGLES * 2 * CYCLES,
            bytes_accessed=4 * particles * ANGLES * 2 * CYCLES,
            transcendentals=0,
        ),
    )(table, contrast_rows, images)


def pick_kernel(group_ref, roster_ref, source_ref, out_ref):
    planes = source_ref.shape[1] == STEPS
    for step in range(STEPS):
        holder = roster_ref[group_ref[0], step]
        value = source_ref[holder >> 4, step] if planes else source_ref[holder & 15, 0]
        for copy in range(out_ref.shape[0]):
            out_ref[copy, step] = value


def pick(group, roster, source, copies):
    smem = pl.BlockSpec(memory_space=pltpu.SMEM)
    vmem = pl.BlockSpec(memory_space=pltpu.VMEM)
    return pl.pallas_call(
        pick_kernel,
        in_specs=[smem, smem, vmem],
        out_specs=vmem,
        out_shape=jax.ShapeDtypeStruct((copies, STEPS, ANGLES, CYCLES), jnp.bfloat16),
        compiler_params=pltpu.CompilerParams(vmem_limit_bytes=2 * 1024 * 1024),
    )(group, roster, source)


def score_kernel(
    core_ref,
    mine_ref,
    other_ref,
    early_ref,
    late_ref,
    low_ref,
    turn_ref,
    back_ref,
    square_ref,
    prior_ref,
    member_ref,
    keep_ref,
    send_ref,
    evidence_ref,
    ref_real,
    ref_imag,
    corr,
    scores,
    power,
    spectra_ref,
    sem,
):
    particles = spectra_ref.shape[1]
    depth, half = ANGLES // CHUNKS, particles // 2
    arriving = [
        pltpu.make_async_copy(
            source.at[pl.ds(n * depth, depth)],
            spectra_ref.at[pl.ds(n * depth, depth), pl.ds(k * half, half)],
            sem.at[n, k],
        )
        for n in range(CHUNKS)
        for k, source in enumerate((early_ref, late_ref))
    ]
    for copy in arriving:
        copy.start()
    first = core_ref[0] == 0
    table = low_ref[...]
    for c in range(CLS_GRP):
        mine, other = mine_ref[c], other_ref[c]
        polar = jnp.concatenate(
            [jnp.where(first, mine, other), jnp.where(first, other, mine)], axis=-1
        )
        real, imag = (
            part.astype(jnp.bfloat16).astype(jnp.float32) for part in spectrum_of(polar, table)
        )
        rows = pl.ds(c, ANGLES, stride=CLS_GRP)
        ref_real[rows, :], ref_imag[rows, :] = real, imag
        power[c : c + 1, :] = jnp.sum(real * real + imag * imag, axis=0, keepdims=True)
    square = square_ref[...]
    across = (((1,), (1,)), ((), ()))
    energy = 0.5 * lax.dot_general(
        power[...], square, across, precision=TOP_PRECISION, preferred_element_type=jnp.float32
    )
    for m in range(ANGLES):
        if m % depth == 0:
            for copy in arriving[m // depth * 2 : m // depth * 2 + 2]:
                copy.wait()
        rows = slice(m * CLS_GRP, (m + 1) * CLS_GRP)
        real, imag = ref_real[rows, :], ref_imag[rows, :]
        both = jnp.concatenate(
            [jnp.concatenate([real, -imag], axis=0), jnp.concatenate([imag, real], axis=0)],
            axis=-1,
        ).astype(jnp.bfloat16)
        corr[m * 2 * CLS_GRP : (m + 1) * 2 * CLS_GRP, :] = lax.dot_general(
            both, spectra_ref[m], across, preferred_element_type=jnp.float32
        )
    turn, prior = turn_ref[...], prior_ref[...]
    best = jnp.full((ANGLES, particles), -jnp.inf, jnp.float32)
    own = jnp.zeros((ANGLES, particles), jnp.float32)
    for c in range(0, CLS_GRP, 2):
        pair = [
            jnp.concatenate(
                [
                    corr[pl.ds(k, ANGLES, stride=2 * CLS_GRP), :],
                    corr[pl.ds(CLS_GRP + k, ANGLES, stride=2 * CLS_GRP), :],
                ],
                axis=0,
            )
            for k in (c, c + 1)
        ]
        rotated = jnp.dot(
            turn,
            jnp.concatenate(pair, axis=-1),
            precision=TOP_PRECISION,
            preferred_element_type=jnp.float32,
        )
        for k in range(2):
            value = rotated[:, k * particles : (k + 1) * particles]
            value = (value - energy[c + k : c + k + 1, :]) * (1.0 / ANGLES) + prior
            scores[c + k] = value
            best = jnp.maximum(best, value)
            own = own + jnp.where(member_ref[c + k : c + k + 1, :] > 0, value, 0.0)
    top = jnp.max(best, axis=0, keepdims=True)
    total = jnp.zeros((ANGLES, particles), jnp.float32)
    for c in range(CLS_GRP):
        total = total + jnp.exp(scores[c] - top)
    evidence_ref[0:1, :] = top
    evidence_ref[1:2, :] = jnp.sum(total, axis=0, keepdims=True)
    weight = jnp.exp(own - jnp.max(own, axis=0, keepdims=True))
    weight = weight / jnp.sum(weight, axis=0, keepdims=True)
    turned_back = jnp.dot(
        back_ref[...], weight, precision=TOP_PRECISION, preferred_element_type=jnp.float32
    )
    h_real = turned_back[:particles].T
    h_imag = turned_back[particles:].T
    member = member_ref[...]
    chosen = member.astype(jnp.bfloat16)
    for m in range(ANGLES):
        x_real = spectra_ref[m, :, :CYCLES].astype(jnp.float32)
        x_imag = spectra_ref[m, :, CYCLES:].astype(jnp.float32)
        hr, hi = h_real[:, m : m + 1], h_imag[:, m : m + 1]
        aligned = jnp.concatenate(
            [x_real * hr - x_imag * hi, x_real * hi + x_imag * hr], axis=-1
        ).astype(jnp.bfloat16)
        sums = jnp.dot(chosen, aligned, preferred_element_type=jnp.float32)
        real_sum, imag_sum = sums[:, :CYCLES], sums[:, CYCLES:]
        keep_ref[m] = jnp.where(first, real_sum, imag_sum)
        send_ref[m] = jnp.where(first, imag_sum, real_sum)
    denom = jnp.dot(
        member, square, precision=TOP_PRECISION, preferred_element_type=jnp.float32
    )
    keep_ref[ANGLES] = denom
    send_ref[ANGLES] = denom


def score(core, mine, other, early, late, low_table, turn, back, square, prior, member):
    particles = 2 * early.shape[1]
    sums = jax.ShapeDtypeStruct((ANGLES + 1, CLS_GRP, CYCLES), jnp.float32)
    evidence = jax.ShapeDtypeStruct((2, particles), jnp.float32)
    vmem = pl.BlockSpec(memory_space=pltpu.VMEM)
    return pl.pallas_call(
        score_kernel,
        in_specs=[pl.BlockSpec(memory_space=pltpu.SMEM), vmem, vmem]
        + [pl.BlockSpec(memory_space=pltpu.HBM)] * 2
        + [vmem] * 6,
        out_specs=(vmem, vmem, vmem),
        out_shape=(sums, sums, evidence),
        scratch_shapes=[
            pltpu.VMEM((ANGLES * CLS_GRP, CYCLES), jnp.float32),
            pltpu.VMEM((ANGLES * CLS_GRP, CYCLES), jnp.float32),
            pltpu.VMEM((ANGLES * 2 * CLS_GRP, particles), jnp.float32),
            pltpu.VMEM((CLS_GRP, ANGLES, particles), jnp.float32),
            pltpu.VMEM((CLS_GRP, CYCLES), jnp.float32),
            pltpu.VMEM((ANGLES, particles, 2 * CYCLES), jnp.bfloat16),
            pltpu.SemaphoreType.DMA((CHUNKS, 2)),
        ],
        compiler_params=pltpu.CompilerParams(vmem_limit_bytes=50 * 1024 * 1024),
    )(core, mine, other, early, late, low_table, turn, back, square, prior, member)


def pack_kernel(keep_ref, got_ref, out_ref):
    denom = keep_ref[ANGLES] + got_ref[ANGLES]
    high = denom.astype(jnp.bfloat16)
    low = (denom - high.astype(jnp.float32)).astype(jnp.bfloat16)
    for m in range(SHARES * ROWS):
        if m < ANGLES:
            value = (keep_ref[m] + got_ref[m]).astype(jnp.bfloat16)
        elif m < ANGLES + 2:
            value = (high, low)[m - ANGLES]
        else:
            value = jnp.zeros_like(high)
        out_ref[m // ROWS, m % ROWS] = value


def pack(keep, got):
    vmem = pl.BlockSpec(memory_space=pltpu.VMEM)
    return pl.pallas_call(
        pack_kernel,
        in_specs=[vmem, vmem],
        out_specs=vmem,
        out_shape=jax.ShapeDtypeStruct((SHARES, ROWS, CLS_GRP, CYCLES), jnp.bfloat16),
        compiler_params=pltpu.CompilerParams(vmem_limit_bytes=4 * 1024 * 1024),
    )(keep, got)


def rotation_prior(rotation_rows):
    counting = jnp.arange(ANGLES, dtype=jnp.int32)
    distance = jnp.abs(counting[None, :] - rotation_rows[:, None])
    distance = jnp.minimum(distance, ANGLES - distance).astype(jnp.float32)
    return -0.5 * (distance / SIGMA_ROT) ** 2


def halve_kernel(blocks_ref, out_ref):
    for half in range(2):
        out_ref[:, half] = blocks_ref[:, :, half * CYCLES : (half + 1) * CYCLES]


def halve(blocks):
    count = 4
    return pl.pallas_call(
        halve_kernel,
        grid=(BLOCK // count,),
        in_specs=[pl.BlockSpec((count, ANGLES, 2 * CYCLES), lambda i: (i, 0, 0))],
        out_specs=pl.BlockSpec((count, 2, ANGLES, CYCLES), lambda i: (i, 0, 0, 0)),
        out_shape=jax.ShapeDtypeStruct((BLOCK, 2, ANGLES, CYCLES), jnp.bfloat16),
        compiler_params=pltpu.CompilerParams(vmem_limit_bytes=60 * 1024 * 1024),
    )(blocks)


def route_kernel(share_ref, place_ref, got_ref, out_ref):
    total = got_ref[0].astype(jnp.float32)
    for peer in range(1, SHARES):
        total = total + got_ref[peer].astype(jnp.float32)
    start = DENOM_ROW * CLS_GRP
    first, second = total[start : start + CLS_GRP], total[start + CLS_GRP : start + 2 * CLS_GRP]
    denom = first + second
    high = denom.astype(jnp.bfloat16).astype(jnp.float32)
    has_denom = share_ref[0] == DENOM_SHARE
    empty = jnp.zeros((CYCLES - ROWS * CLS_GRP, CYCLES), jnp.float32)
    share = jnp.concatenate(
        [
            total[:start],
            jnp.where(has_denom, high, first),
            jnp.where(has_denom, denom - high, second),
            total[start + 2 * CLS_GRP :],
            empty,
        ],
        axis=0,
    ).astype(jnp.bfloat16)
    place = place_ref[...]
    line = lax.broadcasted_iota(jnp.int32, (SLOT_ROWS, CYCLES), 0)
    line = (line // OWN_MAX) * 1024 + line % OWN_MAX - place
    for owner in range(0, 64, 8):
        chosen = jnp.concatenate(
            [jnp.where(line == -OWN_MAX * (owner + k), 1.0, 0.0) for k in range(8)], axis=0
        ).astype(jnp.bfloat16)
        out_ref[owner * SLOT_ROWS : (owner + 8) * SLOT_ROWS, :] = jnp.dot(
            chosen, share, preferred_element_type=jnp.float32
        ).astype(jnp.bfloat16)


def route(share, place, got):
    vmem = pl.BlockSpec(memory_space=pltpu.VMEM)
    return pl.pallas_call(
        route_kernel,
        in_specs=[pl.BlockSpec(memory_space=pltpu.SMEM), vmem, vmem],
        out_specs=vmem,
        out_shape=jax.ShapeDtypeStruct((64 * SLOT_ROWS, CYCLES), jnp.bfloat16),
        compiler_params=pltpu.CompilerParams(vmem_limit_bytes=6 * 1024 * 1024),
    )(share, place, got)


def finish_kernel(table_ref, got_ref, out_ref, held):
    total = got_ref[0].astype(jnp.float32) + got_ref[1].astype(jnp.float32)
    held[...] = total
    at = DENOM_SHARE * 2 * SLOT_ROWS + DENOM_ROW * OWN_MAX
    denom = total[at : at + OWN_MAX] + total[at + OWN_MAX : at + 2 * OWN_MAX]
    scale = (1.0 / ANGLES) / (denom + TAU)
    for slot in range(0, OWN_MAX, 2):
        pair = [
            held[pl.ds(k, held.shape[0] // OWN_MAX, stride=OWN_MAX), :] * scale[k : k + 1]
            for k in (slot, slot + 1)
        ]
        polar = jnp.dot(
            table_ref[...],
            jnp.concatenate(pair, axis=-1),
            precision=TOP_PRECISION,
            preferred_element_type=jnp.float32,
        ).astype(jnp.bfloat16)
        for k in range(2):
            columns = slice(k * CYCLES, (k + 1) * CYCLES)
            out_ref[slot + k, :, :CYCLES] = polar[:ANGLES, columns]
            out_ref[slot + k, :, CYCLES:] = polar[ANGLES:, columns]


def finish(table, got):
    vmem = pl.BlockSpec(memory_space=pltpu.VMEM)
    return pl.pallas_call(
        finish_kernel,
        in_specs=[vmem, vmem],
        out_specs=vmem,
        out_shape=jax.ShapeDtypeStruct((OWN_MAX, ANGLES, 2 * CYCLES), jnp.bfloat16),
        scratch_shapes=[pltpu.VMEM((2 * SHARES * SLOT_ROWS, CYCLES), jnp.float32)],
        compiler_params=pltpu.CompilerParams(vmem_limit_bytes=6 * 1024 * 1024),
    )(table, got)


def finish_table(cosine_table, sine_table):
    harmonic = np.arange(SHARES)[:, None] * ROWS + np.arange(SLOT_ROWS // OWN_MAX)
    filled = (np.arange(SLOT_ROWS // OWN_MAX) < ROWS) & (harmonic < ANGLES)

    def laid(table):
        return np.where(filled, table[:, harmonic % ANGLES], np.float32(0.0))[:, :, None]

    cosine, sine = laid(cosine_table), laid(sine_table)
    real = np.concatenate([cosine, -sine], axis=2).reshape(ANGLES, -1)
    imag = np.concatenate([sine, cosine], axis=2).reshape(ANGLES, -1)
    return np.concatenate([real, imag])


def fetch(blocks, group, roster, images, contrast_rows, table, small):
    halves = halve(blocks).reshape(BLOCK * 2, ANGLES, CYCLES)
    sliced = lax.all_to_all(halves, ("wide_1", "wide_2"), 0, 0, tiled=True)
    early = image_spectra(images, 0, contrast_rows, table)
    sliced, early, later = lax.optimization_barrier((sliced, early, contrast_rows))
    picked = pick(group, roster, sliced[:, None], 4)
    planes = lax.all_to_all(picked, HIGH, 0, 0, tiled=True)
    late = image_spectra(images, 1, later, table)
    planes, late, small = lax.optimization_barrier((planes, late, small))
    picked = pick(group, roster, planes, 8)
    mine = lax.all_to_all(picked, "wide_1", 0, 0, tiled=True).reshape(CLS_GRP, ANGLES, CYCLES)
    return mine, early, late, small


def exchanged_evidence(pair, bit):
    got = lax.ppermute(pair, "narrow", [(k, k ^ bit) for k in range(8)])
    top = jnp.maximum(pair[:1], got[:1])
    total = pair[1:] * jnp.exp(pair[:1] - top) + got[1:] * jnp.exp(got[:1] - top)
    return jnp.concatenate([top, total])


def per_device(images, defocus, class_index, rotation_index, owner_map, roster, ref_store):
    class_group = lax.axis_index("narrow")
    core = lax.axis_index("wide_2")
    cosine_table, sine_table = angle_tables(ANGLES)
    leading_class = class_group * CLS_GRP
    arrival = jnp.arange(CLS_GRP, dtype=jnp.int32)
    within = arrival % STEPS * BLOCK + arrival // STEPS
    class_ids = leading_class + within
    mine_group = jnp.arange(8, dtype=jnp.int32)[:, None] == class_group

    low_table = np.concatenate([cosine_table, sine_table]).astype(jnp.bfloat16)
    turn = np.concatenate([cosine_table, -sine_table], axis=-1)
    filled = ((0, CYCLES - ANGLES), (0, 0))
    back = np.concatenate([np.pad(cosine_table, filled), np.pad(sine_table, filled)])
    contrast_rows = contrast(defocus)
    square = contrast_rows * contrast_rows
    prior = rotation_prior(rotation_index).T
    member = (class_index[None, :] == class_ids[:, None]).astype(jnp.float32)
    def places(owner_map):
        owners = jnp.sum(jnp.where(mine_group, owner_map.reshape(8, CLS_GRP), 0), axis=0)
        owners = owners.reshape(STEPS, BLOCK).T.reshape(CLS_GRP)
        same = owners[:, None] == owners[None, :]
        ranking = jnp.sum(same & (within[None, :] < within[:, None]), axis=1)
        place = owners * OWN_MAX + ranking
        place = jnp.arange(ROWS, dtype=jnp.int32)[:, None] * 1024 + place[None, :]
        return jnp.pad(
            place.reshape(1, ROWS * CLS_GRP),
            ((0, 0), (0, CYCLES - ROWS * CLS_GRP)),
            constant_values=2**20,
        )

    table = finish_table(cosine_table, sine_table)
    small = (square, prior, member)

    mine, early, late, small = fetch(
        ref_store[0, 0], class_group.reshape(1), roster, images, contrast_rows, low_table, small
    )
    square, prior, member = small
    other = swapped(mine)
    keep, send, evidence = score(
        core.reshape(1), mine, other, early, late, low_table, turn, back, square, prior, member
    )
    send, owner_map = lax.optimization_barrier((send, owner_map))
    got, place = lax.optimization_barrier((swapped(send), places(owner_map)))
    share = pack(keep, got)
    share = share.reshape(SHARES, ROWS * CLS_GRP, CYCLES)
    share, evidence = lax.optimization_barrier((share, evidence))
    share = lax.all_to_all(share, ("wide_low", "wide_1"), 0, 0, tiled=True)
    for bit in (1,):
        evidence = exchanged_evidence(evidence, bit)
    share, evidence = lax.optimization_barrier((share, evidence))
    own_share = lax.axis_index(("wide_low", "wide_1"))
    sent = route(own_share.reshape(1), place, share).reshape(64, SLOT_ROWS, CYCLES)
    sent, evidence = lax.optimization_barrier((sent, evidence))
    got = lax.all_to_all(sent, WIDE, 0, 0, tiled=True)
    evidence = exchanged_evidence(exchanged_evidence(evidence, 2), 4)
    log_evidence = evidence[0] + jnp.log(evidence[1])
    got = got.reshape(2, 2 * SHARES * SLOT_ROWS, CYCLES)
    new_references = finish(table, got).reshape(1, 1, OWN_MAX, ANGLES, 2 * CYCLES)
    return (new_references, log_evidence)


def solution(mesh):
    split = Mesh(
        mesh.devices.reshape(2, 2, 8, 2, mesh.shape["narrow"]),
        (*WIDE, "narrow"),
    )
    placed = (
        P(WIDE, None, None),
        P(WIDE),
        P(WIDE),
        P(WIDE),
        P(),
        P(),
        P(WIDE, "narrow", None, None, None),
    )
    return jax.shard_map(
        per_device,
        mesh=split,
        in_specs=placed,
        out_specs=(P(WIDE, "narrow", None, None, None), P(WIDE)),
        check_vma=False,
    )
```
